512 devices in a mesh: seq: 64 (over x, z, core), dp: 8 (over y).
Axes of the slice: x: 4, y: 8, z: 8, core: 2. Of those that a mesh axis runs over, the one named last changes fastest.
Arguments:
- inputs: bfloat16 [8, 8192, 768], P('dp', 'seq'), may hold values from -150 to 150
- cotangent: bfloat16 [8, 8192, 768], P('dp', 'seq'), may hold values from -16 to 16
- conv_weight: bfloat16 [768, 768], replicated, may hold values from -0.125 to 0.125
- proj_weight: bfloat16 [256, 768], replicated, may hold values from -0.375 to 0.375
- gain_in: float32 [768], replicated, may hold values from 0.5 to 1.5
- bias_in: float32 [768], replicated, may hold values from -0.5 to 0.5
- gain_mid: float32 [256], replicated, may hold values from 0.5 to 1.5
- bias_mid: float32 [256], replicated, may hold values from -0.5 to 0.5
Outputs:
- block_out: bfloat16 [8, 8192, 768], P('dp', 'seq')
- input_grad: bfloat16 [8, 8192, 768], P('dp', 'seq')
- conv_grad: float32 [768, 768], P('seq')
- proj_grad: float32 [768, 256], P('seq')
The draws below stay inside these ranges and needn't reach their ends.
All inputs are finite; a program needn't handle non-finite values.
Results may differ from the reference program's by a relative error of at most 0.015.
Values may be sent and summed in bfloat16 or wider, within the bound.
No kernel may reach another device: no remote copies, remote signals or barrier semaphores. Data moves between devices by JAX's collectives and lax.ppermute only.
A program may use at most 64 MiB of HBM per device.

```python
import math
import jax
import jax.numpy as jnp
from jax import lax

CH = 768
MID = 256
LENGTH = 8192
BATCH = 8
DILATION_RATE = 1024


def draw_inputs(key, part):
    key_base, key_chan = jax.random.split(jax.random.fold_in(key, 17), 2)
    places = jnp.arange(LENGTH, dtype=jnp.float32)
    rising = 1.0 + 2.0 * places / (LENGTH - 1)
    channel_scale = jnp.exp(jax.random.uniform(key_chan, (CH,), jnp.float32, 0.0, math.log(10.0)))
    base = jax.random.truncated_normal(key_base, -4.0, 4.0, (BATCH, LENGTH, CH), jnp.float32)
    return (base * rising[None, :, None] * channel_scale).astype(jnp.bfloat16)


def with_spikes(result, rng, source, target, shards_of, factor):
    owner, partner = [(jnp.arange(result.shape[dim]) // (result.shape[dim] // shards_of)).reshape([-1 if axis == dim else 1 for axis in range(result.ndim)]) for dim in (source, target)]
    chosen = jax.random.permutation(rng, shards_of)[partner]
    strong = (owner == chosen) | (owner == (partner + shards_of // 2) % shards_of)
    return jnp.where(strong, factor * result, result)


def level_of(key, shape, shards, low, top_value):
    factor_of, own = 1.0, jax.random.fold_in(key, 6)
    for dim, parts in shards:
        steps = jnp.exp(jax.random.uniform(jax.random.fold_in(own, dim), (parts,), jnp.float32, low / len(shards), top_value / len(shards)))
        factor_of = factor_of * jnp.repeat(steps, shape[dim] // parts).reshape([-1 if axis == dim else 1 for axis in range(len(shape))])
    return factor_of


def gaussian(stream_key, dims, scale, reach, cuts=(), held_as=jnp.bfloat16):
    factor_of = level_of(stream_key, dims, cuts, -0.22, 0.18) if cuts else 1.0
    drawn = jax.random.normal(stream_key, dims, jnp.float32) * scale * factor_of
    return jnp.minimum(jnp.maximum(drawn, -reach), reach).astype(held_as)


def bell_draw_with(key, extent, scale, reach, cuts, heavy, kind=jnp.bfloat16):
    entries = scale * jax.random.normal(key, extent, jnp.float32)
    if cuts:
        entries = entries * level_of(key, extent, cuts, -0.22, 0.18)
    return jnp.clip(with_spikes(entries, jax.random.fold_in(key, 3), *heavy), -reach, reach).astype(kind)


def setup_inputs(seed: int = 0) -> dict:
    keys = jax.random.split(jax.random.key(seed), 9)
    inputs = draw_inputs(jax.random.fold_in(keys[8], 71), 0)
    cotangent = bell_draw_with(keys[1], (BATCH, LENGTH, CH), 1.0, 16.0, ((0, 8), (1, 64)), (1, 2, 64, 4.0))
    conv_weight = gaussian(keys[2], (CH, 3 * MID), (3 * CH) ** -0.5, 0.125)
    proj_weight = gaussian(keys[3], (MID, CH), MID ** -0.5, 0.375)
    gain_in = jnp.clip(1.0 + 0.1 * jax.random.normal(keys[4], (CH,), jnp.float32), 0.5, 1.5)
    bias_in = jnp.clip(jax.random.uniform(keys[5], (CH,), jnp.float32, -0.5, 0.5), -0.5, 0.5)
    gain_mid = jnp.clip(1.0 + 0.1 * jax.random.normal(keys[6], (MID,), jnp.float32), 0.5, 1.5)
    bias_mid = jnp.clip(jax.random.uniform(keys[7], (MID,), jnp.float32, -0.5, 0.5), -0.5, 0.5)
    return dict(inputs=inputs, cotangent=cotangent, conv_weight=conv_weight, proj_weight=proj_weight, gain_in=gain_in, bias_in=bias_in, gain_mid=gain_mid, bias_mid=bias_mid)


def gelu_tanh(value):
    coeff = math.sqrt(2.0 / math.pi)
    return 0.5 * value * (1.0 + jnp.tanh(coeff * (value + 0.044715 * value * value * value)))

def gelu_slope(value):
    coeff = math.sqrt(2.0 / math.pi)
    inner = jnp.tanh(coeff * (value + 0.044715 * value * value * value))
    return 0.5 * (1.0 + inner) + 0.5 * value * (1.0 - inner * inner) * coeff * (1.0 + 3.0 * 0.044715 * value * value)

def following_window(value, steps):
    return jnp.concatenate([jnp.zeros_like(value[:, :steps]), value[:, :-steps]], axis=1)

def preceding_window(value, steps):
    return jnp.concatenate([value[:, steps:], jnp.zeros_like(value[:, :steps])], axis=1)

def normalize(value):
    center = lax.optimization_barrier(jnp.mean(value, axis=(0, 1)))
    spread = jnp.sqrt(lax.optimization_barrier(jnp.mean((value - center) ** 2, axis=(0, 1))) + 1e-05)
    return ((value - center) / spread, spread)

def back_norm(dpre, normed, gain, spread):
    first = lax.optimization_barrier(jnp.mean(dpre, axis=(0, 1)))
    second = lax.optimization_barrier(jnp.mean(dpre * normed, axis=(0, 1)))
    return gain * (dpre - first - normed * second) / spread

def reference(inputs, cotangent, conv_weight, proj_weight, gain_in, bias_in, gain_mid, bias_mid):
    width = CH
    central_window = MID
    overall_row_count = BATCH * LENGTH
    stream = inputs.astype(jnp.float32)
    normed_in, spread_in = normalize(stream)
    pre_in = gain_in * normed_in + bias_in
    act_in = gelu_tanh(pre_in).astype(jnp.bfloat16)
    flat_in = act_in.reshape(overall_row_count, width)
    summand_terms = jnp.dot(flat_in, conv_weight, preferred_element_type=jnp.float32).reshape(BATCH, LENGTH, 3 * central_window)
    dilated_filter_output = following_window(summand_terms[..., :central_window], DILATION_RATE) + summand_terms[..., central_window:2 * central_window] + preceding_window(summand_terms[..., 2 * central_window:], DILATION_RATE)
    normed_mid, spread_mid = normalize(dilated_filter_output)
    pre_mid = gain_mid * normed_mid + bias_mid
    act_mid = gelu_tanh(pre_mid).astype(jnp.bfloat16)
    flat_mid = act_mid.reshape(overall_row_count, central_window)
    update = jnp.dot(flat_mid, proj_weight, preferred_element_type=jnp.float32).reshape(BATCH, LENGTH, width)
    block_out = (stream + update).astype(jnp.bfloat16)
    flat_cot = cotangent.reshape(overall_row_count, width)
    proj_grad = lax.dot_general(flat_cot, flat_mid, (((0,), (0,)), ((), ())), preferred_element_type=jnp.float32)
    dact_mid = lax.dot_general(flat_cot, proj_weight, (((1,), (1,)), ((), ())), preferred_element_type=jnp.float32)
    dpre_mid = dact_mid.reshape(BATCH, LENGTH, central_window) * gelu_slope(pre_mid)
    filter_output_gradient = back_norm(dpre_mid, normed_mid, gain_mid, spread_mid).astype(jnp.bfloat16)
    stacked_windows = jnp.concatenate([preceding_window(filter_output_gradient, DILATION_RATE), filter_output_gradient, following_window(filter_output_gradient, DILATION_RATE)], axis=2).reshape(overall_row_count, 3 * central_window)
    conv_grad = lax.dot_general(flat_in, stacked_windows, (((0,), (0,)), ((), ())), preferred_element_type=jnp.float32)
    dact_in = lax.dot_general(stacked_windows, conv_weight, (((1,), (1,)), ((), ())), preferred_element_type=jnp.float32)
    dpre_in = dact_in.reshape(BATCH, LENGTH, width) * gelu_slope(pre_in)
    input_grad = (cotangent.astype(jnp.float32) + back_norm(dpre_in, normed_in, gain_in, spread_in)).astype(jnp.bfloat16)
    return (block_out, input_grad, conv_grad, proj_grad)
```

```python
import math

import jax
import jax.numpy as jnp
from jax import lax
from jax.sharding import Mesh
from jax.sharding import PartitionSpec as P

SEQ = ("x", "z_hi", "z_lo", "core")
CHAIN = ("x", "z_hi")
PLANE = ("x", "z_hi", "z_lo")
LINE = ("core", "dp")
BF16, F32 = jnp.bfloat16, jnp.float32


def exchange(pieces, axes):
    return lax.all_to_all(pieces, axes, split_axis=0, concat_axis=0, tiled=True)


def over_copies(x, axes):
    count = lax.axis_size(axes)
    return exchange(jnp.broadcast_to(x, (count, *x.shape)), axes).sum(axis=0)


def over_all(x):
    return over_copies(over_copies(x, LINE), PLANE)


def inner_tanh(value):
    coeff = math.sqrt(2.0 / math.pi)
    return jnp.tanh(coeff * (value + 0.044715 * value * value * value))


def gelu_tanh(value):
    return 0.5 * value * (1.0 + inner_tanh(value))


def gelu_slope(value):
    coeff = math.sqrt(2.0 / math.pi)
    inner = inner_tanh(value)
    return 0.5 * (1.0 + inner) + 0.5 * value * (1.0 - inner * inner) * coeff * (
        1.0 + 3.0 * 0.044715 * value * value
    )


def sums(a, b):
    return jnp.concatenate([jnp.sum(a, axis=0), jnp.sum(b, axis=0)])[None]


def moments(total, counted):
    center, second = jnp.split(total[0] / counted, 2)
    return center, jnp.sqrt(second - center * center + 1e-05)


def later(x, rows):
    return jnp.concatenate([jnp.zeros_like(x[:rows]), x[:-rows]], axis=0)


def earlier(x, rows):
    return jnp.concatenate([x[rows:], jnp.zeros_like(x[:rows])], axis=0)


def matmul(a, b, dims):
    return lax.dot_general(a, b, (dims, ((), ())), preferred_element_type=F32)


def per_device(inputs, cotangent, conv_weight, proj_weight, gain_in, bias_in, gain_mid, bias_mid):
    samples, places, width = inputs.shape
    rows = samples * places
    mid = proj_weight.shape[0]
    links = lax.axis_size(CHAIN)
    step = rows // links
    counted = rows * lax.axis_size(SEQ) * lax.axis_size("dp")
    own_in = inputs.reshape(rows, width)
    own_cot = cotangent.reshape(rows, width)

    with jax.named_scope("spread"):
        both = jnp.concatenate([own_in, own_cot], axis=1).reshape(links, step, 2 * width)
        both = exchange(both, CHAIN).reshape(rows, 2 * width)
    stream = own_in.astype(F32)
    with jax.named_scope("stat_in"):
        center_in, spread_in = moments(over_all(sums(stream, stream * stream)), counted)

    x, cot = both[:, :width], both[:, width:]
    normed_in = (x.astype(F32) - center_in) / spread_in
    pre_in = gain_in * normed_in + bias_in
    act_in = gelu_tanh(pre_in).astype(BF16)
    terms = matmul(act_in, conv_weight, ((1,), (0,)))
    conv = later(terms[:, :mid], step) + terms[:, mid : 2 * mid] + earlier(terms[:, 2 * mid :], step)
    with jax.named_scope("stat_mid"):
        center_mid, spread_mid = moments(over_all(sums(conv, conv * conv)), counted)
    normed_mid = (conv - center_mid) / spread_mid
    pre_mid = gain_mid * normed_mid + bias_mid
    act_mid = gelu_tanh(pre_mid).astype(BF16)
    dact_mid = matmul(cot, proj_weight, ((1,), (1,)))
    dpre_mid = dact_mid * gelu_slope(pre_mid)
    with jax.named_scope("back_mid"):
        total = over_all(sums(dpre_mid, dpre_mid * normed_mid))
        first, second = jnp.split(total[0] / counted, 2)
    dconv = (gain_mid * (dpre_mid - first - normed_mid * second) / spread_mid).astype(BF16)
    stacked = jnp.concatenate([earlier(dconv, step), dconv, later(dconv, step)], axis=1)

    part_conv = matmul(act_in, stacked, ((0,), (0,)))
    part_proj = matmul(cot, act_mid, ((0,), (0,)))
    half = (3 * mid + mid) // 2
    with jax.named_scope("grad_core"):
        parts = jnp.concatenate([part_conv, part_proj], axis=1).astype(BF16)
        parts = jnp.stack([parts[:, :half], parts[:, half:]])
        parts = exchange(parts, "core").astype(F32).sum(axis=0)
    with jax.named_scope("grad_plane"):
        planes = lax.axis_size(PLANE)
        block = exchange(parts.astype(BF16).reshape(planes, width // planes, half), PLANE)

    dact_in = matmul(stacked, conv_weight, ((1,), (1,)))
    dpre_in = dact_in * gelu_slope(pre_in)
    with jax.named_scope("gather"):
        back = jnp.concatenate([dpre_in.astype(BF16), act_mid], axis=1)
        back = exchange(back.reshape(links, step, width + mid), CHAIN).reshape(rows, width + mid)
    with jax.named_scope("back_in"):
        total = over_all(sums(dpre_in, dpre_in * normed_in))
        first, second = jnp.split(total[0] / counted, 2)
    normed = (stream - center_in) / spread_in
    dpre = back[:, :width].astype(F32)
    change = gain_in * (dpre - first - normed * second) / spread_in
    input_grad = (own_cot.astype(F32) + change).astype(BF16)
    block_out = (stream + matmul(back[:, width:], proj_weight, ((1,), (0,)))).astype(BF16)

    with jax.named_scope("grad_line"):
        cores, batch = lax.axis_size("core"), lax.axis_size("dp")
        block = block.astype(F32).sum(axis=0).astype(BF16).reshape(cores, 1, -1, half)
        block = jnp.broadcast_to(block, (cores, batch, *block.shape[2:]))
        block = exchange(block.reshape(cores * batch, -1, half), LINE)
        block = block.reshape(cores, batch, -1, half).astype(F32).sum(axis=1)
    grads = jnp.concatenate([block[0], block[1]], axis=1)
    return (
        block_out.reshape(inputs.shape),
        input_grad.reshape(inputs.shape),
        grads[:, : 3 * mid],
        grads[:, 3 * mid :],
    )


def solution(mesh):
    split = Mesh(
        mesh.devices.reshape(4, 2, 4, 2, mesh.shape["dp"]), ("x", "z_hi", "z_lo", "core", "dp")
    )
    rows = P("dp", SEQ, None)
    return jax.shard_map(
        per_device,
        mesh=split,
        in_specs=(rows, rows, P(), P(), P(), P(), P(), P()),
        out_specs=(rows, rows, P(SEQ, None), P(SEQ, None)),
        check_vma=False,
    )
```

```python
import math

import jax
import jax.numpy as jnp
from jax import lax
from jax.experimental import pallas as pl
from jax.experimental.pallas import tpu as pltpu
from jax.sharding import Mesh
from jax.sharding import PartitionSpec as P

SEQ = ("x", "z_hi", "z_lo", "core")
PLANE = ("x", "z_hi", "z_lo")
LINE = ("core", "dp")
BF16, F32 = jnp.bfloat16, jnp.float32
CH, MID = 768, 256
ROWS, SHIFT = 128, 16
PLANES, LINES, BATCH = 32, 16, 8
HALF = 512
COUNTED = 8.0 * 8192.0
COEFF = math.sqrt(2.0 / math.pi)


def exchange(pieces, axes):
    return lax.all_to_all(pieces, axes, split_axis=0, concat_axis=0, tiled=True)


def kernel(body, *outs, name):
    shapes = tuple(jax.ShapeDtypeStruct(shape, dtype) for shape, dtype in outs)
    whole = pl.BlockSpec(memory_space=pltpu.VMEM)

    def call(*args):
        return pl.pallas_call(
            body,
            out_shape=shapes,
            in_specs=[whole] * len(args),
            out_specs=(whole,) * len(shapes),
            name=name,
        )(*args)

    return call


def matmul(a, b, dims):
    return lax.dot_general(a, b, (dims, ((), ())), preferred_element_type=F32)


def later(x):
    return jnp.concatenate([jnp.zeros_like(x[:SHIFT]), x[:-SHIFT]], axis=0)


def earlier(x):
    return jnp.concatenate([x[SHIFT:], jnp.zeros_like(x[:SHIFT])], axis=0)


def upper(shape):
    return lax.broadcasted_iota(jnp.int32, shape, 1) < shape[1] // 2


def woven(a, b):
    a, b = (v.astype(F32).reshape(ROWS // 8, 8, v.shape[1]) for v in (a, b))
    first = upper(a.shape)
    even = jnp.where(first, a, pltpu.roll(b, 4, axis=1))
    odd = jnp.where(first, pltpu.roll(a, 4, axis=1), b)
    pieces = jnp.stack([even, odd], axis=1)
    return pieces.reshape(PLANES, 8, a.shape[2]).astype(BF16)


def unwoven(pieces):
    pairs = pieces.astype(F32).reshape(ROWS // 8, 2, 8, pieces.shape[2])
    even, odd = pairs[:, 0], pairs[:, 1]
    first = upper(even.shape)
    a = jnp.where(first, even, pltpu.roll(odd, 4, axis=1))
    b = jnp.where(first, pltpu.roll(even, 4, axis=1), odd)
    return a.reshape(ROWS, -1), b.reshape(ROWS, -1)


def split_up(value, parts, width):
    pieces = []
    for _ in range(parts):
        rounded = value.astype(BF16).astype(F32)
        pieces += [rounded[:, k : k + width] for k in range(0, value.shape[1], width)]
        value = value - rounded
    row = lax.broadcasted_iota(jnp.int32, (8, width), 0)
    tile = jnp.zeros((8, width), F32)
    for k, piece in enumerate(pieces):
        tile = jnp.where(row == k, piece, tile)
    return tile.astype(BF16)


def put_together(tile, parts, count):
    rows = [tile[k : k + 1] for k in range(parts * count)]
    return [sum(rows[k::count][1:], rows[k]) for k in range(count)]


def sum_rows(value):
    return jnp.sum(value, axis=0, keepdims=True)


def copies(ref, index, row):
    ref[:, :, index] = jnp.broadcast_to(row, (ref.shape[0], 1, row.shape[1]))


def tanh_of(value):
    return jnp.tanh(COEFF * (value + 0.044715 * value * value * value))


def gelu_of(value, inner):
    return 0.5 * value * (1.0 + inner)


def slope_of(value, inner):
    return 0.5 * (1.0 + inner) + 0.5 * value * (1.0 - inner * inner) * COEFF * (
        1.0 + 3.0 * 0.044715 * value * value
    )


def moments(totals, squares):
    center = totals * (1.0 / COUNTED)
    return center, jnp.sqrt(squares * (1.0 / COUNTED) - center * center + 1e-05)


def first_sums(x_ref, out_ref):
    x = x_ref[...].astype(F32)
    copies(out_ref, slice(0, CH), sum_rows(x))
    copies(out_ref, slice(CH, 2 * CH), sum_rows(x * x))


def spread_data(x_ref, cot_ref, out_ref):
    out_ref[...] = woven(x_ref[...], cot_ref[...])


def spread_all(data_ref, sums_ref, out_ref):
    total = jnp.sum(sums_ref[...], axis=0)
    tile = split_up(total, 3, CH)
    out_ref[:, 0:8, :] = data_ref[...]
    out_ref[:, 8:16, :] = jnp.broadcast_to(tile[None], (PLANES, 8, CH))


def forward_conv(
    got_ref, weight_ref, gain_ref, bias_ref, act_ref, conv_ref, sums_ref, stat_ref
):
    tile = jnp.sum(got_ref[:, 8:16, :].astype(F32), axis=0)
    center, spread = moments(*put_together(tile, 3, 2))
    stat_ref[0:1, :] = center
    stat_ref[1:2, :] = spread
    x, _ = unwoven(got_ref[:, 0:8, :])
    pre = gain_ref[...] * ((x - center) / spread) + bias_ref[...]
    act = gelu_of(pre, tanh_of(pre)).astype(BF16)
    act_ref[...] = act
    terms = matmul(act, weight_ref[...], ((1,), (0,)))
    conv = later(terms[:, :MID]) + terms[:, MID : 2 * MID] + earlier(terms[:, 2 * MID :])
    conv_ref[...] = conv
    copies(sums_ref, slice(0, MID), sum_rows(conv))
    copies(sums_ref, slice(MID, 2 * MID), sum_rows(conv * conv))


def beside_conv(got_ref, stat_ref, gain_ref, bias_ref, proj_ref, normed_ref, slope_ref, cot_ref, dact_ref):
    x, cot = unwoven(got_ref[:, 0:8, :])
    normed = (x - stat_ref[0:1, :]) / stat_ref[1:2, :]
    pre = gain_ref[...] * normed + bias_ref[...]
    normed_ref[...] = normed
    slope_ref[...] = slope_of(pre, tanh_of(pre))
    cot_ref[...] = cot.astype(BF16)
    dact_ref[...] = matmul(cot.astype(BF16), proj_ref[...], ((1,), (1,)))


def middle(got_ref, conv_ref, dact_ref, gain_ref, bias_ref, act_ref, normed_ref, dpre_ref, sums_ref, stat_ref):
    total = jnp.sum(got_ref[...], axis=0)
    center, spread = moments(total[:, :MID], total[:, MID:])
    stat_ref[...] = spread
    normed = (conv_ref[...] - center) / spread
    pre = gain_ref[...] * normed + bias_ref[...]
    inner = tanh_of(pre)
    act_ref[...] = gelu_of(pre, inner).astype(BF16)
    dpre = dact_ref[...] * slope_of(pre, inner)
    normed_ref[...] = normed
    dpre_ref[...] = dpre
    copies(sums_ref, slice(0, MID), sum_rows(dpre))
    copies(sums_ref, slice(MID, 2 * MID), sum_rows(dpre * normed))


def filter_parts(
    got_ref, dpre_ref, normed_ref, spread_ref, gain_ref, act_in_ref, act_ref, cot_ref, stacked_ref, parts_ref
):
    total = jnp.sum(got_ref[...], axis=0) * (1.0 / COUNTED)
    first, second = total[:, :MID], total[:, MID:]
    dconv = gain_ref[...] * (dpre_ref[...] - first - normed_ref[...] * second) / spread_ref[...]
    stacked = jnp.concatenate([earlier(dconv), dconv, later(dconv)], axis=1).astype(BF16)
    stacked_ref[...] = stacked
    conv_part = matmul(act_in_ref[...], stacked, ((0,), (0,)))
    parts_ref[0] = conv_part[:, :HALF].astype(BF16)
    parts_ref[1, :, : HALF - MID] = conv_part[:, HALF:].astype(BF16)
    proj_part = matmul(cot_ref[...], act_ref[...], ((0,), (0,)))
    parts_ref[1, :, HALF - MID :] = proj_part.astype(BF16)


def back_rows(stacked_ref, weight_ref, slope_ref, normed_ref, act_ref, out_ref, sums_ref):
    dpre = matmul(stacked_ref[...], weight_ref[...], ((1,), (1,))) * slope_ref[...]
    sums = jnp.concatenate([sum_rows(dpre), sum_rows(dpre * normed_ref[...])], axis=1)
    sums_ref[...] = split_up(sums, 2, HALF)
    tail = jnp.concatenate([dpre[:, HALF:], act_ref[...].astype(F32)], axis=1)
    out_ref[...] = woven(dpre[:, :HALF], tail)


def to_plane(parts_ref, rows_ref, sums_ref, out_ref):
    both = parts_ref[0].astype(F32) + parts_ref[1].astype(F32)
    out_ref[:, 0:24, :] = both.astype(BF16).reshape(PLANES, 24, HALF)
    out_ref[:, 24:32, :] = rows_ref[...]
    out_ref[:, 32:40, :] = jnp.broadcast_to(sums_ref[...][None], (PLANES, 8, HALF))


def to_line(got_ref, out_ref):
    block = jnp.sum(got_ref[:, 0:24, :].astype(F32), axis=0)
    tile = jnp.sum(got_ref[:, 32:40, :].astype(F32), axis=0)
    tile = split_up(jnp.concatenate(put_together(tile, 2, 3), axis=1), 2, HALF)
    own = (block[:16], pltpu.roll(block, 12, axis=0)[:16])
    for core in range(2):
        piece = own[core].astype(BF16)
        out_ref[core * BATCH : (core + 1) * BATCH, 0:16, :] = jnp.broadcast_to(
            piece[None], (BATCH, 16, HALF)
        )
    out_ref[:, 16:24, :] = jnp.broadcast_to(tile[None], (LINES, 8, HALF))


def block_rows(got_ref, x_ref, proj_ref, out_ref, dpre_ref):
    low, tail = unwoven(got_ref[:, 24:32, :])
    dpre_ref[:, :HALF] = low
    dpre_ref[:, HALF:] = tail[:, :MID]
    update = matmul(tail[:, MID:].astype(BF16), proj_ref[...], ((1,), (0,)))
    out_ref[...] = (x_ref[...].astype(F32) + update).astype(BF16)


def last_rows(got_ref, dpre_ref, x_ref, cot_ref, stat_ref, gain_ref, grad_ref, conv_ref, proj_ref):
    tile = jnp.sum(got_ref[:, 16:24, :].astype(F32), axis=0)
    total = jnp.concatenate(put_together(tile, 2, 3), axis=1) * (1.0 / COUNTED)
    first, second = total[:, :CH], total[:, CH:]
    center, spread = stat_ref[0:1, :], stat_ref[1:2, :]
    normed = (x_ref[...].astype(F32) - center) / spread
    change = gain_ref[...] * (dpre_ref[...] - first - normed * second) / spread
    grad_ref[...] = (cot_ref[...].astype(F32) + change).astype(BF16)
    left = jnp.sum(got_ref[0:BATCH, 0:16, :].astype(F32), axis=0)
    right = jnp.sum(got_ref[BATCH:LINES, 0:16, :].astype(F32), axis=0)
    conv_ref[:, :HALF] = left[:12]
    conv_ref[:, HALF:] = right[:12, : CH - HALF]
    proj_ref[...] = right[:12, CH - HALF :]


def per_device(inputs, cotangent, conv_weight, proj_weight, gain_in, bias_in, gain_mid, bias_mid):
    x = inputs.reshape(ROWS, CH)
    cot = cotangent.reshape(ROWS, CH)
    gain_in, bias_in, gain_mid, bias_mid = (v[None] for v in (gain_in, bias_in, gain_mid, bias_mid))
    rows, rows_mid = (ROWS, CH), (ROWS, MID)

    (sums,) = kernel(first_sums, ((LINES, 1, 2 * CH), F32), name="first_sums")(x)
    (data,) = kernel(spread_data, ((PLANES, 8, CH), BF16), name="spread_data")(x, cot)
    sums = exchange(sums, LINE)
    (both,) = kernel(spread_all, ((PLANES, 16, CH), BF16), name="spread_all")(data, sums)
    both = exchange(both, PLANE)

    act_in, conv, sums, stat_in = kernel(
        forward_conv,
        (rows, BF16),
        (rows_mid, F32),
        ((LINES, 1, 2 * MID), F32),
        ((8, CH), F32),
        name="forward_conv",
    )(both, conv_weight, gain_in, bias_in)
    normed_in, slope_in, far_cot, dact_mid = kernel(
        beside_conv, (rows, F32), (rows, F32), (rows, BF16), (rows_mid, F32), name="beside_conv"
    )(both, stat_in, gain_in, bias_in, proj_weight)
    sums = exchange(sums, LINE).sum(axis=0)
    sums = exchange(jnp.broadcast_to(sums, (PLANES, 1, 2 * MID)), PLANE)

    act_mid, normed_mid, dpre_mid, sums, spread_mid = kernel(
        middle,
        (rows_mid, BF16),
        (rows_mid, F32),
        (rows_mid, F32),
        ((LINES, 1, 2 * MID), F32),
        ((1, MID), F32),
        name="middle",
    )(sums, conv, dact_mid, gain_mid, bias_mid)
    sums = exchange(sums, LINE).sum(axis=0)
    sums = exchange(jnp.broadcast_to(sums, (PLANES, 1, 2 * MID)), PLANE)

    stacked, parts = kernel(
        filter_parts, (rows, BF16), ((2, CH, HALF), BF16), name="filter_parts"
    )(sums, dpre_mid, normed_mid, spread_mid, gain_mid, act_in, act_mid, far_cot)
    parts = exchange(parts, "core")
    back, sums = kernel(
        back_rows, ((PLANES, 8, HALF), BF16), ((8, HALF), BF16), name="back_rows"
    )(stacked, conv_weight, slope_in, normed_in, act_mid)
    (plane,) = kernel(to_plane, ((PLANES, 40, HALF), BF16), name="to_plane")(parts, back, sums)
    plane = exchange(plane, PLANE)
    (line,) = kernel(to_line, ((LINES, 24, HALF), BF16), name="to_line")(plane)
    line = exchange(line, LINE)
    block_out, dpre_in = kernel(block_rows, (rows, BF16), (rows, F32), name="block_rows")(
        plane, x, proj_weight
    )
    input_grad, conv_grad, proj_grad = kernel(
        last_rows, (rows, BF16), ((12, CH), F32), ((12, MID), F32), name="last_rows"
    )(line, dpre_in, x, cot, stat_in, gain_in)
    return (
        block_out.reshape(inputs.shape),
        input_grad.reshape(inputs.shape),
        conv_grad,
        proj_grad,
    )


def solution(mesh):
    split = Mesh(mesh.devices.reshape(4, 2, 4, 2, 8), ("x", "z_hi", "z_lo", "core", "dp"))
    rows = P("dp", SEQ, None)
    return jax.shard_map(
        per_device,
        mesh=split,
        in_specs=(rows, rows, P(), P(), P(), P(), P(), P()),
        out_specs=(rows, rows, P(SEQ, None), P(SEQ, None)),
        check_vma=False,
    )
```

```python
import math

import jax
import jax.numpy as jnp
from jax import lax
from jax.experimental import pallas as pl
from jax.experimental.pallas import tpu as pltpu
from jax.sharding import Mesh
from jax.sharding import PartitionSpec as P

SEQ = ("x", "z_hi", "z_lo", "core")
PLANE = ("x", "z_hi", "z_lo")
LINE = ("core", "dp")
BF16, F32 = jnp.bfloat16, jnp.float32
CH, MID = 768, 256
ROWS, SHIFT = 128, 16
PLANES, LINES, BATCH = 32, 16, 8
HALF = 512
COUNTED = 8.0 * 8192.0
COEFF = math.sqrt(2.0 / math.pi)


def exchange(pieces, axes):
    return lax.all_to_all(pieces, axes, split_axis=0, concat_axis=0, tiled=True)


def kernel(body, *outs, name):
    shapes = tuple(jax.ShapeDtypeStruct(shape, dtype) for shape, dtype in outs)
    whole = pl.BlockSpec(memory_space=pltpu.VMEM)

    def call(*args, near=()):
        near = tuple(pltpu.with_memory_space_constraint(a, pltpu.VMEM) for a in near)
        args = (*near, *args)
        return pl.pallas_call(
            body,
            out_shape=shapes,
            in_specs=[whole] * len(args),
            out_specs=(whole,) * len(shapes),
            name=name,
            compiler_params=pltpu.CompilerParams(vmem_limit_bytes=24 << 20),
        )(*args)

    return call


def matmul(a, b, dims):
    return lax.dot_general(a, b, (dims, ((), ())), preferred_element_type=F32)


def later(x):
    return jnp.concatenate([jnp.zeros_like(x[:SHIFT]), x[:-SHIFT]], axis=0)


def earlier(x):
    return jnp.concatenate([x[SHIFT:], jnp.zeros_like(x[:SHIFT])], axis=0)


def woven(value):
    width = value.shape[1] // 2
    tiles = value.astype(F32).reshape(ROWS // 8, 8, 2 * width)
    a, b = tiles[:, :, :width], tiles[:, :, width:]
    upper = lax.broadcasted_iota(jnp.int32, a.shape, 1) < 4
    even = jnp.where(upper, a, pltpu.roll(b, 4, axis=1))
    odd = jnp.where(upper, pltpu.roll(a, 4, axis=1), b)
    return jnp.stack([even, odd], axis=1).reshape(PLANES, 8, width).astype(BF16)


def unwoven(pieces):
    width = pieces.shape[2]
    pairs = pieces.astype(F32).reshape(ROWS // 8, 2, 8, width)
    even, odd = pairs[:, 0], pairs[:, 1]
    upper = lax.broadcasted_iota(jnp.int32, even.shape, 1) < 4
    a = jnp.where(upper, even, pltpu.roll(odd, 4, axis=1))
    b = jnp.where(upper, pltpu.roll(even, 4, axis=1), odd)
    return jnp.concatenate([a.reshape(ROWS, width), b.reshape(ROWS, width)], axis=1)


def rounded(value):
    return value.astype(BF16).astype(F32)


def tile_of(pieces, width):
    row = lax.broadcasted_iota(jnp.int32, (8, width), 0)
    tile = jnp.zeros((8, width), F32)
    for k, piece in enumerate(pieces):
        tile = jnp.where(row == k, piece, tile)
    return tile


def in_two(value, width):
    high = rounded(value)
    return [
        part[:, k : k + width] for part in (high, value - high) for k in range(0, value.shape[1], width)
    ]


def row_of(tile, rows):
    return jnp.concatenate([tile[k : k + 1] for k in rows], axis=1)


def sum_rows(value):
    return jnp.sum(value, axis=0, keepdims=True)


def copies(ref, index, row):
    ref[:, :, index] = jnp.broadcast_to(row, (ref.shape[0], 1, row.shape[1]))


def tanh_of(value):
    return jnp.tanh(COEFF * (value + 0.044715 * value * value * value))


def gelu_of(value, inner):
    return 0.5 * value * (1.0 + inner)


def slope_of(value, inner):
    return 0.5 * (1.0 + inner) + 0.5 * value * (1.0 - inner * inner) * COEFF * (
        1.0 + 3.0 * 0.044715 * value * value
    )


def first_sums(x_ref, out_ref):
    x = x_ref[...].astype(F32)
    mean = sum_rows(x) * (1.0 / ROWS)
    apart = x - mean
    copies(out_ref, slice(0, CH), mean)
    copies(out_ref, slice(CH, 2 * CH), sum_rows(apart * apart))


def spread_data(x_ref, cot_ref, proj_ref, out_ref):
    out_ref[:, :, : CH // 2] = woven(x_ref[...])
    out_ref[:, :, CH // 2 :] = woven(matmul(cot_ref[...], proj_ref[...], ((1,), (1,))))


def spread_all(sums_ref, data_ref, out_ref):
    sums = sums_ref[...]
    means = sums[:, :, :CH]
    mean = jnp.sum(means, axis=0) * (1.0 / LINES)
    apart = means - mean[None]
    squares = jnp.sum(sums[:, :, CH:] + float(ROWS) * (apart * apart), axis=0)
    tile = tile_of(in_two(mean, CH // 2) + in_two(squares, CH // 2), CH // 2).astype(BF16)
    out_ref[:, :, :HALF] = data_ref[...]
    out_ref[:, :, HALF:] = jnp.broadcast_to(tile[None], (PLANES, 8, CH // 2))


def forward_conv(got_ref, weight_ref, gain_ref, bias_ref, act_ref, conv_ref, sums_ref, stat_ref):
    parts = got_ref[:, :, HALF:].astype(F32)
    parts = parts + pltpu.roll(parts, 6, axis=1)
    total = jnp.sum(parts, axis=0)
    mean = total * (1.0 / PLANES)
    apart = parts - mean[None]
    between = jnp.sum(apart * apart, axis=0) * float(ROWS * LINES)
    center = row_of(mean, (0, 1))
    variance = (row_of(total, (4, 5)) + row_of(between, (0, 1))) * (1.0 / COUNTED)
    spread = jnp.sqrt(variance + 1e-05)
    stat_ref[0:1, :] = center
    stat_ref[1:2, :] = spread
    x = unwoven(got_ref[:, :, : CH // 2])
    pre = gain_ref[...] * ((x - center) / spread) + bias_ref[...]
    act = gelu_of(pre, tanh_of(pre)).astype(BF16)
    act_ref[...] = act
    terms = matmul(act, weight_ref[...], ((1,), (0,)))
    conv = later(terms[:, :MID]) + terms[:, MID : 2 * MID] + earlier(terms[:, 2 * MID :])
    conv_ref[...] = conv
    copies(sums_ref, slice(0, MID), sum_rows(conv))
    copies(sums_ref, slice(MID, 2 * MID), sum_rows(conv * conv))


def beside_conv(got_ref, stat_ref, gain_ref, bias_ref, normed_ref, slope_ref, dact_ref):
    normed = (unwoven(got_ref[:, :, : CH // 2]) - stat_ref[0:1, :]) / stat_ref[1:2, :]
    pre = gain_ref[...] * normed + bias_ref[...]
    normed_ref[...] = normed
    slope_ref[...] = slope_of(pre, tanh_of(pre))
    dact_ref[...] = unwoven(got_ref[:, :, CH // 2 : HALF])


def middle(got_ref, conv_ref, dact_ref, gain_ref, bias_ref, act_ref, normed_ref, dpre_ref, sums_ref, spread_ref):
    total = jnp.sum(got_ref[...], axis=0) * (1.0 / COUNTED)
    center = total[:, :MID]
    spread = jnp.sqrt(total[:, MID:] - center * center + 1e-05)
    spread_ref[...] = spread
    normed = (conv_ref[...] - center) / spread
    pre = gain_ref[...] * normed + bias_ref[...]
    inner = tanh_of(pre)
    dpre = dact_ref[...] * slope_of(pre, inner)
    copies(sums_ref, slice(0, MID), sum_rows(dpre))
    copies(sums_ref, slice(MID, 2 * MID), sum_rows(dpre * normed))
    normed_ref[...] = normed
    dpre_ref[...] = dpre
    act_ref[...] = woven(gelu_of(pre, inner))


def middle_plane(sums_ref, act_ref, out_ref):
    tile = tile_of(in_two(jnp.sum(sums_ref[...], axis=0), 128), 128).astype(BF16)
    out_ref[:, :, :128] = act_ref[...]
    out_ref[:, :, 128:] = jnp.broadcast_to(tile[None], (PLANES, 8, 128))


def filter_parts(
    got_ref, dpre_ref, normed_ref, spread_ref, gain_ref, act_in_ref, cot_ref, stacked_ref, parts_ref, act_ref
):
    tile = jnp.sum(got_ref[:, :, 128:].astype(F32), axis=0) * (1.0 / COUNTED)
    tile = tile + pltpu.roll(tile, 4, axis=0)
    first, second = row_of(tile, (0, 1)), row_of(tile, (2, 3))
    dconv = gain_ref[...] * (dpre_ref[...] - first - normed_ref[...] * second) / spread_ref[...]
    stacked = jnp.concatenate([earlier(dconv), dconv, later(dconv)], axis=1).astype(BF16)
    stacked_ref[...] = stacked
    conv_part = matmul(act_in_ref[...], stacked, ((0,), (0,)))
    parts_ref[0] = conv_part[:, :HALF].astype(BF16)
    parts_ref[1, :, : HALF - MID] = conv_part[:, HALF:].astype(BF16)
    act = unwoven(got_ref[:, :, :128]).astype(BF16)
    act_ref[...] = act
    proj_part = matmul(cot_ref[...], act, ((0,), (0,)))
    parts_ref[1, :, HALF - MID :] = proj_part.astype(BF16)


def back_rows(weight_ref, stacked_ref, slope_ref, normed_ref, out_ref):
    dpre = matmul(stacked_ref[...], weight_ref[...], ((1,), (1,))) * slope_ref[...]
    sums = jnp.concatenate([sum_rows(dpre), sum_rows(dpre * normed_ref[...])], axis=1)
    rows = [sums[:, k : k + 128] for k in range(0, 2 * CH, 128)]
    out_ref[:, :, : CH // 2] = woven(dpre)
    for k in range(2):
        tile = tile_of(rows[6 * k : 6 * k + 6], 128).astype(BF16)
        lanes = slice(CH // 2 + 128 * k, CH // 2 + 128 * (k + 1))
        out_ref[:, :, lanes] = jnp.broadcast_to(tile[None], (PLANES, 8, 128))


def to_plane(parts_ref, back_ref, out_ref):
    both = (parts_ref[0].astype(F32) + parts_ref[1].astype(F32)).astype(BF16)
    both = both.reshape(PLANES, 3, 8, HALF)
    for k in range(3):
        out_ref[:, :, HALF * k : HALF * (k + 1)] = both[:, k]
    out_ref[:, :, 3 * HALF :] = back_ref[...]


def to_line(got_ref, out_ref):
    tiles = [
        jnp.sum(got_ref[:, :, HALF * k : HALF * (k + 1)].astype(F32), axis=0) for k in range(3)
    ]
    sums = jnp.sum(got_ref[:, :, 3 * HALF + CH // 2 :].astype(F32), axis=0)
    sums = [row_of(sums[:, 128 * k : 128 * (k + 1)], range(6)) for k in range(2)]
    sums = jnp.concatenate(sums, axis=1)
    low = pltpu.roll(tile_of([sums[:, k : k + HALF] for k in range(0, 2 * CH, HALF)], HALF), 4, axis=0)
    upper = lax.broadcasted_iota(jnp.int32, (8, HALF), 0) < 4
    turned = [pltpu.roll(tile, 4, axis=0) for tile in tiles]
    own = (
        (tiles[0], jnp.where(upper, tiles[1], low)),
        (jnp.where(upper, turned[1], turned[2]), jnp.where(upper, turned[2], low)),
    )
    for core in range(2):
        for k in range(2):
            out_ref[core * BATCH : (core + 1) * BATCH, :, HALF * k : HALF * (k + 1)] = (
                jnp.broadcast_to(own[core][k].astype(BF16)[None], (BATCH, 8, HALF))
            )


def block_rows(act_ref, x_ref, proj_ref, out_ref):
    update = matmul(act_ref[...], proj_ref[...], ((1,), (0,)))
    out_ref[...] = (x_ref[...].astype(F32) + update).astype(BF16)


def beside_line(got_ref, x_ref, cot_ref, stat_ref, gain_ref, base_ref, normed_ref):
    dpre = unwoven(got_ref[:, :, 3 * HALF : 3 * HALF + CH // 2])
    spread = stat_ref[1:2, :]
    normed_ref[...] = (x_ref[...].astype(F32) - stat_ref[0:1, :]) / spread
    base_ref[...] = cot_ref[...].astype(F32) + dpre * (gain_ref[...] / spread)


def last_rows(got_ref, base_ref, normed_ref, stat_ref, gain_ref, grad_ref, conv_ref, proj_ref):
    left, right = (
        jnp.sum(got_ref[BATCH * k : BATCH * (k + 1)].astype(F32), axis=0) for k in range(2)
    )
    tile = left[4:8, HALF:] + right[4:8, HALF:]
    total = row_of(tile, range(3)) * (1.0 / COUNTED)
    scale = gain_ref[...] / stat_ref[1:2, :]
    grad = base_ref[...] - scale * total[:, :CH] - normed_ref[...] * (scale * total[:, CH:])
    grad_ref[...] = grad.astype(BF16)
    for rows, lanes, count in ((slice(0, 8), 0, 8), (slice(8, 12), HALF, 4)):
        conv_ref[rows, :HALF] = left[:count, lanes : lanes + HALF]
        conv_ref[rows, HALF:] = right[:count, lanes : lanes + CH - HALF]
        proj_ref[rows, :] = right[:count, lanes + CH - HALF : lanes + HALF]


def per_device(inputs, cotangent, conv_weight, proj_weight, gain_in, bias_in, gain_mid, bias_mid):
    x = inputs.reshape(ROWS, CH)
    cot = cotangent.reshape(ROWS, CH)
    gain_in, bias_in, gain_mid, bias_mid = (v[None] for v in (gain_in, bias_in, gain_mid, bias_mid))
    rows, rows_mid = (ROWS, CH), (ROWS, MID)

    (sums,) = kernel(first_sums, ((LINES, 1, 2 * CH), F32), name="first_sums")(x)
    (data,) = kernel(spread_data, ((PLANES, 8, HALF), BF16), name="spread_data")(x, cot, proj_weight)
    sums = exchange(sums, LINE)
    (both,) = kernel(spread_all, ((PLANES, 8, HALF + CH // 2), BF16), name="spread_all")(
        near=(sums, data)
    )
    both = exchange(both, PLANE)

    act_in, conv, sums, stat_in = kernel(
        forward_conv,
        (rows, BF16),
        (rows_mid, F32),
        ((LINES, 1, 2 * MID), F32),
        ((8, CH), F32),
        name="forward_conv",
    )(near=(both, conv_weight, gain_in, bias_in))
    normed_in, slope_in, dact_mid = kernel(
        beside_conv, (rows, F32), (rows, F32), (rows_mid, F32), name="beside_conv"
    )(stat_in, gain_in, bias_in, near=(both,))
    sums = exchange(sums, LINE).sum(axis=0)
    sums = exchange(jnp.broadcast_to(sums, (PLANES, 1, 2 * MID)), PLANE)

    act_mid, normed_mid, dpre_mid, sums, spread_mid = kernel(
        middle,
        ((PLANES, 8, 128), BF16),
        (rows_mid, F32),
        (rows_mid, F32),
        ((LINES, 1, 2 * MID), F32),
        ((1, MID), F32),
        name="middle",
    )(conv, dact_mid, gain_mid, bias_mid, near=(sums,))
    sums = exchange(sums, LINE)
    (both,) = kernel(middle_plane, ((PLANES, 8, 256), BF16), name="middle_plane")(
        act_mid, near=(sums,)
    )
    both = exchange(both, PLANE)

    stacked, parts, act_mid = kernel(
        filter_parts, (rows, BF16), ((2, CH, HALF), BF16), (rows_mid, BF16), name="filter_parts"
    )(dpre_mid, normed_mid, spread_mid, gain_mid, act_in, cot, near=(both,))
    parts = exchange(parts, "core")
    (back,) = kernel(back_rows, ((PLANES, 8, CH // 2 + 256), BF16), name="back_rows")(
        stacked, slope_in, normed_in, near=(conv_weight,)
    )
    (plane,) = kernel(to_plane, ((PLANES, 8, 3 * HALF + CH // 2 + 256), BF16), name="to_plane")(
        back, near=(parts,)
    )
    plane = exchange(plane, PLANE)
    (line,) = kernel(to_line, ((LINES, 8, 2 * HALF), BF16), name="to_line")(near=(plane,))
    line = exchange(line, LINE)
    (block_out,) = kernel(block_rows, (rows, BF16), name="block_rows")(act_mid, x, proj_weight)
    base, normed = kernel(beside_line, (rows, F32), (rows, F32), name="beside_line")(
        x, cot, stat_in, gain_in, near=(plane,)
    )
    input_grad, conv_grad, proj_grad = kernel(
        last_rows, (rows, BF16), ((12, CH), F32), ((12, MID), F32), name="last_rows"
    )(stat_in, gain_in, near=(line, base, normed))
    return (
        block_out.reshape(inputs.shape),
        input_grad.reshape(inputs.shape),
        conv_grad,
        proj_grad,
    )


def solution(mesh):
    split = Mesh(mesh.devices.reshape(4, 2, 4, 2, 8), ("x", "z_hi", "z_lo", "core", "dp"))
    rows = P("dp", SEQ, None)
    return jax.shard_map(
        per_device,
        mesh=split,
        in_specs=(rows, rows, P(), P(), P(), P(), P(), P()),
        out_specs=(rows, rows, P(SEQ, None), P(SEQ, None)),
        check_vma=False,
    )
```

```python
import math

import jax
import jax.numpy as jnp
from jax import lax
from jax.experimental import pallas as pl
from jax.experimental.pallas import tpu as pltpu
from jax.sharding import Mesh
from jax.sharding import PartitionSpec as P

SEQ = ("x", "z_hi", "z_lo", "core")
PLANE = ("x", "z_hi", "z_lo")
LINE = ("core", "dp")
BF16, F32 = jnp.bfloat16, jnp.float32
CH, MID = 768, 256
ROWS, SHIFT = 128, 16
PLANES, LINES, BATCH = 32, 16, 8
HALF = 512
COUNTED = 8.0 * 8192.0
COEFF = math.sqrt(2.0 / math.pi)


def exchange(pieces, axes):
    return lax.all_to_all(pieces, axes, split_axis=0, concat_axis=0, tiled=True)


def kernel(body, *outs, name):
    shapes = tuple(jax.ShapeDtypeStruct(shape, dtype) for shape, dtype in outs)
    whole = pl.BlockSpec(memory_space=pltpu.VMEM)

    def call(*args, near=()):
        near = tuple(pltpu.with_memory_space_constraint(a, pltpu.VMEM) for a in near)
        args = (*near, *args)
        return pl.pallas_call(
            body,
            out_shape=shapes,
            in_specs=[whole] * len(args),
            out_specs=(whole,) * len(shapes),
            name=name,
            compiler_params=pltpu.CompilerParams(vmem_limit_bytes=24 << 20),
        )(*args)

    return call


def matmul(a, b, dims):
    return lax.dot_general(a, b, (dims, ((), ())), preferred_element_type=F32)


def later(x):
    return jnp.concatenate([jnp.zeros_like(x[:SHIFT]), x[:-SHIFT]], axis=0)


def earlier(x):
    return jnp.concatenate([x[SHIFT:], jnp.zeros_like(x[:SHIFT])], axis=0)


def woven(value):
    width = value.shape[1] // 2
    tiles = value.astype(F32).reshape(ROWS // 8, 8, 2 * width)
    a, b = tiles[:, :, :width], tiles[:, :, width:]
    upper = lax.broadcasted_iota(jnp.int32, a.shape, 1) < 4
    even = jnp.where(upper, a, pltpu.roll(b, 4, axis=1))
    odd = jnp.where(upper, pltpu.roll(a, 4, axis=1), b)
    return jnp.stack([even, odd], axis=1).reshape(PLANES, 8, width).astype(BF16)


def unwoven(pieces):
    width = pieces.shape[2]
    pairs = pieces.astype(F32).reshape(ROWS // 8, 2, 8, width)
    even, odd = pairs[:, 0], pairs[:, 1]
    upper = lax.broadcasted_iota(jnp.int32, even.shape, 1) < 4
    a = jnp.where(upper, even, pltpu.roll(odd, 4, axis=1))
    b = jnp.where(upper, pltpu.roll(even, 4, axis=1), odd)
    return jnp.concatenate([a.reshape(ROWS, width), b.reshape(ROWS, width)], axis=1)


def rounded(value):
    return value.astype(BF16).astype(F32)


def tile_of(pieces, width):
    row = lax.broadcasted_iota(jnp.int32, (8, width), 0)
    tile = jnp.zeros((8, width), F32)
    for k, piece in enumerate(pieces):
        tile = jnp.where(row == k, piece, tile)
    return tile


def in_two(value, width):
    high = rounded(value)
    return [
        part[:, k : k + width] for part in (high, value - high) for k in range(0, value.shape[1], width)
    ]


def row_of(tile, rows):
    return jnp.concatenate([tile[k : k + 1] for k in rows], axis=1)


def sum_rows(value):
    return jnp.sum(value, axis=0, keepdims=True)


def flat(ref):
    return ref[...].reshape(1, ref.shape[0])


def copies(ref, index, row):
    ref[:, :, index] = jnp.broadcast_to(row, (ref.shape[0], 1, row.shape[1]))


def tanh_of(value):
    return jnp.tanh(COEFF * (value + 0.044715 * value * value * value))


def gelu_of(value, inner):
    return 0.5 * value * (1.0 + inner)


def slope_of(value, inner):
    return 0.5 * (1.0 + inner) + 0.5 * value * (1.0 - inner * inner) * COEFF * (
        1.0 + 3.0 * 0.044715 * value * value
    )


def opening(x_hbm, cot_hbm, proj_hbm, sums_ref, data_ref, x_ref, cot_ref, proj_ref, sems):
    pairs = ((x_hbm, x_ref), (cot_hbm, cot_ref), (proj_hbm, proj_ref))
    loads = [pltpu.make_async_copy(*pair, sems.at[k]) for k, pair in enumerate(pairs)]
    for load in loads:
        load.start()
    loads[0].wait()
    x = x_ref[...].astype(F32)
    mean = sum_rows(x) * (1.0 / ROWS)
    apart = x - mean
    copies(sums_ref, slice(0, CH), mean)
    copies(sums_ref, slice(CH, 2 * CH), sum_rows(apart * apart))
    data_ref[:, :, : CH // 2] = woven(x)
    loads[1].wait()
    loads[2].wait()
    data_ref[:, :, CH // 2 :] = woven(matmul(cot_ref[...], proj_ref[...], ((1,), (1,))))


def spread_all(sums_ref, data_ref, out_ref):
    sums = sums_ref[...]
    means = sums[:, :, :CH]
    mean = jnp.sum(means, axis=0) * (1.0 / LINES)
    apart = means - mean[None]
    squares = jnp.sum(sums[:, :, CH:] + float(ROWS) * (apart * apart), axis=0)
    tile = tile_of(in_two(mean, CH // 2) + in_two(squares, CH // 2), CH // 2).astype(BF16)
    out_ref[:, :, :HALF] = data_ref[...]
    out_ref[:, :, HALF:] = jnp.broadcast_to(tile[None], (PLANES, 8, CH // 2))


def forward_conv(got_ref, weight_ref, gain_ref, bias_ref, act_ref, x_ref, conv_ref, dact_ref, sums_ref, stat_ref):
    parts = got_ref[:, :, HALF:].astype(F32)
    parts = parts + pltpu.roll(parts, 6, axis=1)
    total = jnp.sum(parts, axis=0)
    mean = total * (1.0 / PLANES)
    apart = parts - mean[None]
    between = jnp.sum(apart * apart, axis=0) * float(ROWS * LINES)
    center = row_of(mean, (0, 1))
    variance = (row_of(total, (4, 5)) + row_of(between, (0, 1))) * (1.0 / COUNTED)
    spread = jnp.sqrt(variance + 1e-05)
    stat_ref[0:1, :] = center
    stat_ref[1:2, :] = spread
    x = unwoven(got_ref[:, :, : CH // 2])
    x_ref[...] = x.astype(BF16)
    pre = flat(gain_ref) * ((x - center) / spread) + flat(bias_ref)
    act = gelu_of(pre, tanh_of(pre)).astype(BF16)
    act_ref[...] = act
    terms = matmul(act, weight_ref[...], ((1,), (0,)))
    conv = later(terms[:, :MID]) + terms[:, MID : 2 * MID] + earlier(terms[:, 2 * MID :])
    conv_ref[...] = conv
    copies(sums_ref, slice(0, MID), sum_rows(conv))
    copies(sums_ref, slice(MID, 2 * MID), sum_rows(conv * conv))
    dact_ref[...] = unwoven(got_ref[:, :, CH // 2 : HALF])


def middle(got_ref, gain_ref, bias_ref, conv_ref, dact_ref, act_ref, normed_ref, dpre_ref, sums_ref, spread_ref):
    total = jnp.sum(got_ref[...], axis=0) * (1.0 / COUNTED)
    center = total[:, :MID]
    spread = jnp.sqrt(total[:, MID:] - center * center + 1e-05)
    spread_ref[0:1, :] = spread
    normed = (conv_ref[...] - center) / spread
    pre = flat(gain_ref) * normed + flat(bias_ref)
    inner = tanh_of(pre)
    dpre = dact_ref[...] * slope_of(pre, inner)
    copies(sums_ref, slice(0, MID), sum_rows(dpre))
    copies(sums_ref, slice(MID, 2 * MID), sum_rows(dpre * normed))
    normed_ref[...] = normed
    dpre_ref[...] = dpre
    act_ref[...] = woven(gelu_of(pre, inner))


def middle_plane(sums_ref, act_ref, out_ref):
    tile = tile_of(in_two(jnp.sum(sums_ref[...], axis=0), 128), 128).astype(BF16)
    out_ref[:, :, :128] = act_ref[...]
    out_ref[:, :, 128:] = jnp.broadcast_to(tile[None], (PLANES, 8, 128))


def filter_parts(
    got_ref, gain_ref, cot_ref, dpre_ref, normed_ref, spread_ref, act_in_ref, stacked_ref, parts_ref, act_ref
):
    tile = jnp.sum(got_ref[:, :, 128:].astype(F32), axis=0) * (1.0 / COUNTED)
    tile = tile + pltpu.roll(tile, 4, axis=0)
    first, second = row_of(tile, (0, 1)), row_of(tile, (2, 3))
    dconv = dpre_ref[...] - first - normed_ref[...] * second
    dconv = flat(gain_ref) * dconv / spread_ref[0:1, :]
    stacked = jnp.concatenate([earlier(dconv), dconv, later(dconv)], axis=1).astype(BF16)
    stacked_ref[...] = stacked
    conv_part = matmul(act_in_ref[...], stacked, ((0,), (0,)))
    parts_ref[0] = conv_part[:, :HALF].astype(BF16)
    parts_ref[1, :, : HALF - MID] = conv_part[:, HALF:].astype(BF16)
    act = unwoven(got_ref[:, :, :128]).astype(BF16)
    act_ref[...] = act
    proj_part = matmul(cot_ref[...], act, ((0,), (0,)))
    parts_ref[1, :, HALF - MID :] = proj_part.astype(BF16)


def to_plane(parts_ref, weight_ref, gain_ref, bias_ref, stacked_ref, x_ref, stat_ref, out_ref):
    normed = (x_ref[...].astype(F32) - stat_ref[0:1, :]) / stat_ref[1:2, :]
    pre = flat(gain_ref) * normed + flat(bias_ref)
    dpre = matmul(stacked_ref[...], weight_ref[...], ((1,), (1,))) * slope_of(pre, tanh_of(pre))
    sums = jnp.concatenate([sum_rows(dpre), sum_rows(dpre * normed)], axis=1)
    rows = [sums[:, k : k + 128] for k in range(0, 2 * CH, 128)]
    both = (parts_ref[0].astype(F32) + parts_ref[1].astype(F32)).astype(BF16)
    both = both.reshape(PLANES, 3, 8, HALF)
    for k in range(3):
        out_ref[:, :, HALF * k : HALF * (k + 1)] = both[:, k]
    begin = 3 * HALF + CH // 2
    out_ref[:, :, 3 * HALF : begin] = woven(dpre)
    for k in range(2):
        tile = tile_of(rows[6 * k : 6 * k + 6], 128).astype(BF16)
        out_ref[:, :, begin + 128 * k : begin + 128 * (k + 1)] = jnp.broadcast_to(
            tile[None], (PLANES, 8, 128)
        )


def to_line(got_ref, out_ref):
    tiles = [
        jnp.sum(got_ref[:, :, HALF * k : HALF * (k + 1)].astype(F32), axis=0) for k in range(3)
    ]
    sums = jnp.sum(got_ref[:, :, 3 * HALF + CH // 2 :].astype(F32), axis=0)
    sums = [row_of(sums[:, 128 * k : 128 * (k + 1)], range(6)) for k in range(2)]
    sums = jnp.concatenate(sums, axis=1)
    low = pltpu.roll(tile_of([sums[:, k : k + HALF] for k in range(0, 2 * CH, HALF)], HALF), 4, axis=0)
    upper = lax.broadcasted_iota(jnp.int32, (8, HALF), 0) < 4
    turned = [pltpu.roll(tile, 4, axis=0) for tile in tiles]
    own = (
        (tiles[0], jnp.where(upper, tiles[1], low)),
        (jnp.where(upper, turned[1], turned[2]), jnp.where(upper, turned[2], low)),
    )
    for core in range(2):
        for k in range(2):
            out_ref[core * BATCH : (core + 1) * BATCH, :, HALF * k : HALF * (k + 1)] = (
                jnp.broadcast_to(own[core][k].astype(BF16)[None], (BATCH, 8, HALF))
            )


def last_rows(
    got_ref, plane_ref, x_ref, cot_ref, proj_ref, gain_ref, act_ref, stat_ref, out_ref, grad_ref, conv_ref, proj_grad_ref
):
    x = x_ref[...].astype(F32)
    update = matmul(act_ref[...], proj_ref[...], ((1,), (0,)))
    out_ref[...] = (x + update).astype(BF16)
    left, right = (
        jnp.sum(got_ref[BATCH * k : BATCH * (k + 1)].astype(F32), axis=0) for k in range(2)
    )
    total = row_of(left[4:8, HALF:] + right[4:8, HALF:], range(3)) * (1.0 / COUNTED)
    spread = stat_ref[1:2, :]
    normed = (x - stat_ref[0:1, :]) / spread
    dpre = unwoven(plane_ref[:, :, 3 * HALF : 3 * HALF + CH // 2])
    change = flat(gain_ref) * (dpre - total[:, :CH] - normed * total[:, CH:]) / spread
    grad_ref[...] = (cot_ref[...].astype(F32) + change).astype(BF16)
    for rows, lanes, count in ((slice(0, 8), 0, 8), (slice(8, 12), HALF, 4)):
        conv_ref[rows, :HALF] = left[:count, lanes : lanes + HALF]
        conv_ref[rows, HALF:] = right[:count, lanes : lanes + CH - HALF]
        proj_grad_ref[rows, :] = right[:count, lanes + CH - HALF : lanes + HALF]


def per_device(inputs, cotangent, conv_weight, proj_weight, gain_in, bias_in, gain_mid, bias_mid):
    x = inputs.reshape(ROWS, CH)
    cot = cotangent.reshape(ROWS, CH)
    rows, rows_mid = (ROWS, CH), (ROWS, MID)

    far, near = pl.BlockSpec(memory_space=pltpu.HBM), pl.BlockSpec(memory_space=pltpu.VMEM)
    sums, data = pl.pallas_call(
        opening,
        out_shape=(
            jax.ShapeDtypeStruct((LINES, 1, 2 * CH), F32),
            jax.ShapeDtypeStruct((PLANES, 8, HALF), BF16),
        ),
        in_specs=[far] * 3,
        out_specs=(near, near),
        scratch_shapes=[
            pltpu.VMEM(rows, BF16),
            pltpu.VMEM(rows, BF16),
            pltpu.VMEM((MID, CH), BF16),
            pltpu.SemaphoreType.DMA((3,)),
        ],
        name="opening",
        compiler_params=pltpu.CompilerParams(vmem_limit_bytes=24 << 20),
    )(*(pltpu.with_memory_space_constraint(v, pltpu.HBM) for v in (x, cot, proj_weight)))
    sums = exchange(sums, LINE)
    (both,) = kernel(spread_all, ((PLANES, 8, HALF + CH // 2), BF16), name="spread_all")(
        data, near=(sums,)
    )
    both = exchange(both, PLANE)

    act_in, far_x, conv, dact_mid, sums, stat_in = kernel(
        forward_conv,
        (rows, BF16),
        (rows, BF16),
        (rows_mid, F32),
        (rows_mid, F32),
        ((LINES, 1, 2 * MID), F32),
        ((8, CH), F32),
        name="forward_conv",
    )(near=(both, conv_weight, gain_in, bias_in))
    sums = exchange(sums, LINE).sum(axis=0)
    sums = exchange(jnp.broadcast_to(sums, (PLANES, 1, 2 * MID)), PLANE)

    act_mid, normed_mid, dpre_mid, sums, spread_mid = kernel(
        middle,
        ((PLANES, 8, 128), BF16),
        (rows_mid, F32),
        (rows_mid, F32),
        ((LINES, 1, 2 * MID), F32),
        ((8, MID), F32),
        name="middle",
    )(conv, dact_mid, near=(sums, gain_mid, bias_mid))
    sums = exchange(sums, LINE)
    (both,) = kernel(middle_plane, ((PLANES, 8, 256), BF16), name="middle_plane")(
        act_mid, near=(sums,)
    )
    both = exchange(both, PLANE)

    stacked, parts, act_mid = kernel(
        filter_parts, (rows, BF16), ((2, CH, HALF), BF16), (rows_mid, BF16), name="filter_parts"
    )(dpre_mid, normed_mid, spread_mid, act_in, near=(both, gain_mid, cot))
    parts = exchange(parts, "core")
    (plane,) = kernel(to_plane, ((PLANES, 8, 3 * HALF + CH // 2 + 256), BF16), name="to_plane")(
        stacked, far_x, stat_in, near=(parts, conv_weight, gain_in, bias_in)
    )
    plane = exchange(plane, PLANE)
    (line,) = kernel(to_line, ((LINES, 8, 2 * HALF), BF16), name="to_line")(near=(plane,))
    line = exchange(line, LINE)
    block_out, input_grad, conv_grad, proj_grad = kernel(
        last_rows, (rows, BF16), (rows, BF16), ((12, CH), F32), ((12, MID), F32), name="last_rows"
    )(act_mid, stat_in, near=(line, plane, x, cot, proj_weight, gain_in))
    return (
        block_out.reshape(inputs.shape),
        input_grad.reshape(inputs.shape),
        conv_grad,
        proj_grad,
    )


def solution(mesh):
    split = Mesh(mesh.devices.reshape(4, 2, 4, 2, 8), ("x", "z_hi", "z_lo", "core", "dp"))
    rows = P("dp", SEQ, None)
    return jax.shard_map(
        per_device,
        mesh=split,
        in_specs=(rows, rows, P(), P(), P(), P(), P(), P()),
        out_specs=(rows, rows, P(SEQ, None), P(SEQ, None)),
        check_vma=False,
    )
```

```python
import math

import jax
import jax.numpy as jnp
from jax import lax
from jax.experimental import pallas as pl
from jax.experimental.pallas import tpu as pltpu
from jax.sharding import Mesh
from jax.sharding import PartitionSpec as P

SEQ = ("x", "z_hi", "z_lo", "core")
PLANE = ("x", "z_hi", "z_lo")
LINE = ("core", "dp")
BF16, F32 = jnp.bfloat16, jnp.float32
CH, MID = 768, 256
ROWS, SHIFT = 128, 16
PLANES, LINES, BATCH = 32, 16, 8
HALF = 512
COUNTED = 8.0 * 8192.0
COEFF = math.sqrt(2.0 / math.pi)


def exchange(pieces, axes):
    return lax.all_to_all(pieces, axes, split_axis=0, concat_axis=0, tiled=True)


def kernel(body, *outs, name):
    shapes = tuple(jax.ShapeDtypeStruct(shape, dtype) for shape, dtype in outs)
    whole = pl.BlockSpec(memory_space=pltpu.VMEM)

    def call(*args, near=()):
        near = tuple(pltpu.with_memory_space_constraint(a, pltpu.VMEM) for a in near)
        args = (*near, *args)
        return pl.pallas_call(
            body,
            out_shape=shapes,
            in_specs=[whole] * len(args),
            out_specs=(whole,) * len(shapes),
            name=name,
            compiler_params=pltpu.CompilerParams(vmem_limit_bytes=24 << 20),
        )(*args)

    return call


def matmul(a, b, dims):
    return lax.dot_general(a, b, (dims, ((), ())), preferred_element_type=F32)


def later(x):
    return jnp.concatenate([jnp.zeros_like(x[:SHIFT]), x[:-SHIFT]], axis=0)


def earlier(x):
    return jnp.concatenate([x[SHIFT:], jnp.zeros_like(x[:SHIFT])], axis=0)


def woven(value):
    width = value.shape[1] // 2
    tiles = value.astype(F32).reshape(ROWS // 8, 8, 2 * width)
    a, b = tiles[:, :, :width], tiles[:, :, width:]
    upper = lax.broadcasted_iota(jnp.int32, a.shape, 1) < 4
    even = jnp.where(upper, a, pltpu.roll(b, 4, axis=1))
    odd = jnp.where(upper, pltpu.roll(a, 4, axis=1), b)
    return jnp.stack([even, odd], axis=1).reshape(PLANES, 8, width).astype(BF16)


def unwoven(pieces):
    width = pieces.shape[2]
    pairs = pieces.astype(F32).reshape(ROWS // 8, 2, 8, width)
    even, odd = pairs[:, 0], pairs[:, 1]
    upper = lax.broadcasted_iota(jnp.int32, even.shape, 1) < 4
    a = jnp.where(upper, even, pltpu.roll(odd, 4, axis=1))
    b = jnp.where(upper, pltpu.roll(even, 4, axis=1), odd)
    return jnp.concatenate([a.reshape(ROWS, width), b.reshape(ROWS, width)], axis=1)


def rounded(value):
    return value.astype(BF16).astype(F32)


def tile_of(pieces, width):
    row = lax.broadcasted_iota(jnp.int32, (8, width), 0)
    tile = jnp.zeros((8, width), F32)
    for k, piece in enumerate(pieces):
        tile = jnp.where(row == k, piece, tile)
    return tile


def in_two(value, width):
    high = rounded(value)
    return [
        part[:, k : k + width] for part in (high, value - high) for k in range(0, value.shape[1], width)
    ]


def row_of(tile, rows):
    return jnp.concatenate([tile[k : k + 1] for k in rows], axis=1)


def sum_rows(value):
    return jnp.sum(value, axis=0, keepdims=True)


def flat(ref):
    return ref[...].reshape(1, ref.shape[0])


def copies(ref, index, row):
    ref[:, :, index] = jnp.broadcast_to(row, (ref.shape[0], 1, row.shape[1]))


def tanh_of(value):
    return jnp.tanh(COEFF * (value + 0.044715 * value * value * value))


def gelu_of(value, inner):
    return 0.5 * value * (1.0 + inner)


def slope_of(value, inner):
    return 0.5 * (1.0 + inner) + 0.5 * value * (1.0 - inner * inner) * COEFF * (
        1.0 + 3.0 * 0.044715 * value * value
    )


def opening(x_hbm, cot_hbm, proj_hbm, sums_ref, data_ref, x_ref, cot_ref, proj_ref, sems):
    pairs = ((x_hbm, x_ref), (cot_hbm, cot_ref), (proj_hbm, proj_ref))
    loads = [pltpu.make_async_copy(*pair, sems.at[k]) for k, pair in enumerate(pairs)]
    for load in loads:
        load.start()
    loads[0].wait()
    x = x_ref[...].astype(F32)
    mean = sum_rows(x) * (1.0 / ROWS)
    apart = x - mean
    copies(sums_ref, slice(0, CH), mean)
    copies(sums_ref, slice(CH, 2 * CH), sum_rows(apart * apart))
    data_ref[:, :, : CH // 2] = woven(x)
    loads[1].wait()
    loads[2].wait()
    data_ref[:, :, CH // 2 :] = woven(matmul(cot_ref[...], proj_ref[...], ((1,), (1,))))


def spread_all(sums_ref, data_ref, out_ref):
    sums = sums_ref[...]
    means = sums[:, :, :CH]
    mean = jnp.sum(means, axis=0) * (1.0 / LINES)
    apart = means - mean[None]
    squares = jnp.sum(sums[:, :, CH:] + float(ROWS) * (apart * apart), axis=0)
    tile = tile_of(in_two(mean, CH // 2) + in_two(squares, CH // 2), CH // 2).astype(BF16)
    out_ref[:, :, :HALF] = data_ref[...]
    out_ref[:, :, HALF:] = jnp.broadcast_to(tile[None], (PLANES, 8, CH // 2))


def forward_conv(got_ref, weight_ref, gain_ref, bias_ref, act_ref, x_ref, conv_ref, dact_ref, sums_ref, stat_ref):
    parts = got_ref[:, :, HALF:].astype(F32)
    parts = parts + pltpu.roll(parts, 6, axis=1)
    total = jnp.sum(parts, axis=0)
    mean = total * (1.0 / PLANES)
    apart = parts - mean[None]
    between = jnp.sum(apart * apart, axis=0) * float(ROWS * LINES)
    center = row_of(mean, (0, 1))
    variance = (row_of(total, (4, 5)) + row_of(between, (0, 1))) * (1.0 / COUNTED)
    spread = jnp.sqrt(variance + 1e-05)
    stat_ref[0:1, :] = center
    stat_ref[1:2, :] = spread
    x = unwoven(got_ref[:, :, : CH // 2])
    x_ref[...] = x.astype(BF16)
    pre = flat(gain_ref) * ((x - center) / spread) + flat(bias_ref)
    act = gelu_of(pre, tanh_of(pre)).astype(BF16)
    act_ref[...] = act
    terms = matmul(act, weight_ref[...], ((1,), (0,)))
    conv = later(terms[:, :MID]) + terms[:, MID : 2 * MID] + earlier(terms[:, 2 * MID :])
    conv_ref[...] = conv
    copies(sums_ref, slice(0, MID), sum_rows(conv))
    copies(sums_ref, slice(MID, 2 * MID), sum_rows(conv * conv))
    dact_ref[...] = unwoven(got_ref[:, :, CH // 2 : HALF])


def middle(got_ref, gain_ref, bias_ref, conv_ref, dact_ref, act_ref, normed_ref, dpre_ref, sums_ref, spread_ref):
    total = jnp.sum(got_ref[...], axis=0) * (1.0 / COUNTED)
    center = total[:, :MID]
    spread = jnp.sqrt(total[:, MID:] - center * center + 1e-05)
    spread_ref[0:1, :] = spread
    normed = (conv_ref[...] - center) / spread
    pre = flat(gain_ref) * normed + flat(bias_ref)
    inner = tanh_of(pre)
    dpre = dact_ref[...] * slope_of(pre, inner)
    copies(sums_ref, slice(0, MID), sum_rows(dpre))
    copies(sums_ref, slice(MID, 2 * MID), sum_rows(dpre * normed))
    normed_ref[...] = normed
    dpre_ref[...] = dpre
    act_ref[...] = woven(gelu_of(pre, inner))


def middle_plane(sums_ref, act_ref, out_ref):
    tile = tile_of(in_two(jnp.sum(sums_ref[...], axis=0), 128), 128).astype(BF16)
    out_ref[:, :, :128] = act_ref[...]
    out_ref[:, :, 128:] = jnp.broadcast_to(tile[None], (PLANES, 8, 128))


def in_four(value):
    blank = jnp.zeros((1, HALF - CH // 2), F32)
    return tile_of([jnp.concatenate([row, blank], axis=1) for row in in_two(value, CH // 2)], HALF)


def from_four(tile):
    return jnp.concatenate([tile[k : k + 1, : CH // 2] + tile[k + 2 : k + 3, : CH // 2] for k in range(2)], axis=1)


def filter_parts(
    got_ref,
    gain_ref,
    cot_ref,
    weight_ref,
    gain_in_ref,
    bias_in_ref,
    dpre_ref,
    normed_ref,
    spread_ref,
    act_in_ref,
    x_ref,
    stat_ref,
    parts_ref,
    act_ref,
    back_ref,
):
    tile = jnp.sum(got_ref[:, :, 128:].astype(F32), axis=0) * (1.0 / COUNTED)
    tile = tile + pltpu.roll(tile, 4, axis=0)
    first, second = row_of(tile, (0, 1)), row_of(tile, (2, 3))
    dconv = dpre_ref[...] - first - normed_ref[...] * second
    dconv = flat(gain_ref) * dconv / spread_ref[0:1, :]
    stacked = jnp.concatenate([earlier(dconv), dconv, later(dconv)], axis=1).astype(BF16)
    conv_part = matmul(act_in_ref[...], stacked, ((0,), (0,)))
    parts_ref[0, :CH, :] = conv_part[:, :HALF].astype(BF16)
    parts_ref[1, :CH, : HALF - MID] = conv_part[:, HALF:].astype(BF16)
    act = unwoven(got_ref[:, :, :128]).astype(BF16)
    act_ref[...] = act
    proj_part = matmul(cot_ref[...], act, ((0,), (0,)))
    parts_ref[1, :CH, HALF - MID :] = proj_part.astype(BF16)
    normed = (x_ref[...].astype(F32) - stat_ref[0:1, :]) / stat_ref[1:2, :]
    pre = flat(gain_in_ref) * normed + flat(bias_in_ref)
    dpre = matmul(stacked, weight_ref[...], ((1,), (1,))) * slope_of(pre, tanh_of(pre))
    parts_ref[0, CH:, :] = in_four(sum_rows(dpre)).astype(BF16)
    parts_ref[1, CH:, :] = in_four(sum_rows(dpre * normed)).astype(BF16)
    back_ref[...] = woven(dpre)


def to_plane(parts_ref, back_ref, out_ref):
    both = parts_ref[0].astype(F32) + parts_ref[1].astype(F32)
    pieces = both[:CH].astype(BF16).reshape(PLANES, 3, 8, HALF)
    for k in range(3):
        out_ref[:, :, HALF * k : HALF * (k + 1)] = pieces[:, k]
    begin = 3 * HALF + CH // 2
    out_ref[:, :, 3 * HALF : begin] = back_ref[...]
    sums = from_four(both[CH:])
    tile = tile_of([sums[:, k : k + 128] for k in range(0, CH, 128)], 128).astype(BF16)
    out_ref[:, :, begin:] = jnp.broadcast_to(tile[None], (PLANES, 8, 128))


def to_line(got_ref, out_ref):
    tiles = [
        jnp.sum(got_ref[:, :, HALF * k : HALF * (k + 1)].astype(F32), axis=0) for k in range(3)
    ]
    sums = jnp.sum(got_ref[:, :, 3 * HALF + CH // 2 :].astype(F32), axis=0)
    low = pltpu.roll(in_four(row_of(sums, range(6))), 4, axis=0)
    upper = lax.broadcasted_iota(jnp.int32, (8, HALF), 0) < 4
    turned = [pltpu.roll(tile, 4, axis=0) for tile in tiles]
    own = (
        (tiles[0], jnp.where(upper, tiles[1], low)),
        (jnp.where(upper, turned[1], turned[2]), jnp.where(upper, turned[2], low)),
    )
    for core in range(2):
        for k in range(2):
            out_ref[core * BATCH : (core + 1) * BATCH, :, HALF * k : HALF * (k + 1)] = (
                jnp.broadcast_to(own[core][k].astype(BF16)[None], (BATCH, 8, HALF))
            )


def last_rows(
    got_ref, plane_ref, x_ref, cot_ref, proj_ref, gain_ref, act_ref, stat_ref, out_ref, grad_ref, conv_ref, proj_grad_ref
):
    x = x_ref[...].astype(F32)
    update = matmul(act_ref[...], proj_ref[...], ((1,), (0,)))
    out_ref[...] = (x + update).astype(BF16)
    left, right = (
        jnp.sum(got_ref[BATCH * k : BATCH * (k + 1)].astype(F32), axis=0) for k in range(2)
    )
    first, second = (from_four(half[4:8, HALF:]) * (1.0 / COUNTED) for half in (left, right))
    spread = stat_ref[1:2, :]
    normed = (x - stat_ref[0:1, :]) / spread
    dpre = unwoven(plane_ref[:, :, 3 * HALF : 3 * HALF + CH // 2])
    change = flat(gain_ref) * (dpre - first - normed * second) / spread
    grad_ref[...] = (cot_ref[...].astype(F32) + change).astype(BF16)
    for rows, lanes, count in ((slice(0, 8), 0, 8), (slice(8, 12), HALF, 4)):
        conv_ref[rows, :HALF] = left[:count, lanes : lanes + HALF]
        conv_ref[rows, HALF:] = right[:count, lanes : lanes + CH - HALF]
        proj_grad_ref[rows, :] = right[:count, lanes + CH - HALF : lanes + HALF]


def per_device(inputs, cotangent, conv_weight, proj_weight, gain_in, bias_in, gain_mid, bias_mid):
    x = inputs.reshape(ROWS, CH)
    cot = cotangent.reshape(ROWS, CH)
    rows, rows_mid = (ROWS, CH), (ROWS, MID)

    far, near = pl.BlockSpec(memory_space=pltpu.HBM), pl.BlockSpec(memory_space=pltpu.VMEM)
    sums, data = pl.pallas_call(
        opening,
        out_shape=(
            jax.ShapeDtypeStruct((LINES, 1, 2 * CH), F32),
            jax.ShapeDtypeStruct((PLANES, 8, HALF), BF16),
        ),
        in_specs=[far] * 3,
        out_specs=(near, near),
        scratch_shapes=[
            pltpu.VMEM(rows, BF16),
            pltpu.VMEM(rows, BF16),
            pltpu.VMEM((MID, CH), BF16),
            pltpu.SemaphoreType.DMA((3,)),
        ],
        name="opening",
        compiler_params=pltpu.CompilerParams(vmem_limit_bytes=24 << 20),
    )(*(pltpu.with_memory_space_constraint(v, pltpu.HBM) for v in (x, cot, proj_weight)))
    sums = exchange(sums, LINE)
    (both,) = kernel(spread_all, ((PLANES, 8, HALF + CH // 2), BF16), name="spread_all")(
        data, near=(sums,)
    )
    both = exchange(both, PLANE)

    act_in, far_x, conv, dact_mid, sums, stat_in = kernel(
        forward_conv,
        (rows, BF16),
        (rows, BF16),
        (rows_mid, F32),
        (rows_mid, F32),
        ((PLANES, 1, 2 * MID), F32),
        ((8, CH), F32),
        name="forward_conv",
    )(near=(both, conv_weight, gain_in, bias_in))
    sums = exchange(sums, PLANE).sum(axis=0)
    sums = exchange(jnp.broadcast_to(sums, (LINES, 1, 2 * MID)), LINE)

    act_mid, normed_mid, dpre_mid, sums, spread_mid = kernel(
        middle,
        ((PLANES, 8, 128), BF16),
        (rows_mid, F32),
        (rows_mid, F32),
        ((LINES, 1, 2 * MID), F32),
        ((8, MID), F32),
        name="middle",
    )(conv, dact_mid, near=(sums, gain_mid, bias_mid))
    sums = exchange(sums, LINE)
    (both,) = kernel(middle_plane, ((PLANES, 8, 256), BF16), name="middle_plane")(
        act_mid, near=(sums,)
    )
    both = exchange(both, PLANE)

    parts, act_mid, back = kernel(
        filter_parts,
        ((2, CH + 8, HALF), BF16),
        (rows_mid, BF16),
        ((PLANES, 8, CH // 2), BF16),
        name="filter_parts",
    )(
        dpre_mid,
        normed_mid,
        spread_mid,
        act_in,
        far_x,
        stat_in,
        near=(both, gain_mid, cot, conv_weight, gain_in, bias_in),
    )
    parts = exchange(parts, "core")
    (plane,) = kernel(to_plane, ((PLANES, 8, 3 * HALF + CH // 2 + 128), BF16), name="to_plane")(
        back, near=(parts,)
    )
    plane = exchange(plane, PLANE)
    (line,) = kernel(to_line, ((LINES, 8, 2 * HALF), BF16), name="to_line")(near=(plane,))
    line = exchange(line, LINE)
    block_out, input_grad, conv_grad, proj_grad = kernel(
        last_rows, (rows, BF16), (rows, BF16), ((12, CH), F32), ((12, MID), F32), name="last_rows"
    )(act_mid, stat_in, near=(line, plane, x, cot, proj_weight, gain_in))
    return (
        block_out.reshape(inputs.shape),
        input_grad.reshape(inputs.shape),
        conv_grad,
        proj_grad,
    )


def solution(mesh):
    split = Mesh(mesh.devices.reshape(4, 2, 4, 2, 8), ("x", "z_hi", "z_lo", "core", "dp"))
    rows = P("dp", SEQ, None)
    return jax.shard_map(
        per_device,
        mesh=split,
        in_specs=(rows, rows, P(), P(), P(), P(), P(), P()),
        out_specs=(rows, rows, P(SEQ, None), P(SEQ, None)),
        check_vma=False,
    )
```

```python
import math

import jax
import jax.numpy as jnp
from jax import lax
from jax.experimental import pallas as pl
from jax.experimental.pallas import tpu as pltpu
from jax.sharding import Mesh
from jax.sharding import PartitionSpec as P

SEQ = ("x", "z_hi", "z_lo", "core")
PLANE = ("x", "z_hi", "z_lo")
DEPTH = ("z_hi", "z_lo")
LINE = ("core", "dp")
BF16, F32 = jnp.bfloat16, jnp.float32
CH, MID = 768, 256
ROWS, SHIFT = 128, 16
PLANES, LINES, BATCH = 32, 16, 8
ACROSS, DEEP = 4, 8
HALF = 512
COUNTED = 8.0 * 8192.0
COEFF = math.sqrt(2.0 / math.pi)


def exchange(pieces, axes):
    return lax.all_to_all(pieces, axes, split_axis=0, concat_axis=0, tiled=True)


def kernel(body, *outs, name):
    shapes = tuple(jax.ShapeDtypeStruct(shape, dtype) for shape, dtype in outs)
    whole = pl.BlockSpec(memory_space=pltpu.VMEM)

    def call(*args, near=()):
        near = tuple(pltpu.with_memory_space_constraint(a, pltpu.VMEM) for a in near)
        args = (*near, *args)
        return pl.pallas_call(
            body,
            out_shape=shapes,
            in_specs=[whole] * len(args),
            out_specs=(whole,) * len(shapes),
            name=name,
            compiler_params=pltpu.CompilerParams(vmem_limit_bytes=24 << 20),
        )(*args)

    return call


def matmul(a, b, dims):
    return lax.dot_general(a, b, (dims, ((), ())), preferred_element_type=F32)


def later(x):
    return jnp.concatenate([jnp.zeros_like(x[:SHIFT]), x[:-SHIFT]], axis=0)


def earlier(x):
    return jnp.concatenate([x[SHIFT:], jnp.zeros_like(x[:SHIFT])], axis=0)


def woven(value):
    width = value.shape[1] // 2
    tiles = value.astype(F32).reshape(ROWS // 8, 8, 2 * width)
    a, b = tiles[:, :, :width], tiles[:, :, width:]
    upper = lax.broadcasted_iota(jnp.int32, a.shape, 1) < 4
    even = jnp.where(upper, a, pltpu.roll(b, 4, axis=1))
    odd = jnp.where(upper, pltpu.roll(a, 4, axis=1), b)
    return jnp.stack([even, odd], axis=1).reshape(PLANES, 8, width).astype(BF16)


def unwoven(pieces):
    width = pieces.shape[2]
    pairs = pieces.astype(F32).reshape(ROWS // 8, 2, 8, width)
    even, odd = pairs[:, 0], pairs[:, 1]
    upper = lax.broadcasted_iota(jnp.int32, even.shape, 1) < 4
    a = jnp.where(upper, even, pltpu.roll(odd, 4, axis=1))
    b = jnp.where(upper, pltpu.roll(even, 4, axis=1), odd)
    return jnp.concatenate([a.reshape(ROWS, width), b.reshape(ROWS, width)], axis=1)


def rounded(value):
    return value.astype(BF16).astype(F32)


def tile_of(pieces, width):
    row = lax.broadcasted_iota(jnp.int32, (8, width), 0)
    tile = jnp.zeros((8, width), F32)
    for k, piece in enumerate(pieces):
        tile = jnp.where(row == k, piece, tile)
    return tile


def in_two(value, width):
    high = rounded(value)
    return [
        part[:, k : k + width] for part in (high, value - high) for k in range(0, value.shape[1], width)
    ]


def row_of(tile, rows):
    return jnp.concatenate([tile[k : k + 1] for k in rows], axis=1)


def sum_rows(value):
    return jnp.sum(value, axis=0, keepdims=True)


def flat(ref):
    return ref[...].reshape(1, ref.shape[0])


def copies(ref, index, row):
    ref[:, :, index] = jnp.broadcast_to(row, (ref.shape[0], 1, row.shape[1]))


def tanh_of(value):
    return jnp.tanh(COEFF * (value + 0.044715 * value * value * value))


def gelu_of(value, inner):
    return 0.5 * value * (1.0 + inner)


def slope_of(value, inner):
    return 0.5 * (1.0 + inner) + 0.5 * value * (1.0 - inner * inner) * COEFF * (
        1.0 + 3.0 * 0.044715 * value * value
    )


def opening(x_hbm, cot_hbm, proj_hbm, sums_ref, data_ref, dact_ref, x_ref, cot_ref, proj_ref, sems):
    pairs = ((x_hbm, x_ref), (cot_hbm, cot_ref), (proj_hbm, proj_ref))
    loads = [pltpu.make_async_copy(*pair, sems.at[k]) for k, pair in enumerate(pairs)]
    for load in loads:
        load.start()
    loads[0].wait()
    x = x_ref[...].astype(F32)
    mean = sum_rows(x) * (1.0 / ROWS)
    apart = x - mean
    copies(sums_ref, slice(0, CH), mean)
    copies(sums_ref, slice(CH, 2 * CH), sum_rows(apart * apart))
    data_ref[...] = woven(x)
    loads[1].wait()
    loads[2].wait()
    dact_ref[...] = woven(matmul(cot_ref[...], proj_ref[...], ((1,), (1,))))


def spread_all(sums_ref, data_ref, out_ref):
    sums = sums_ref[...]
    means = sums[:, :, :CH]
    mean = jnp.sum(means, axis=0) * (1.0 / LINES)
    apart = means - mean[None]
    squares = jnp.sum(sums[:, :, CH:] + float(ROWS) * (apart * apart), axis=0)
    tile = tile_of(in_two(mean, CH // 2) + in_two(squares, CH // 2), CH // 2).astype(BF16)
    out_ref[:, :, : CH // 2] = data_ref[...]
    out_ref[:, :, CH // 2 :] = jnp.broadcast_to(tile[None], (PLANES, 8, CH // 2))


def over_pieces(parts, count):
    parts = parts.astype(F32)
    parts = parts + pltpu.roll(parts, 6, axis=1)
    total = jnp.sum(parts, axis=0)
    mean = total * (1.0 / PLANES)
    apart = parts - mean[None]
    between = jnp.sum(apart * apart, axis=0) * float(count)
    return row_of(mean, (0, 1)), row_of(total, (4, 5)) + row_of(between, (0, 1))


def forward_conv(got_ref, weight_ref, gain_ref, bias_ref, dact_ref, act_ref, x_ref, conv_ref, out_ref, stat_ref):
    center, squares = over_pieces(got_ref[:, :, CH // 2 :], ROWS * LINES)
    spread = jnp.sqrt(squares * (1.0 / COUNTED) + 1e-05)
    stat_ref[0:1, :] = center
    stat_ref[1:2, :] = spread
    x = unwoven(got_ref[:, :, : CH // 2])
    x_ref[...] = x.astype(BF16)
    pre = flat(gain_ref) * ((x - center) / spread) + flat(bias_ref)
    act = gelu_of(pre, tanh_of(pre)).astype(BF16)
    act_ref[...] = act
    terms = matmul(act, weight_ref[...], ((1,), (0,)))
    conv = later(terms[:, :MID]) + terms[:, MID : 2 * MID] + earlier(terms[:, 2 * MID :])
    conv_ref[...] = conv
    mean = sum_rows(conv) * (1.0 / ROWS)
    apart = conv - mean
    tile = tile_of(in_two(mean, 128) + in_two(sum_rows(apart * apart), 128), 128).astype(BF16)
    out_ref[:, :, :128] = dact_ref[...]
    out_ref[:, :, 128:] = jnp.broadcast_to(tile[None], (PLANES, 8, 128))


def middle_line(got_ref, out_ref):
    mean, squares = over_pieces(got_ref[:, :, 128:], ROWS)
    copies(out_ref, slice(0, MID), mean)
    copies(out_ref, slice(MID, 2 * MID), squares)


def middle(got_ref, plane_ref, gain_ref, bias_ref, conv_ref, act_ref, normed_ref, dpre_ref, sums_ref, spread_ref):
    means = got_ref[:, :, :MID]
    center = jnp.sum(means, axis=0) * (1.0 / LINES)
    apart = means - center[None]
    squares = jnp.sum(got_ref[:, :, MID:] + float(ROWS * PLANES) * (apart * apart), axis=0)
    spread = jnp.sqrt(squares * (1.0 / COUNTED) + 1e-05)
    spread_ref[0:1, :] = spread
    normed = (conv_ref[...] - center) / spread
    pre = flat(gain_ref) * normed + flat(bias_ref)
    inner = tanh_of(pre)
    dpre = unwoven(plane_ref[:, :, :128]) * slope_of(pre, inner)
    copies(sums_ref, slice(0, MID), sum_rows(dpre))
    copies(sums_ref, slice(MID, 2 * MID), sum_rows(dpre * normed))
    normed_ref[...] = normed
    dpre_ref[...] = dpre
    act_ref[...] = woven(gelu_of(pre, inner))


def middle_plane(sums_ref, act_ref, out_ref):
    tile = tile_of(in_two(jnp.sum(sums_ref[...], axis=0), 128), 128).astype(BF16)
    out_ref[:, :, :128] = act_ref[...]
    out_ref[:, :, 128:] = jnp.broadcast_to(tile[None], (PLANES, 8, 128))


def in_four(value):
    blank = jnp.zeros((1, HALF - CH // 2), F32)
    return tile_of([jnp.concatenate([row, blank], axis=1) for row in in_two(value, CH // 2)], HALF)


def from_four(tile):
    return jnp.concatenate([tile[k : k + 1, : CH // 2] + tile[k + 2 : k + 3, : CH // 2] for k in range(2)], axis=1)


def filter_parts(
    got_ref,
    gain_ref,
    cot_ref,
    weight_ref,
    gain_in_ref,
    bias_in_ref,
    dpre_ref,
    normed_ref,
    spread_ref,
    act_in_ref,
    x_ref,
    stat_ref,
    parts_ref,
    act_ref,
    back_ref,
):
    tile = jnp.sum(got_ref[:, :, 128:].astype(F32), axis=0) * (1.0 / COUNTED)
    tile = tile + pltpu.roll(tile, 4, axis=0)
    first, second = row_of(tile, (0, 1)), row_of(tile, (2, 3))
    dconv = dpre_ref[...] - first - normed_ref[...] * second
    dconv = flat(gain_ref) * dconv / spread_ref[0:1, :]
    stacked = jnp.concatenate([earlier(dconv), dconv, later(dconv)], axis=1).astype(BF16)
    conv_part = matmul(act_in_ref[...], stacked, ((0,), (0,)))
    parts_ref[0, :CH, :] = conv_part[:, :HALF].astype(BF16)
    parts_ref[1, :CH, : HALF - MID] = conv_part[:, HALF:].astype(BF16)
    act = unwoven(got_ref[:, :, :128]).astype(BF16)
    act_ref[...] = act
    proj_part = matmul(cot_ref[...], act, ((0,), (0,)))
    parts_ref[1, :CH, HALF - MID :] = proj_part.astype(BF16)
    normed = (x_ref[...].astype(F32) - stat_ref[0:1, :]) / stat_ref[1:2, :]
    pre = flat(gain_in_ref) * normed + flat(bias_in_ref)
    dpre = matmul(stacked, weight_ref[...], ((1,), (1,))) * slope_of(pre, tanh_of(pre))
    parts_ref[0, CH:, :] = in_four(sum_rows(dpre)).astype(BF16)
    parts_ref[1, CH:, :] = in_four(sum_rows(dpre * normed)).astype(BF16)
    back_ref[...] = woven(dpre)


def to_plane(parts_ref, back_ref, out_ref):
    both = parts_ref[0].astype(F32) + parts_ref[1].astype(F32)
    pieces = both[:CH].astype(BF16).reshape(PLANES, 3, 8, HALF)
    for k in range(3):
        out_ref[:, :, HALF * k : HALF * (k + 1)] = pieces[:, k]
    begin = 3 * HALF + CH // 2
    out_ref[:, :, 3 * HALF : begin] = back_ref[...]
    sums = from_four(both[CH:])
    tile = tile_of([sums[:, k : k + 128] for k in range(0, CH, 128)], 128).astype(BF16)
    out_ref[:, :, begin:] = jnp.broadcast_to(tile[None], (PLANES, 8, 128))


def to_depth(got_ref, out_ref):
    sums = jnp.sum(got_ref[:, :, :, : 3 * HALF].astype(F32), axis=0)
    out_ref[:, :, : 3 * HALF] = sums.astype(BF16)
    begin = 3 * HALF + CH // 2
    for k in range(ACROSS):
        lanes = slice(3 * HALF + k * CH // 2, 3 * HALF + (k + 1) * CH // 2)
        out_ref[:, :, lanes] = got_ref[k, :, :, 3 * HALF : begin]
    sums = jnp.sum(got_ref[:, :, :, begin:].astype(F32), axis=0)
    out_ref[:, :, 3 * HALF + 2 * CH :] = sums.astype(BF16)


def to_line(got_ref, out_ref):
    tiles = [
        jnp.sum(got_ref[:, :, HALF * k : HALF * (k + 1)].astype(F32), axis=0) for k in range(3)
    ]
    sums = jnp.sum(got_ref[:, :, 3 * HALF + 2 * CH :].astype(F32), axis=0)
    low = pltpu.roll(in_four(row_of(sums, range(6))), 4, axis=0)
    upper = lax.broadcasted_iota(jnp.int32, (8, HALF), 0) < 4
    turned = [pltpu.roll(tile, 4, axis=0) for tile in tiles]
    own = (
        (tiles[0], jnp.where(upper, tiles[1], low)),
        (jnp.where(upper, turned[1], turned[2]), jnp.where(upper, turned[2], low)),
    )
    for core in range(2):
        for k in range(2):
            out_ref[core * BATCH : (core + 1) * BATCH, :, HALF * k : HALF * (k + 1)] = (
                jnp.broadcast_to(own[core][k].astype(BF16)[None], (BATCH, 8, HALF))
            )


def last_rows(
    got_ref, depth_ref, x_ref, cot_ref, proj_ref, gain_ref, act_ref, stat_ref, out_ref, grad_ref, conv_ref, proj_grad_ref
):
    x = x_ref[...].astype(F32)
    update = matmul(act_ref[...], proj_ref[...], ((1,), (0,)))
    out_ref[...] = (x + update).astype(BF16)
    left, right = (
        jnp.sum(got_ref[BATCH * k : BATCH * (k + 1)].astype(F32), axis=0) for k in range(2)
    )
    first, second = (from_four(half[4:8, HALF:]) * (1.0 / COUNTED) for half in (left, right))
    spread = stat_ref[1:2, :]
    normed = (x - stat_ref[0:1, :]) / spread
    begins = range(3 * HALF, 3 * HALF + 2 * CH, CH // 2)
    dpre = unwoven(jnp.concatenate([depth_ref[:, :, k : k + CH // 2] for k in begins], axis=0))
    change = flat(gain_ref) * (dpre - first - normed * second) / spread
    grad_ref[...] = (cot_ref[...].astype(F32) + change).astype(BF16)
    for rows, lanes, count in ((slice(0, 8), 0, 8), (slice(8, 12), HALF, 4)):
        conv_ref[rows, :HALF] = left[:count, lanes : lanes + HALF]
        conv_ref[rows, HALF:] = right[:count, lanes : lanes + CH - HALF]
        proj_grad_ref[rows, :] = right[:count, lanes + CH - HALF : lanes + HALF]


def per_device(inputs, cotangent, conv_weight, proj_weight, gain_in, bias_in, gain_mid, bias_mid):
    x = inputs.reshape(ROWS, CH)
    cot = cotangent.reshape(ROWS, CH)
    rows, rows_mid = (ROWS, CH), (ROWS, MID)

    far, near = pl.BlockSpec(memory_space=pltpu.HBM), pl.BlockSpec(memory_space=pltpu.VMEM)
    sums, data, dact = pl.pallas_call(
        opening,
        out_shape=(
            jax.ShapeDtypeStruct((LINES, 1, 2 * CH), F32),
            jax.ShapeDtypeStruct((PLANES, 8, CH // 2), BF16),
            jax.ShapeDtypeStruct((PLANES, 8, 128), BF16),
        ),
        in_specs=[far] * 3,
        out_specs=(near,) * 3,
        scratch_shapes=[
            pltpu.VMEM(rows, BF16),
            pltpu.VMEM(rows, BF16),
            pltpu.VMEM((MID, CH), BF16),
            pltpu.SemaphoreType.DMA((3,)),
        ],
        name="opening",
        compiler_params=pltpu.CompilerParams(vmem_limit_bytes=24 << 20),
    )(*(pltpu.with_memory_space_constraint(v, pltpu.HBM) for v in (x, cot, proj_weight)))
    sums = exchange(sums, LINE)
    (both,) = kernel(spread_all, ((PLANES, 8, CH), BF16), name="spread_all")(
        data, near=(sums,)
    )
    both = exchange(both, PLANE)

    act_in, far_x, conv, both, stat_in = kernel(
        forward_conv,
        (rows, BF16),
        (rows, BF16),
        (rows_mid, F32),
        ((PLANES, 8, 256), BF16),
        ((8, CH), F32),
        name="forward_conv",
    )(dact, near=(both, conv_weight, gain_in, bias_in))
    both = exchange(both, PLANE)
    (sums,) = kernel(middle_line, ((LINES, 1, 2 * MID), F32), name="middle_line")(near=(both,))
    sums = exchange(sums, LINE)

    act_mid, normed_mid, dpre_mid, sums, spread_mid = kernel(
        middle,
        ((PLANES, 8, 128), BF16),
        (rows_mid, F32),
        (rows_mid, F32),
        ((LINES, 1, 2 * MID), F32),
        ((8, MID), F32),
        name="middle",
    )(conv, near=(sums, both, gain_mid, bias_mid))
    sums = exchange(sums, LINE)
    (both,) = kernel(middle_plane, ((PLANES, 8, 256), BF16), name="middle_plane")(
        act_mid, near=(sums,)
    )
    both = exchange(both, PLANE)

    parts, act_mid, back = kernel(
        filter_parts,
        ((2, CH + 8, HALF), BF16),
        (rows_mid, BF16),
        ((PLANES, 8, CH // 2), BF16),
        name="filter_parts",
    )(
        dpre_mid,
        normed_mid,
        spread_mid,
        act_in,
        far_x,
        stat_in,
        near=(both, gain_mid, cot, conv_weight, gain_in, bias_in),
    )
    parts = exchange(parts, "core")
    (plane,) = kernel(to_plane, ((PLANES, 8, 3 * HALF + CH // 2 + 128), BF16), name="to_plane")(
        back, near=(parts,)
    )
    plane = exchange(plane.reshape(ACROSS, DEEP, *plane.shape[1:]), "x")
    (depth,) = kernel(to_depth, ((DEEP, 8, 3 * HALF + 2 * CH + 128), BF16), name="to_depth")(
        near=(plane,)
    )
    depth = exchange(depth, DEPTH)
    (line,) = kernel(to_line, ((LINES, 8, 2 * HALF), BF16), name="to_line")(near=(depth,))
    line = exchange(line, LINE)
    block_out, input_grad, conv_grad, proj_grad = kernel(
        last_rows, (rows, BF16), (rows, BF16), ((12, CH), F32), ((12, MID), F32), name="last_rows"
    )(act_mid, stat_in, near=(line, depth, x, cot, proj_weight, gain_in))
    return (
        block_out.reshape(inputs.shape),
        input_grad.reshape(inputs.shape),
        conv_grad,
        proj_grad,
    )


def solution(mesh):
    split = Mesh(mesh.devices.reshape(4, 2, 4, 2, 8), ("x", "z_hi", "z_lo", "core", "dp"))
    rows = P("dp", SEQ, None)
    return jax.shard_map(
        per_device,
        mesh=split,
        in_specs=(rows, rows, P(), P(), P(), P(), P(), P()),
        out_specs=(rows, rows, P(SEQ, None), P(SEQ, None)),
        check_vma=False,
    )
```

```python
import math

import jax
import jax.numpy as jnp
from jax import lax
from jax.experimental import pallas as pl
from jax.experimental.pallas import tpu as pltpu
from jax.sharding import Mesh
from jax.sharding import PartitionSpec as P

SEQ = ("x", "z_hi", "z_lo", "core")
PLANE = ("x", "z_hi", "z_lo")
LINE = ("core", "dp")
BF16, F32 = jnp.bfloat16, jnp.float32
CH, MID = 768, 256
ROWS, SHIFT = 128, 16
PLANES, LINES, BATCH = 32, 16, 8
WIDE, HALF = CH // 2, MID + CH // 2
COUNTED = 8.0 * 8192.0
COEFF = math.sqrt(2.0 / math.pi)


def exchange(pieces, axes):
    return lax.all_to_all(pieces, axes, split_axis=0, concat_axis=0, tiled=True)


def kernel(body, *outs, name):
    shapes = tuple(jax.ShapeDtypeStruct(shape, dtype) for shape, dtype in outs)
    whole = pl.BlockSpec(memory_space=pltpu.VMEM)

    def call(*args, near=()):
        near = tuple(pltpu.with_memory_space_constraint(a, pltpu.VMEM) for a in near)
        args = (*near, *args)
        return pl.pallas_call(
            body,
            out_shape=shapes,
            in_specs=[whole] * len(args),
            out_specs=(whole,) * len(shapes),
            name=name,
            compiler_params=pltpu.CompilerParams(vmem_limit_bytes=24 << 20),
        )(*args)

    return call


def matmul(a, b, dims):
    return lax.dot_general(a, b, (dims, ((), ())), preferred_element_type=F32)


def later(x):
    return jnp.concatenate([jnp.zeros_like(x[:SHIFT]), x[:-SHIFT]], axis=0)


def earlier(x):
    return jnp.concatenate([x[SHIFT:], jnp.zeros_like(x[:SHIFT])], axis=0)


def woven(value):
    width = value.shape[1] // 2
    tiles = value.astype(F32).reshape(ROWS // 8, 8, 2 * width)
    a, b = tiles[:, :, :width], tiles[:, :, width:]
    upper = lax.broadcasted_iota(jnp.int32, a.shape, 1) < 4
    even = jnp.where(upper, a, pltpu.roll(b, 4, axis=1))
    odd = jnp.where(upper, pltpu.roll(a, 4, axis=1), b)
    return jnp.stack([even, odd], axis=1).reshape(PLANES, 8, width).astype(BF16)


def unwoven(pieces):
    width = pieces.shape[2]
    pairs = pieces.astype(F32).reshape(ROWS // 8, 2, 8, width)
    even, odd = pairs[:, 0], pairs[:, 1]
    upper = lax.broadcasted_iota(jnp.int32, even.shape, 1) < 4
    a = jnp.where(upper, even, pltpu.roll(odd, 4, axis=1))
    b = jnp.where(upper, pltpu.roll(even, 4, axis=1), odd)
    return jnp.concatenate([a.reshape(ROWS, width), b.reshape(ROWS, width)], axis=1)


def rounded(value):
    return value.astype(BF16).astype(F32)


def tile_of(pieces, width):
    row = lax.broadcasted_iota(jnp.int32, (8, width), 0)
    tile = jnp.zeros((8, width), F32)
    for k, piece in enumerate(pieces):
        tile = jnp.where(row == k, piece, tile)
    return tile


def in_two(value, width):
    high = rounded(value)
    return [
        part[:, k : k + width] for part in (high, value - high) for k in range(0, value.shape[1], width)
    ]


def row_of(tile, rows):
    return jnp.concatenate([tile[k : k + 1] for k in rows], axis=1)


def sum_rows(value):
    return jnp.sum(value, axis=0, keepdims=True)


def flat(ref):
    return ref[...].reshape(1, ref.shape[0])


def copies(ref, index, row):
    ref[:, :, index] = jnp.broadcast_to(row, (ref.shape[0], 1, row.shape[1]))


def tanh_of(value):
    return jnp.tanh(COEFF * (value + 0.044715 * value * value * value))


def gelu_of(value, inner):
    return 0.5 * value * (1.0 + inner)


def slope_of(value, inner):
    return 0.5 * (1.0 + inner) + 0.5 * value * (1.0 - inner * inner) * COEFF * (
        1.0 + 3.0 * 0.044715 * value * value
    )


def opening(x_hbm, cot_hbm, sums_ref, data_ref, far_cot_ref, x_ref, cot_ref, sems):
    pairs = ((x_hbm, x_ref), (cot_hbm, cot_ref))
    loads = [pltpu.make_async_copy(*pair, sems.at[k]) for k, pair in enumerate(pairs)]
    for load in loads:
        load.start()
    loads[0].wait()
    x = x_ref[...].astype(F32)
    mean = sum_rows(x) * (1.0 / ROWS)
    apart = x - mean
    copies(sums_ref, slice(0, CH), mean)
    copies(sums_ref, slice(CH, 2 * CH), sum_rows(apart * apart))
    data_ref[...] = woven(x)
    loads[1].wait()
    far_cot_ref[...] = woven(cot_ref[...])


def spread_all(sums_ref, data_ref, out_ref):
    sums = sums_ref[...]
    means = sums[:, :, :CH]
    mean = jnp.sum(means, axis=0) * (1.0 / LINES)
    apart = means - mean[None]
    squares = jnp.sum(sums[:, :, CH:] + float(ROWS) * (apart * apart), axis=0)
    tile = tile_of(in_two(mean, WIDE) + in_two(squares, WIDE), WIDE).astype(BF16)
    out_ref[:, :, :WIDE] = data_ref[...]
    out_ref[:, :, WIDE :] = jnp.broadcast_to(tile[None], (PLANES, 8, WIDE))


def over_pieces(parts, count):
    parts = parts.astype(F32)
    parts = parts + pltpu.roll(parts, 6, axis=1)
    total = jnp.sum(parts, axis=0)
    mean = total * (1.0 / PLANES)
    apart = parts - mean[None]
    between = jnp.sum(apart * apart, axis=0) * float(count)
    return row_of(mean, (0, 1)), row_of(total, (4, 5)) + row_of(between, (0, 1))


def forward_conv(got_ref, weight_ref, gain_ref, bias_ref, cot_ref, act_ref, x_ref, conv_ref, out_ref, stat_ref):
    center, squares = over_pieces(got_ref[:, :, WIDE :], ROWS * LINES)
    spread = jnp.sqrt(squares * (1.0 / COUNTED) + 1e-05)
    stat_ref[0:1, :] = center
    stat_ref[1:2, :] = spread
    x = unwoven(got_ref[:, :, : WIDE])
    x_ref[...] = x.astype(BF16)
    pre = flat(gain_ref) * ((x - center) / spread) + flat(bias_ref)
    act = gelu_of(pre, tanh_of(pre)).astype(BF16)
    act_ref[...] = act
    terms = matmul(act, weight_ref[...], ((1,), (0,)))
    conv = later(terms[:, :MID]) + terms[:, MID : 2 * MID] + earlier(terms[:, 2 * MID :])
    conv_ref[...] = conv
    mean = sum_rows(conv) * (1.0 / ROWS)
    apart = conv - mean
    tile = tile_of(in_two(mean, 128) + in_two(sum_rows(apart * apart), 128), 128).astype(BF16)
    out_ref[:, :, :WIDE] = cot_ref[...]
    out_ref[:, :, WIDE:] = jnp.broadcast_to(tile[None], (PLANES, 8, 128))


def middle_line(got_ref, out_ref):
    mean, squares = over_pieces(got_ref[:, :, WIDE:], ROWS)
    copies(out_ref, slice(0, MID), mean)
    copies(out_ref, slice(MID, 2 * MID), squares)


def middle(
    got_ref,
    plane_ref,
    gain_ref,
    bias_ref,
    proj_ref,
    conv_ref,
    data_ref,
    normed_ref,
    dpre_ref,
    sums_ref,
    spread_ref,
):
    means = got_ref[:, :, :MID]
    center = jnp.sum(means, axis=0) * (1.0 / LINES)
    apart = means - center[None]
    squares = jnp.sum(got_ref[:, :, MID:] + float(ROWS * PLANES) * (apart * apart), axis=0)
    spread = jnp.sqrt(squares * (1.0 / COUNTED) + 1e-05)
    spread_ref[0:1, :] = spread
    normed = (conv_ref[...] - center) / spread
    pre = flat(gain_ref) * normed + flat(bias_ref)
    inner = tanh_of(pre)
    cot = unwoven(plane_ref[:, :, :WIDE]).astype(BF16)
    dpre = matmul(cot, proj_ref[...], ((1,), (1,))) * slope_of(pre, inner)
    copies(sums_ref, slice(0, MID), sum_rows(dpre))
    copies(sums_ref, slice(MID, 2 * MID), sum_rows(dpre * normed))
    normed_ref[...] = normed
    dpre_ref[...] = dpre
    act = gelu_of(pre, inner)
    data_ref[:, :, :128] = woven(act)
    part = matmul(cot, act.astype(BF16), ((0,), (0,))).astype(BF16).reshape(PLANES, 3, 8, MID)
    for k in range(3):
        data_ref[:, :, 128 + MID * k : 128 + MID * (k + 1)] = part[:, k]


def middle_plane(sums_ref, data_ref, out_ref):
    tile = tile_of(in_two(jnp.sum(sums_ref[...], axis=0), 128), 128).astype(BF16)
    out_ref[:, :, : 128 + CH] = data_ref[...]
    out_ref[:, :, 128 + CH :] = jnp.broadcast_to(tile[None], (PLANES, 8, 128))


def filter_parts(
    got_ref,
    gain_ref,
    weight_ref,
    gain_in_ref,
    bias_in_ref,
    dpre_ref,
    normed_ref,
    spread_ref,
    act_in_ref,
    x_ref,
    stat_ref,
    parts_ref,
    act_ref,
    proj_ref,
    back_ref,
):
    tile = jnp.sum(got_ref[:, :, 128 + CH :].astype(F32), axis=0) * (1.0 / COUNTED)
    tile = tile + pltpu.roll(tile, 4, axis=0)
    first, second = row_of(tile, (0, 1)), row_of(tile, (2, 3))
    dconv = dpre_ref[...] - first - normed_ref[...] * second
    dconv = flat(gain_ref) * dconv / spread_ref[0:1, :]
    stacked = jnp.concatenate([earlier(dconv), dconv, later(dconv)], axis=1).astype(BF16)
    part = matmul(act_in_ref[...], stacked, ((0,), (0,)))
    parts_ref[0, :CH, :] = part[:, :WIDE].astype(BF16)
    parts_ref[1, :CH, :] = part[:, WIDE:].astype(BF16)
    act_ref[...] = unwoven(got_ref[:, :, :128]).astype(BF16)
    proj_ref[...] = jnp.sum(got_ref[:, :, 128 : 128 + CH].astype(F32), axis=0)
    normed = (x_ref[...].astype(F32) - stat_ref[0:1, :]) / stat_ref[1:2, :]
    pre = flat(gain_in_ref) * normed + flat(bias_in_ref)
    dpre = matmul(stacked, weight_ref[...], ((1,), (1,))) * slope_of(pre, tanh_of(pre))
    parts_ref[0, CH:, :] = tile_of(in_two(sum_rows(dpre), WIDE), WIDE).astype(BF16)
    parts_ref[1, CH:, :] = tile_of(in_two(sum_rows(dpre * normed), WIDE), WIDE).astype(BF16)
    back_ref[...] = woven(dpre)


def rows_of_128(value):
    return tile_of([value[:, k : k + 128] for k in range(0, value.shape[1], 128)], 128)


def to_plane(parts_ref, back_ref, out_ref):
    both = parts_ref[0].astype(F32) + parts_ref[1].astype(F32)
    pieces = both[:CH].astype(BF16).reshape(PLANES, 3, 8, WIDE)
    for k in range(3):
        out_ref[:, :, WIDE * k : WIDE * (k + 1)] = pieces[:, k]
    out_ref[:, :, 3 * WIDE : 4 * WIDE] = back_ref[...]
    sums = both[CH:] + pltpu.roll(both[CH:], 6, axis=0)
    tile = rows_of_128(row_of(sums, (0, 1))).astype(BF16)
    out_ref[:, :, 4 * WIDE :] = jnp.broadcast_to(tile[None], (PLANES, 8, 128))


def to_line(got_ref, proj_ref, out_ref):
    conv = [
        jnp.sum(got_ref[:, :, WIDE * k : WIDE * (k + 1)].astype(F32), axis=0) for k in range(3)
    ]
    proj = [proj_ref[:, MID * k : MID * (k + 1)] for k in range(3)]
    sums = jnp.sum(got_ref[:, :, 4 * WIDE :].astype(F32), axis=0)

    def own(core, tiles):
        upper = lax.broadcasted_iota(jnp.int32, tiles[0].shape, 0) < 4
        if core == 0:
            return tiles[0], tiles[1]
        return (
            jnp.where(upper, pltpu.roll(tiles[1], 4, axis=0), pltpu.roll(tiles[2], 4, axis=0)),
            pltpu.roll(tiles[2], 4, axis=0),
        )

    blank = jnp.zeros((8, WIDE - MID), F32)
    upper = lax.broadcasted_iota(jnp.int32, (8, WIDE), 0) < 4
    for core in range(2):
        conv_rows, conv_rest = own(core, conv)
        proj_rows, proj_rest = own(core, proj)
        proj_rest = jnp.concatenate([pltpu.roll(proj_rest, 4, axis=0), blank], axis=1)
        rest = jnp.where(upper, conv_rest, proj_rest)
        piece = jnp.concatenate([conv_rows, proj_rows, rest, sums], axis=1).astype(BF16)
        out_ref[core * BATCH : (core + 1) * BATCH] = jnp.broadcast_to(
            piece[None], (BATCH, 8, HALF + WIDE + 128)
        )


def last_rows(
    got_ref, plane_ref, x_ref, cot_ref, proj_ref, gain_ref, act_ref, stat_ref, out_ref, grad_ref, conv_ref, proj_grad_ref
):
    x = x_ref[...].astype(F32)
    update = matmul(act_ref[...], proj_ref[...], ((1,), (0,)))
    out_ref[...] = (x + update).astype(BF16)
    left, right = (
        jnp.sum(got_ref[BATCH * k : BATCH * (k + 1)].astype(F32), axis=0) for k in range(2)
    )
    first, second = (
        row_of(half[:, HALF + WIDE :], range(6)) * (1.0 / COUNTED) for half in (left, right)
    )
    spread = stat_ref[1:2, :]
    normed = (x - stat_ref[0:1, :]) / spread
    dpre = unwoven(plane_ref[:, :, 3 * WIDE : 4 * WIDE])
    change = flat(gain_ref) * (dpre - first - normed * second) / spread
    grad_ref[...] = (cot_ref[...].astype(F32) + change).astype(BF16)
    for k, half in enumerate((left, right)):
        conv_ref[0:8, WIDE * k : WIDE * (k + 1)] = half[:, :WIDE]
        conv_ref[8:12, WIDE * k : WIDE * (k + 1)] = half[:4, HALF : HALF + WIDE]
    both = left + right
    proj_grad_ref[0:8, :] = both[:, WIDE:HALF]
    proj_grad_ref[8:12, :] = both[4:8, HALF : HALF + MID]


def per_device(inputs, cotangent, conv_weight, proj_weight, gain_in, bias_in, gain_mid, bias_mid):
    x = inputs.reshape(ROWS, CH)
    cot = cotangent.reshape(ROWS, CH)
    rows, rows_mid = (ROWS, CH), (ROWS, MID)

    far, near = pl.BlockSpec(memory_space=pltpu.HBM), pl.BlockSpec(memory_space=pltpu.VMEM)
    sums, data, far_cot = pl.pallas_call(
        opening,
        out_shape=(
            jax.ShapeDtypeStruct((LINES, 1, 2 * CH), F32),
            jax.ShapeDtypeStruct((PLANES, 8, WIDE), BF16),
            jax.ShapeDtypeStruct((PLANES, 8, WIDE), BF16),
        ),
        in_specs=[far] * 2,
        out_specs=(near,) * 3,
        scratch_shapes=[
            pltpu.VMEM(rows, BF16),
            pltpu.VMEM(rows, BF16),
            pltpu.SemaphoreType.DMA((2,)),
        ],
        name="opening",
        compiler_params=pltpu.CompilerParams(vmem_limit_bytes=24 << 20),
    )(*(pltpu.with_memory_space_constraint(v, pltpu.HBM) for v in (x, cot)))
    sums = exchange(sums, LINE)
    (both,) = kernel(spread_all, ((PLANES, 8, 2 * WIDE), BF16), name="spread_all")(
        data, near=(sums,)
    )
    both = exchange(both, PLANE)

    act_in, far_x, conv, both, stat_in = kernel(
        forward_conv,
        (rows, BF16),
        (rows, BF16),
        (rows_mid, F32),
        ((PLANES, 8, WIDE + 128), BF16),
        ((8, CH), F32),
        name="forward_conv",
    )(far_cot, near=(both, conv_weight, gain_in, bias_in))
    both = exchange(both, PLANE)
    (sums,) = kernel(middle_line, ((LINES, 1, 2 * MID), F32), name="middle_line")(near=(both,))
    sums = exchange(sums, LINE)

    data, normed_mid, dpre_mid, sums, spread_mid = kernel(
        middle,
        ((PLANES, 8, 128 + CH), BF16),
        (rows_mid, F32),
        (rows_mid, F32),
        ((LINES, 1, 2 * MID), F32),
        ((8, MID), F32),
        name="middle",
    )(conv, near=(sums, both, gain_mid, bias_mid, proj_weight))
    sums = exchange(sums, LINE)
    (both,) = kernel(middle_plane, ((PLANES, 8, CH + 256), BF16), name="middle_plane")(
        data, near=(sums,)
    )
    both = exchange(both, PLANE)

    parts, act_mid, proj_part, back = kernel(
        filter_parts,
        ((2, CH + 8, WIDE), BF16),
        (rows_mid, BF16),
        ((8, CH), F32),
        ((PLANES, 8, WIDE), BF16),
        name="filter_parts",
    )(
        dpre_mid,
        normed_mid,
        spread_mid,
        act_in,
        far_x,
        stat_in,
        near=(both, gain_mid, conv_weight, gain_in, bias_in),
    )
    parts = exchange(parts, "core")
    (plane,) = kernel(to_plane, ((PLANES, 8, 4 * WIDE + 128), BF16), name="to_plane")(
        back, near=(parts,)
    )
    plane = exchange(plane, PLANE)
    (line,) = kernel(to_line, ((LINES, 8, HALF + WIDE + 128), BF16), name="to_line")(
        proj_part, near=(plane,)
    )
    line = exchange(line, LINE)
    block_out, input_grad, conv_grad, proj_grad = kernel(
        last_rows, (rows, BF16), (rows, BF16), ((12, CH), F32), ((12, MID), F32), name="last_rows"
    )(act_mid, stat_in, near=(line, plane, x, cot, proj_weight, gain_in))
    return (
        block_out.reshape(inputs.shape),
        input_grad.reshape(inputs.shape),
        conv_grad,
        proj_grad,
    )


def solution(mesh):
    split = Mesh(mesh.devices.reshape(4, 2, 4, 2, 8), ("x", "z_hi", "z_lo", "core", "dp"))
    rows = P("dp", SEQ, None)
    return jax.shard_map(
        per_device,
        mesh=split,
        in_specs=(rows, rows, P(), P(), P(), P(), P(), P()),
        out_specs=(rows, rows, P(SEQ, None), P(SEQ, None)),
        check_vma=False,
    )
```

```python
import math

import jax
import jax.numpy as jnp
from jax import lax
from jax.experimental import pallas as pl
from jax.experimental.pallas import tpu as pltpu
from jax.sharding import Mesh
from jax.sharding import PartitionSpec as P

SEQ = ("x", "z_hi", "z_lo", "core")
PLANE = ("x", "z_hi", "z_lo")
LINE = ("core", "dp")
BF16, F32 = jnp.bfloat16, jnp.float32
CH, MID = 768, 256
ROWS, SHIFT = 128, 16
PLANES, LINES, BATCH = 32, 16, 8
HALF = 512
COUNTED = 8.0 * 8192.0
COEFF = math.sqrt(2.0 / math.pi)


def exchange(pieces, axes):
    return lax.all_to_all(pieces, axes, split_axis=0, concat_axis=0, tiled=True)


def kernel(body, *outs, name):
    shapes = tuple(jax.ShapeDtypeStruct(shape, dtype) for shape, dtype in outs)
    whole = pl.BlockSpec(memory_space=pltpu.VMEM)

    def call(*args, near=()):
        near = tuple(pltpu.with_memory_space_constraint(a, pltpu.VMEM) for a in near)
        args = (*near, *args)
        return pl.pallas_call(
            body,
            out_shape=shapes,
            in_specs=[whole] * len(args),
            out_specs=(whole,) * len(shapes),
            name=name,
            compiler_params=pltpu.CompilerParams(vmem_limit_bytes=24 << 20),
        )(*args)

    return call


def matmul(a, b, dims):
    return lax.dot_general(a, b, (dims, ((), ())), preferred_element_type=F32)


def later(x):
    return jnp.concatenate([jnp.zeros_like(x[:SHIFT]), x[:-SHIFT]], axis=0)


def earlier(x):
    return jnp.concatenate([x[SHIFT:], jnp.zeros_like(x[:SHIFT])], axis=0)


def woven(value):
    width = value.shape[1] // 2
    tiles = value.astype(F32).reshape(ROWS // 8, 8, 2 * width)
    a, b = tiles[:, :, :width], tiles[:, :, width:]
    upper = lax.broadcasted_iota(jnp.int32, a.shape, 1) < 4
    even = jnp.where(upper, a, pltpu.roll(b, 4, axis=1))
    odd = jnp.where(upper, pltpu.roll(a, 4, axis=1), b)
    return jnp.stack([even, odd], axis=1).reshape(PLANES, 8, width).astype(BF16)


def unwoven(pieces):
    width = pieces.shape[2]
    pairs = pieces.astype(F32).reshape(ROWS // 8, 2, 8, width)
    even, odd = pairs[:, 0], pairs[:, 1]
    upper = lax.broadcasted_iota(jnp.int32, even.shape, 1) < 4
    a = jnp.where(upper, even, pltpu.roll(odd, 4, axis=1))
    b = jnp.where(upper, pltpu.roll(even, 4, axis=1), odd)
    return jnp.concatenate([a.reshape(ROWS, width), b.reshape(ROWS, width)], axis=1)


def rounded(value):
    return value.astype(BF16).astype(F32)


def tile_of(pieces, width):
    row = lax.broadcasted_iota(jnp.int32, (8, width), 0)
    tile = jnp.zeros((8, width), F32)
    for k, piece in enumerate(pieces):
        tile = jnp.where(row == k, piece, tile)
    return tile


def in_two(value, width):
    high = rounded(value)
    return [
        part[:, k : k + width] for part in (high, value - high) for k in range(0, value.shape[1], width)
    ]


def row_of(tile, rows):
    return jnp.concatenate([tile[k : k + 1] for k in rows], axis=1)


def sum_rows(value):
    return jnp.sum(value, axis=0, keepdims=True)


def flat(ref):
    return ref[...].reshape(1, ref.shape[0])


def copies(ref, index, row):
    ref[:, :, index] = jnp.broadcast_to(row, (ref.shape[0], 1, row.shape[1]))


def tanh_of(value):
    return jnp.tanh(COEFF * (value + 0.044715 * value * value * value))


def gelu_of(value, inner):
    return 0.5 * value * (1.0 + inner)


def slope_of(value, inner):
    return 0.5 * (1.0 + inner) + 0.5 * value * (1.0 - inner * inner) * COEFF * (
        1.0 + 3.0 * 0.044715 * value * value
    )


def opening(x_hbm, cot_hbm, proj_hbm, sums_ref, data_ref, dact_ref, x_ref, cot_ref, proj_ref, sems):
    pairs = ((x_hbm, x_ref), (cot_hbm, cot_ref), (proj_hbm, proj_ref))
    loads = [pltpu.make_async_copy(*pair, sems.at[k]) for k, pair in enumerate(pairs)]
    for load in loads:
        load.start()
    loads[0].wait()
    x = x_ref[...].astype(F32)
    mean = sum_rows(x) * (1.0 / ROWS)
    apart = x - mean
    copies(sums_ref, slice(0, CH), mean)
    copies(sums_ref, slice(CH, 2 * CH), sum_rows(apart * apart))
    data_ref[...] = woven(x)
    loads[1].wait()
    loads[2].wait()
    dact_ref[...] = woven(matmul(cot_ref[...], proj_ref[...], ((1,), (1,))))


def spread_all(sums_ref, data_ref, out_ref):
    sums = sums_ref[...]
    means = sums[:, :, :CH]
    mean = jnp.sum(means, axis=0) * (1.0 / LINES)
    apart = means - mean[None]
    squares = jnp.sum(sums[:, :, CH:] + float(ROWS) * (apart * apart), axis=0)
    tile = tile_of(in_two(mean, CH // 2) + in_two(squares, CH // 2), CH // 2).astype(BF16)
    out_ref[:, :, : CH // 2] = data_ref[...]
    out_ref[:, :, CH // 2 :] = jnp.broadcast_to(tile[None], (PLANES, 8, CH // 2))


def over_pieces(parts, count):
    parts = parts.astype(F32)
    parts = parts + pltpu.roll(parts, 6, axis=1)
    total = jnp.sum(parts, axis=0)
    mean = total * (1.0 / PLANES)
    apart = parts - mean[None]
    between = jnp.sum(apart * apart, axis=0) * float(count)
    return row_of(mean, (0, 1)), row_of(total, (4, 5)) + row_of(between, (0, 1))


def forward_conv(got_ref, weight_ref, gain_ref, bias_ref, dact_ref, act_ref, x_ref, conv_ref, out_ref, stat_ref):
    center, squares = over_pieces(got_ref[:, :, CH // 2 :], ROWS * LINES)
    spread = jnp.sqrt(squares * (1.0 / COUNTED) + 1e-05)
    stat_ref[0:1, :] = center
    stat_ref[1:2, :] = spread
    x = unwoven(got_ref[:, :, : CH // 2])
    x_ref[...] = x.astype(BF16)
    pre = flat(gain_ref) * ((x - center) / spread) + flat(bias_ref)
    act = gelu_of(pre, tanh_of(pre)).astype(BF16)
    act_ref[...] = act
    terms = matmul(act, weight_ref[...], ((1,), (0,)))
    conv = later(terms[:, :MID]) + terms[:, MID : 2 * MID] + earlier(terms[:, 2 * MID :])
    conv_ref[...] = conv
    mean = sum_rows(conv) * (1.0 / ROWS)
    apart = conv - mean
    tile = tile_of(in_two(mean, 128) + in_two(sum_rows(apart * apart), 128), 128).astype(BF16)
    out_ref[:, :, :128] = dact_ref[...]
    out_ref[:, :, 128:] = jnp.broadcast_to(tile[None], (PLANES, 8, 128))


def middle_line(got_ref, out_ref):
    mean, squares = over_pieces(got_ref[:, :, 128:], ROWS)
    copies(out_ref, slice(0, MID), mean)
    copies(out_ref, slice(MID, 2 * MID), squares)


def middle(got_ref, plane_ref, gain_ref, bias_ref, conv_ref, act_ref, normed_ref, dpre_ref, sums_ref, spread_ref):
    means = got_ref[:, :, :MID]
    center = jnp.sum(means, axis=0) * (1.0 / LINES)
    apart = means - center[None]
    squares = jnp.sum(got_ref[:, :, MID:] + float(ROWS * PLANES) * (apart * apart), axis=0)
    spread = jnp.sqrt(squares * (1.0 / COUNTED) + 1e-05)
    spread_ref[0:1, :] = spread
    normed = (conv_ref[...] - center) / spread
    pre = flat(gain_ref) * normed + flat(bias_ref)
    inner = tanh_of(pre)
    dpre = unwoven(plane_ref[:, :, :128]) * slope_of(pre, inner)
    copies(sums_ref, slice(0, MID), sum_rows(dpre))
    copies(sums_ref, slice(MID, 2 * MID), sum_rows(dpre * normed))
    normed_ref[...] = normed
    dpre_ref[...] = dpre
    act_ref[...] = woven(gelu_of(pre, inner))


def middle_plane(sums_ref, act_ref, out_ref):
    tile = tile_of(in_two(jnp.sum(sums_ref[...], axis=0), 128), 128).astype(BF16)
    out_ref[:, :, :128] = act_ref[...]
    out_ref[:, :, 128:] = jnp.broadcast_to(tile[None], (PLANES, 8, 128))


def in_four(value):
    blank = jnp.zeros((1, HALF - CH // 2), F32)
    return tile_of([jnp.concatenate([row, blank], axis=1) for row in in_two(value, CH // 2)], HALF)


def from_four(tile):
    return jnp.concatenate([tile[k : k + 1, : CH // 2] + tile[k + 2 : k + 3, : CH // 2] for k in range(2)], axis=1)


def filter_parts(
    got_ref,
    gain_ref,
    cot_ref,
    weight_ref,
    gain_in_ref,
    bias_in_ref,
    dpre_ref,
    normed_ref,
    spread_ref,
    act_in_ref,
    x_ref,
    stat_ref,
    parts_ref,
    act_ref,
    back_ref,
):
    tile = jnp.sum(got_ref[:, :, 128:].astype(F32), axis=0) * (1.0 / COUNTED)
    tile = tile + pltpu.roll(tile, 4, axis=0)
    first, second = row_of(tile, (0, 1)), row_of(tile, (2, 3))
    dconv = dpre_ref[...] - first - normed_ref[...] * second
    dconv = flat(gain_ref) * dconv / spread_ref[0:1, :]
    stacked = jnp.concatenate([earlier(dconv), dconv, later(dconv)], axis=1).astype(BF16)
    conv_part = matmul(act_in_ref[...], stacked, ((0,), (0,)))
    parts_ref[0, :CH, :] = conv_part[:, :HALF].astype(BF16)
    parts_ref[1, :CH, : HALF - MID] = conv_part[:, HALF:].astype(BF16)
    act = unwoven(got_ref[:, :, :128]).astype(BF16)
    act_ref[...] = act
    proj_part = matmul(cot_ref[...], act, ((0,), (0,)))
    parts_ref[1, :CH, HALF - MID :] = proj_part.astype(BF16)
    normed = (x_ref[...].astype(F32) - stat_ref[0:1, :]) / stat_ref[1:2, :]
    pre = flat(gain_in_ref) * normed + flat(bias_in_ref)
    dpre = matmul(stacked, weight_ref[...], ((1,), (1,))) * slope_of(pre, tanh_of(pre))
    parts_ref[0, CH:, :] = in_four(sum_rows(dpre)).astype(BF16)
    parts_ref[1, CH:, :] = in_four(sum_rows(dpre * normed)).astype(BF16)
    back_ref[...] = woven(dpre)


def to_plane(parts_ref, back_ref, out_hbm, out_ref, sem):
    both = parts_ref[0].astype(F32) + parts_ref[1].astype(F32)
    pieces = both[:CH].astype(BF16).reshape(PLANES, 3, 8, HALF)
    for k in range(3):
        out_ref[:, :, HALF * k : HALF * (k + 1)] = pieces[:, k]
    begin = 3 * HALF + CH // 2
    out_ref[:, :, 3 * HALF : begin] = back_ref[...]
    sums = from_four(both[CH:])
    tile = tile_of([sums[:, k : k + 128] for k in range(0, CH, 128)], 128).astype(BF16)
    out_ref[:, :, begin:] = jnp.broadcast_to(tile[None], (PLANES, 8, 128))
    store = pltpu.make_async_copy(out_ref, out_hbm, sem)
    store.start()
    store.wait()


def to_line(got_ref, out_ref):
    tiles = [
        jnp.sum(got_ref[:, :, HALF * k : HALF * (k + 1)].astype(F32), axis=0) for k in range(3)
    ]
    sums = jnp.sum(got_ref[:, :, 3 * HALF + CH // 2 :].astype(F32), axis=0)
    low = pltpu.roll(in_four(row_of(sums, range(6))), 4, axis=0)
    upper = lax.broadcasted_iota(jnp.int32, (8, HALF), 0) < 4
    turned = [pltpu.roll(tile, 4, axis=0) for tile in tiles]
    own = (
        (tiles[0], jnp.where(upper, tiles[1], low)),
        (jnp.where(upper, turned[1], turned[2]), jnp.where(upper, turned[2], low)),
    )
    for core in range(2):
        for k in range(2):
            out_ref[core * BATCH : (core + 1) * BATCH, :, HALF * k : HALF * (k + 1)] = (
                jnp.broadcast_to(own[core][k].astype(BF16)[None], (BATCH, 8, HALF))
            )


def last_rows(
    got_ref, plane_ref, x_ref, cot_ref, proj_ref, gain_ref, act_ref, stat_ref, out_ref, grad_ref, conv_ref, proj_grad_ref
):
    x = x_ref[...].astype(F32)
    update = matmul(act_ref[...], proj_ref[...], ((1,), (0,)))
    out_ref[...] = (x + update).astype(BF16)
    left, right = (
        jnp.sum(got_ref[BATCH * k : BATCH * (k + 1)].astype(F32), axis=0) for k in range(2)
    )
    first, second = (from_four(half[4:8, HALF:]) * (1.0 / COUNTED) for half in (left, right))
    spread = stat_ref[1:2, :]
    normed = (x - stat_ref[0:1, :]) / spread
    dpre = unwoven(plane_ref[:, :, 3 * HALF : 3 * HALF + CH // 2])
    change = flat(gain_ref) * (dpre - first - normed * second) / spread
    grad_ref[...] = (cot_ref[...].astype(F32) + change).astype(BF16)
    for rows, lanes, count in ((slice(0, 8), 0, 8), (slice(8, 12), HALF, 4)):
        conv_ref[rows, :HALF] = left[:count, lanes : lanes + HALF]
        conv_ref[rows, HALF:] = right[:count, lanes : lanes + CH - HALF]
        proj_grad_ref[rows, :] = right[:count, lanes + CH - HALF : lanes + HALF]


def per_device(inputs, cotangent, conv_weight, proj_weight, gain_in, bias_in, gain_mid, bias_mid):
    x = inputs.reshape(ROWS, CH)
    cot = cotangent.reshape(ROWS, CH)
    rows, rows_mid = (ROWS, CH), (ROWS, MID)

    far, near = pl.BlockSpec(memory_space=pltpu.HBM), pl.BlockSpec(memory_space=pltpu.VMEM)
    sums, data, dact = pl.pallas_call(
        opening,
        out_shape=(
            jax.ShapeDtypeStruct((LINES, 1, 2 * CH), F32),
            jax.ShapeDtypeStruct((PLANES, 8, CH // 2), BF16),
            jax.ShapeDtypeStruct((PLANES, 8, 128), BF16),
        ),
        in_specs=[far] * 3,
        out_specs=(near,) * 3,
        scratch_shapes=[
            pltpu.VMEM(rows, BF16),
            pltpu.VMEM(rows, BF16),
            pltpu.VMEM((MID, CH), BF16),
            pltpu.SemaphoreType.DMA((3,)),
        ],
        name="opening",
        compiler_params=pltpu.CompilerParams(vmem_limit_bytes=24 << 20),
    )(*(pltpu.with_memory_space_constraint(v, pltpu.HBM) for v in (x, cot, proj_weight)))
    sums = exchange(sums, LINE)
    (both,) = kernel(spread_all, ((PLANES, 8, CH), BF16), name="spread_all")(
        data, near=(sums,)
    )
    both = exchange(both, PLANE)

    act_in, far_x, conv, both, stat_in = kernel(
        forward_conv,
        (rows, BF16),
        (rows, BF16),
        (rows_mid, F32),
        ((PLANES, 8, 256), BF16),
        ((8, CH), F32),
        name="forward_conv",
    )(dact, near=(both, conv_weight, gain_in, bias_in))
    both = exchange(both, PLANE)
    (sums,) = kernel(middle_line, ((LINES, 1, 2 * MID), F32), name="middle_line")(near=(both,))
    sums = exchange(sums, LINE)

    act_mid, normed_mid, dpre_mid, sums, spread_mid = kernel(
        middle,
        ((PLANES, 8, 128), BF16),
        (rows_mid, F32),
        (rows_mid, F32),
        ((LINES, 1, 2 * MID), F32),
        ((8, MID), F32),
        name="middle",
    )(conv, near=(sums, both, gain_mid, bias_mid))
    sums = exchange(sums, LINE)
    (both,) = kernel(middle_plane, ((PLANES, 8, 256), BF16), name="middle_plane")(
        act_mid, near=(sums,)
    )
    both = exchange(both, PLANE)

    parts, act_mid, back = kernel(
        filter_parts,
        ((2, CH + 8, HALF), BF16),
        (rows_mid, BF16),
        ((PLANES, 8, CH // 2), BF16),
        name="filter_parts",
    )(
        dpre_mid,
        normed_mid,
        spread_mid,
        act_in,
        far_x,
        stat_in,
        near=(both, gain_mid, cot, conv_weight, gain_in, bias_in),
    )
    parts = exchange(parts, "core")
    shape = (PLANES, 8, 3 * HALF + CH // 2 + 128)
    plane = pl.pallas_call(
        to_plane,
        out_shape=pltpu.HBM(shape, BF16),
        in_specs=[near] * 2,
        out_specs=far,
        scratch_shapes=[pltpu.VMEM(shape, BF16), pltpu.SemaphoreType.DMA],
        name="to_plane",
        compiler_params=pltpu.CompilerParams(vmem_limit_bytes=24 << 20),
    )(pltpu.with_memory_space_constraint(parts, pltpu.VMEM), back)
    plane = exchange(plane, PLANE)
    (line,) = kernel(to_line, ((LINES, 8, 2 * HALF), BF16), name="to_line")(near=(plane,))
    line = exchange(line, LINE)
    block_out, input_grad, conv_grad, proj_grad = kernel(
        last_rows, (rows, BF16), (rows, BF16), ((12, CH), F32), ((12, MID), F32), name="last_rows"
    )(act_mid, stat_in, near=(line, plane, x, cot, proj_weight, gain_in))
    return (
        block_out.reshape(inputs.shape),
        input_grad.reshape(inputs.shape),
        conv_grad,
        proj_grad,
    )


def solution(mesh):
    split = Mesh(mesh.devices.reshape(4, 2, 4, 2, 8), ("x", "z_hi", "z_lo", "core", "dp"))
    rows = P("dp", SEQ, None)
    return jax.shard_map(
        per_device,
        mesh=split,
        in_specs=(rows, rows, P(), P(), P(), P(), P(), P()),
        out_specs=(rows, rows, P(SEQ, None), P(SEQ, None)),
        check_vma=False,
    )
```

```python
import math

import jax
import jax.numpy as jnp
from jax import lax
from jax.experimental import pallas as pl
from jax.experimental.pallas import tpu as pltpu
from jax.sharding import Mesh
from jax.sharding import PartitionSpec as P

SEQ = ("x", "z_hi", "z_lo", "core")
PLANE = ("x", "z_hi", "z_lo")
LINE = ("core", "dp")
BF16, F32 = jnp.bfloat16, jnp.float32
CH, MID = 768, 256
ROWS, SHIFT = 128, 16
PLANES, LINES, BATCH = 32, 16, 8
HALF = 512
COUNTED = 8.0 * 8192.0
COEFF = math.sqrt(2.0 / math.pi)


def exchange(pieces, axes):
    return lax.all_to_all(pieces, axes, split_axis=0, concat_axis=0, tiled=True)


def kernel(body, *outs, name):
    shapes = tuple(jax.ShapeDtypeStruct(shape, dtype) for shape, dtype in outs)
    whole = pl.BlockSpec(memory_space=pltpu.VMEM)

    def call(*args, near=()):
        near = tuple(pltpu.with_memory_space_constraint(a, pltpu.VMEM) for a in near)
        args = (*near, *args)
        return pl.pallas_call(
            body,
            out_shape=shapes,
            in_specs=[whole] * len(args),
            out_specs=(whole,) * len(shapes),
            name=name,
            compiler_params=pltpu.CompilerParams(vmem_limit_bytes=24 << 20),
        )(*args)

    return call


def matmul(a, b, dims):
    return lax.dot_general(a, b, (dims, ((), ())), preferred_element_type=F32)


def later(x):
    return jnp.concatenate([jnp.zeros_like(x[:SHIFT]), x[:-SHIFT]], axis=0)


def earlier(x):
    return jnp.concatenate([x[SHIFT:], jnp.zeros_like(x[:SHIFT])], axis=0)


def woven(value):
    width = value.shape[1] // 2
    tiles = value.astype(F32).reshape(ROWS // 8, 8, 2 * width)
    a, b = tiles[:, :, :width], tiles[:, :, width:]
    upper = lax.broadcasted_iota(jnp.int32, a.shape, 1) < 4
    even = jnp.where(upper, a, pltpu.roll(b, 4, axis=1))
    odd = jnp.where(upper, pltpu.roll(a, 4, axis=1), b)
    return jnp.stack([even, odd], axis=1).reshape(PLANES, 8, width).astype(BF16)


def unwoven(pieces):
    width = pieces.shape[2]
    pairs = pieces.astype(F32).reshape(ROWS // 8, 2, 8, width)
    even, odd = pairs[:, 0], pairs[:, 1]
    upper = lax.broadcasted_iota(jnp.int32, even.shape, 1) < 4
    a = jnp.where(upper, even, pltpu.roll(odd, 4, axis=1))
    b = jnp.where(upper, pltpu.roll(even, 4, axis=1), odd)
    return jnp.concatenate([a.reshape(ROWS, width), b.reshape(ROWS, width)], axis=1)


def rounded(value):
    return value.astype(BF16).astype(F32)


def tile_of(pieces, width):
    row = lax.broadcasted_iota(jnp.int32, (8, width), 0)
    tile = jnp.zeros((8, width), F32)
    for k, piece in enumerate(pieces):
        tile = jnp.where(row == k, piece, tile)
    return tile


def in_two(value, width):
    high = rounded(value)
    return [
        part[:, k : k + width] for part in (high, value - high) for k in range(0, value.shape[1], width)
    ]


def row_of(tile, rows):
    return jnp.concatenate([tile[k : k + 1] for k in rows], axis=1)


def sum_rows(value):
    return jnp.sum(value, axis=0, keepdims=True)


def flat(ref):
    return ref[...].reshape(1, ref.shape[0])


def copies(ref, index, row):
    ref[:, :, index] = jnp.broadcast_to(row, (ref.shape[0], 1, row.shape[1]))


def tanh_of(value):
    return jnp.tanh(COEFF * (value + 0.044715 * value * value * value))


def gelu_of(value, inner):
    return 0.5 * value * (1.0 + inner)


def slope_of(value, inner):
    return 0.5 * (1.0 + inner) + 0.5 * value * (1.0 - inner * inner) * COEFF * (
        1.0 + 3.0 * 0.044715 * value * value
    )


def opening(x_hbm, cot_hbm, proj_hbm, sums_ref, data_ref, dact_ref, x_ref, cot_ref, proj_ref, sems):
    pairs = ((x_hbm, x_ref), (cot_hbm, cot_ref), (proj_hbm, proj_ref))
    loads = [pltpu.make_async_copy(*pair, sems.at[k]) for k, pair in enumerate(pairs)]
    for load in loads:
        load.start()
    loads[0].wait()
    x = x_ref[...].astype(F32)
    mean = sum_rows(x) * (1.0 / ROWS)
    apart = x - mean
    copies(sums_ref, slice(0, CH), mean)
    copies(sums_ref, slice(CH, 2 * CH), sum_rows(apart * apart))
    data_ref[...] = woven(x)
    loads[1].wait()
    loads[2].wait()
    dact_ref[...] = woven(matmul(cot_ref[...], proj_ref[...], ((1,), (1,))))


def spread_all(sums_ref, data_ref, out_ref):
    sums = sums_ref[...]
    means = sums[:, :, :CH]
    mean = jnp.sum(means, axis=0) * (1.0 / LINES)
    apart = means - mean[None]
    squares = jnp.sum(sums[:, :, CH:] + float(ROWS) * (apart * apart), axis=0)
    tile = tile_of(in_two(mean, CH // 2) + in_two(squares, CH // 2), CH // 2).astype(BF16)
    out_ref[:, :, : CH // 2] = data_ref[...]
    out_ref[:, :, CH // 2 :] = jnp.broadcast_to(tile[None], (PLANES, 8, CH // 2))


def over_pieces(parts, count):
    parts = parts.astype(F32)
    parts = parts + pltpu.roll(parts, 6, axis=1)
    total = jnp.sum(parts, axis=0)
    mean = total * (1.0 / PLANES)
    apart = parts - mean[None]
    between = jnp.sum(apart * apart, axis=0) * float(count)
    return row_of(mean, (0, 1)), row_of(total, (4, 5)) + row_of(between, (0, 1))


def forward_conv(got_ref, weight_ref, gain_ref, bias_ref, dact_ref, act_ref, x_ref, conv_ref, out_ref, stat_ref):
    center, squares = over_pieces(got_ref[:, :, CH // 2 :], ROWS * LINES)
    spread = jnp.sqrt(squares * (1.0 / COUNTED) + 1e-05)
    stat_ref[0:1, :] = center
    stat_ref[1:2, :] = spread
    x = unwoven(got_ref[:, :, : CH // 2])
    x_ref[...] = x.astype(BF16)
    pre = flat(gain_ref) * ((x - center) / spread) + flat(bias_ref)
    act = gelu_of(pre, tanh_of(pre)).astype(BF16)
    act_ref[...] = act
    terms = matmul(act, weight_ref[...], ((1,), (0,)))
    conv = later(terms[:, :MID]) + terms[:, MID : 2 * MID] + earlier(terms[:, 2 * MID :])
    conv_ref[...] = conv
    mean = sum_rows(conv) * (1.0 / ROWS)
    apart = conv - mean
    tile = tile_of(in_two(mean, 128) + in_two(sum_rows(apart * apart), 128), 128).astype(BF16)
    out_ref[:, :, :128] = dact_ref[...]
    out_ref[:, :, 128:] = jnp.broadcast_to(tile[None], (PLANES, 8, 128))


def middle_line(got_ref, out_ref):
    mean, squares = over_pieces(got_ref[:, :, 128:], ROWS)
    copies(out_ref, slice(0, MID), mean)
    copies(out_ref, slice(MID, 2 * MID), squares)


def middle(got_ref, plane_ref, gain_ref, bias_ref, conv_ref, act_ref, normed_ref, dpre_ref, sums_ref, spread_ref):
    means = got_ref[:, :, :MID]
    center = jnp.sum(means, axis=0) * (1.0 / LINES)
    apart = means - center[None]
    squares = jnp.sum(got_ref[:, :, MID:] + float(ROWS * PLANES) * (apart * apart), axis=0)
    spread = jnp.sqrt(squares * (1.0 / COUNTED) + 1e-05)
    spread_ref[0:1, :] = spread
    normed = (conv_ref[...] - center) / spread
    pre = flat(gain_ref) * normed + flat(bias_ref)
    inner = tanh_of(pre)
    dpre = unwoven(plane_ref[:, :, :128]) * slope_of(pre, inner)
    copies(sums_ref, slice(0, MID), sum_rows(dpre))
    copies(sums_ref, slice(MID, 2 * MID), sum_rows(dpre * normed))
    normed_ref[...] = normed
    dpre_ref[...] = dpre
    act_ref[...] = woven(gelu_of(pre, inner))


def middle_plane(sums_ref, act_ref, out_ref):
    tile = tile_of(in_two(jnp.sum(sums_ref[...], axis=0), 128), 128).astype(BF16)
    out_ref[:, :, :128] = act_ref[...]
    out_ref[:, :, 128:] = jnp.broadcast_to(tile[None], (PLANES, 8, 128))


def in_four(value):
    blank = jnp.zeros((1, HALF - CH // 2), F32)
    return tile_of([jnp.concatenate([row, blank], axis=1) for row in in_two(value, CH // 2)], HALF)


def from_four(tile):
    return jnp.concatenate([tile[k : k + 1, : CH // 2] + tile[k + 2 : k + 3, : CH // 2] for k in range(2)], axis=1)


def filter_parts(
    got_ref,
    gain_ref,
    cot_ref,
    weight_ref,
    gain_in_ref,
    bias_in_ref,
    dpre_ref,
    normed_ref,
    spread_ref,
    act_in_ref,
    x_ref,
    stat_ref,
    parts_ref,
    act_ref,
    back_ref,
):
    tile = jnp.sum(got_ref[:, :, 128:].astype(F32), axis=0) * (1.0 / COUNTED)
    tile = tile + pltpu.roll(tile, 4, axis=0)
    first, second = row_of(tile, (0, 1)), row_of(tile, (2, 3))
    dconv = dpre_ref[...] - first - normed_ref[...] * second
    dconv = flat(gain_ref) * dconv / spread_ref[0:1, :]
    stacked = jnp.concatenate([earlier(dconv), dconv, later(dconv)], axis=1).astype(BF16)
    conv_part = matmul(act_in_ref[...], stacked, ((0,), (0,)))
    parts_ref[0, :CH, :] = conv_part[:, :HALF].astype(BF16)
    parts_ref[1, :CH, : HALF - MID] = conv_part[:, HALF:].astype(BF16)
    act = unwoven(got_ref[:, :, :128]).astype(BF16)
    act_ref[...] = act
    proj_part = matmul(cot_ref[...], act, ((0,), (0,)))
    parts_ref[1, :CH, HALF - MID :] = proj_part.astype(BF16)
    normed = (x_ref[...].astype(F32) - stat_ref[0:1, :]) / stat_ref[1:2, :]
    pre = flat(gain_in_ref) * normed + flat(bias_in_ref)
    dpre = matmul(stacked, weight_ref[...], ((1,), (1,))) * slope_of(pre, tanh_of(pre))
    parts_ref[0, CH:, :] = in_four(sum_rows(dpre)).astype(BF16)
    parts_ref[1, CH:, :] = in_four(sum_rows(dpre * normed)).astype(BF16)
    back_ref[...] = woven(dpre)


def to_plane(parts_ref, back_ref, out_ref):
    both = parts_ref[0].astype(F32) + parts_ref[1].astype(F32)
    pieces = both[:CH].astype(BF16).reshape(PLANES, 3, 8, HALF)
    for k in range(3):
        out_ref[:, :, HALF * k : HALF * (k + 1)] = pieces[:, k]
    begin = 3 * HALF + CH // 2
    out_ref[:, :, 3 * HALF : begin] = back_ref[...]
    sums = from_four(both[CH:])
    tile = tile_of([sums[:, k : k + 128] for k in range(0, CH, 128)], 128).astype(BF16)
    out_ref[:, :, begin:] = jnp.broadcast_to(tile[None], (PLANES, 8, 128))


def to_line(got_ref, out_ref):
    tiles = [
        jnp.sum(got_ref[:, :, HALF * k : HALF * (k + 1)].astype(F32), axis=0) for k in range(3)
    ]
    sums = jnp.sum(got_ref[:, :, 3 * HALF + CH // 2 :].astype(F32), axis=0)
    low = pltpu.roll(in_four(row_of(sums, range(6))), 4, axis=0)
    upper = lax.broadcasted_iota(jnp.int32, (8, HALF), 0) < 4
    turned = [pltpu.roll(tile, 4, axis=0) for tile in tiles]
    own = (
        (tiles[0], jnp.where(upper, tiles[1], low)),
        (jnp.where(upper, turned[1], turned[2]), jnp.where(upper, turned[2], low)),
    )
    for core in range(2):
        for k in range(2):
            out_ref[core * BATCH : (core + 1) * BATCH, :, HALF * k : HALF * (k + 1)] = (
                jnp.broadcast_to(own[core][k].astype(BF16)[None], (BATCH, 8, HALF))
            )


def last_rows(
    got_ref,
    plane_ref,
    x_ref,
    cot_ref,
    proj_ref,
    gain_ref,
    act_ref,
    stat_ref,
    out_hbm,
    grad_hbm,
    conv_hbm,
    proj_hbm,
    out_ref,
    grad_ref,
    conv_ref,
    proj_grad_ref,
    sems,
):
    pairs = ((out_ref, out_hbm), (conv_ref, conv_hbm), (proj_grad_ref, proj_hbm), (grad_ref, grad_hbm))
    stores = [pltpu.make_async_copy(*pair, sems.at[k]) for k, pair in enumerate(pairs)]
    update = matmul(act_ref[...], proj_ref[...], ((1,), (0,)))
    out_ref[...] = (x_ref[...].astype(F32) + update).astype(BF16)
    stores[0].start()
    left, right = (
        jnp.sum(got_ref[BATCH * k : BATCH * (k + 1)].astype(F32), axis=0) for k in range(2)
    )
    for rows, lanes, count in ((slice(0, 8), 0, 8), (slice(8, 12), HALF, 4)):
        conv_ref[rows, :HALF] = left[:count, lanes : lanes + HALF]
        conv_ref[rows, HALF:] = right[:count, lanes : lanes + CH - HALF]
        proj_grad_ref[rows, :] = right[:count, lanes + CH - HALF : lanes + HALF]
    stores[1].start()
    stores[2].start()
    first, second = (from_four(half[4:8, HALF:]) * (1.0 / COUNTED) for half in (left, right))
    spread = stat_ref[1:2, :]
    normed = (x_ref[...].astype(F32) - stat_ref[0:1, :]) / spread
    dpre = unwoven(plane_ref[:, :, 3 * HALF : 3 * HALF + CH // 2])
    change = flat(gain_ref) * (dpre - first - normed * second) / spread
    grad_ref[...] = (cot_ref[...].astype(F32) + change).astype(BF16)
    stores[3].start()
    for store in stores:
        store.wait()


def per_device(inputs, cotangent, conv_weight, proj_weight, gain_in, bias_in, gain_mid, bias_mid):
    x = inputs.reshape(ROWS, CH)
    cot = cotangent.reshape(ROWS, CH)
    rows, rows_mid = (ROWS, CH), (ROWS, MID)

    far, near = pl.BlockSpec(memory_space=pltpu.HBM), pl.BlockSpec(memory_space=pltpu.VMEM)
    sums, data, dact = pl.pallas_call(
        opening,
        out_shape=(
            jax.ShapeDtypeStruct((LINES, 1, 2 * CH), F32),
            jax.ShapeDtypeStruct((PLANES, 8, CH // 2), BF16),
            jax.ShapeDtypeStruct((PLANES, 8, 128), BF16),
        ),
        in_specs=[far] * 3,
        out_specs=(near,) * 3,
        scratch_shapes=[
            pltpu.VMEM(rows, BF16),
            pltpu.VMEM(rows, BF16),
            pltpu.VMEM((MID, CH), BF16),
            pltpu.SemaphoreType.DMA((3,)),
        ],
        name="opening",
        compiler_params=pltpu.CompilerParams(vmem_limit_bytes=24 << 20),
    )(*(pltpu.with_memory_space_constraint(v, pltpu.HBM) for v in (x, cot, proj_weight)))
    sums = exchange(sums, LINE)
    (both,) = kernel(spread_all, ((PLANES, 8, CH), BF16), name="spread_all")(
        data, near=(sums,)
    )
    both = exchange(both, PLANE)

    act_in, far_x, conv, both, stat_in = kernel(
        forward_conv,
        (rows, BF16),
        (rows, BF16),
        (rows_mid, F32),
        ((PLANES, 8, 256), BF16),
        ((8, CH), F32),
        name="forward_conv",
    )(dact, near=(both, conv_weight, gain_in, bias_in))
    both = exchange(both, PLANE)
    (sums,) = kernel(middle_line, ((LINES, 1, 2 * MID), F32), name="middle_line")(near=(both,))
    sums = exchange(sums, LINE)

    act_mid, normed_mid, dpre_mid, sums, spread_mid = kernel(
        middle,
        ((PLANES, 8, 128), BF16),
        (rows_mid, F32),
        (rows_mid, F32),
        ((LINES, 1, 2 * MID), F32),
        ((8, MID), F32),
        name="middle",
    )(conv, near=(sums, both, gain_mid, bias_mid))
    sums = exchange(sums, LINE)
    (both,) = kernel(middle_plane, ((PLANES, 8, 256), BF16), name="middle_plane")(
        act_mid, near=(sums,)
    )
    both = exchange(both, PLANE)

    parts, act_mid, back = kernel(
        filter_parts,
        ((2, CH + 8, HALF), BF16),
        (rows_mid, BF16),
        ((PLANES, 8, CH // 2), BF16),
        name="filter_parts",
    )(
        dpre_mid,
        normed_mid,
        spread_mid,
        act_in,
        far_x,
        stat_in,
        near=(both, gain_mid, cot, conv_weight, gain_in, bias_in),
    )
    parts = exchange(parts, "core")
    (plane,) = kernel(to_plane, ((PLANES, 8, 3 * HALF + CH // 2 + 128), BF16), name="to_plane")(
        back, near=(parts,)
    )
    plane = exchange(plane, PLANE)
    (line,) = kernel(to_line, ((LINES, 8, 2 * HALF), BF16), name="to_line")(near=(plane,))
    line = exchange(line, LINE)
    ends = ((rows, BF16), (rows, BF16), ((12, CH), F32), ((12, MID), F32))
    held = (line, plane, x, cot, proj_weight, gain_in)
    block_out, input_grad, conv_grad, proj_grad = pl.pallas_call(
        last_rows,
        out_shape=tuple(pltpu.HBM(*end) for end in ends),
        in_specs=[near] * 8,
        out_specs=(far,) * 4,
        scratch_shapes=[*(pltpu.VMEM(*end) for end in ends), pltpu.SemaphoreType.DMA((4,))],
        name="last_rows",
        compiler_params=pltpu.CompilerParams(vmem_limit_bytes=24 << 20),
    )(*(pltpu.with_memory_space_constraint(v, pltpu.VMEM) for v in held), act_mid, stat_in)
    return (
        block_out.reshape(inputs.shape),
        input_grad.reshape(inputs.shape),
        conv_grad,
        proj_grad,
    )


def solution(mesh):
    split = Mesh(mesh.devices.reshape(4, 2, 4, 2, 8), ("x", "z_hi", "z_lo", "core", "dp"))
    rows = P("dp", SEQ, None)
    return jax.shard_map(
        per_device,
        mesh=split,
        in_specs=(rows, rows, P(), P(), P(), P(), P(), P()),
        out_specs=(rows, rows, P(SEQ, None), P(SEQ, None)),
        check_vma=False,
    )
```

```python
import math

import jax
import jax.numpy as jnp
from jax import lax
from jax.experimental import pallas as pl
from jax.experimental.pallas import tpu as pltpu
from jax.sharding import Mesh
from jax.sharding import PartitionSpec as P

SEQ = ("x", "z_hi", "z_lo", "core")
PLANE = ("x", "z_hi", "z_lo")
LINE = ("core", "dp")
BF16, F32 = jnp.bfloat16, jnp.float32
CH, MID = 768, 256
ROWS, SHIFT = 128, 16
PLANES, LINES, BATCH = 32, 16, 8
HALF = 512
COUNTED = 8.0 * 8192.0
COEFF = math.sqrt(2.0 / math.pi)


def exchange(pieces, axes):
    return lax.all_to_all(pieces, axes, split_axis=0, concat_axis=0, tiled=True)


def kernel(body, *outs, name):
    shapes = tuple(jax.ShapeDtypeStruct(shape, dtype) for shape, dtype in outs)
    whole = pl.BlockSpec(memory_space=pltpu.VMEM)

    def call(*args, near=()):
        near = tuple(pltpu.with_memory_space_constraint(a, pltpu.VMEM) for a in near)
        args = (*near, *args)
        return pl.pallas_call(
            body,
            out_shape=shapes,
            in_specs=[whole] * len(args),
            out_specs=(whole,) * len(shapes),
            name=name,
            compiler_params=pltpu.CompilerParams(vmem_limit_bytes=24 << 20),
        )(*args)

    return call


def matmul(a, b, dims):
    return lax.dot_general(a, b, (dims, ((), ())), preferred_element_type=F32)


def later(x):
    return jnp.concatenate([jnp.zeros_like(x[:SHIFT]), x[:-SHIFT]], axis=0)


def earlier(x):
    return jnp.concatenate([x[SHIFT:], jnp.zeros_like(x[:SHIFT])], axis=0)


def woven(value):
    width = value.shape[1] // 2
    tiles = value.astype(F32).reshape(ROWS // 8, 8, 2 * width)
    a, b = tiles[:, :, :width], tiles[:, :, width:]
    upper = lax.broadcasted_iota(jnp.int32, a.shape, 1) < 4
    even = jnp.where(upper, a, pltpu.roll(b, 4, axis=1))
    odd = jnp.where(upper, pltpu.roll(a, 4, axis=1), b)
    return jnp.stack([even, odd], axis=1).reshape(PLANES, 8, width).astype(BF16)


def unwoven(pieces):
    width = pieces.shape[2]
    pairs = pieces.astype(F32).reshape(ROWS // 8, 2, 8, width)
    even, odd = pairs[:, 0], pairs[:, 1]
    upper = lax.broadcasted_iota(jnp.int32, even.shape, 1) < 4
    a = jnp.where(upper, even, pltpu.roll(odd, 4, axis=1))
    b = jnp.where(upper, pltpu.roll(even, 4, axis=1), odd)
    return jnp.concatenate([a.reshape(ROWS, width), b.reshape(ROWS, width)], axis=1)


def rounded(value):
    return value.astype(BF16).astype(F32)


def tile_of(pieces, width):
    row = lax.broadcasted_iota(jnp.int32, (8, width), 0)
    tile = jnp.zeros((8, width), F32)
    for k, piece in enumerate(pieces):
        tile = jnp.where(row == k, piece, tile)
    return tile


def in_two(value, width):
    high = rounded(value)
    return [
        part[:, k : k + width] for part in (high, value - high) for k in range(0, value.shape[1], width)
    ]


def row_of(tile, rows):
    return jnp.concatenate([tile[k : k + 1] for k in rows], axis=1)


def sum_rows(value):
    return jnp.sum(value, axis=0, keepdims=True)


def flat(ref):
    return ref[...].reshape(1, ref.shape[0])


def copies(ref, index, row):
    ref[:, :, index] = jnp.broadcast_to(row, (ref.shape[0], 1, row.shape[1]))


def tanh_of(value):
    return jnp.tanh(COEFF * (value + 0.044715 * value * value * value))


def gelu_of(value, inner):
    return 0.5 * value * (1.0 + inner)


def slope_of(value, inner):
    return 0.5 * (1.0 + inner) + 0.5 * value * (1.0 - inner * inner) * COEFF * (
        1.0 + 3.0 * 0.044715 * value * value
    )


def opening(x_hbm, cot_hbm, proj_hbm, sums_ref, data_ref, dact_ref, x_ref, cot_ref, proj_ref, sems):
    pairs = ((x_hbm, x_ref), (cot_hbm, cot_ref), (proj_hbm, proj_ref))
    loads = [pltpu.make_async_copy(*pair, sems.at[k]) for k, pair in enumerate(pairs)]
    for load in loads:
        load.start()
    loads[0].wait()
    x = x_ref[...].astype(F32)
    mean = sum_rows(x) * (1.0 / ROWS)
    apart = x - mean
    copies(sums_ref, slice(0, CH), mean)
    copies(sums_ref, slice(CH, 2 * CH), sum_rows(apart * apart))
    data_ref[...] = woven(x)
    loads[1].wait()
    loads[2].wait()
    dact_ref[...] = woven(matmul(cot_ref[...], proj_ref[...], ((1,), (1,))))


def spread_all(sums_ref, data_ref, out_ref):
    sums = sums_ref[...]
    means = sums[:, :, :CH]
    mean = jnp.sum(means, axis=0) * (1.0 / LINES)
    apart = means - mean[None]
    squares = jnp.sum(sums[:, :, CH:] + float(ROWS) * (apart * apart), axis=0)
    tile = tile_of(in_two(mean, CH // 2) + in_two(squares, CH // 2), CH // 2).astype(BF16)
    out_ref[:, :, : CH // 2] = data_ref[...]
    out_ref[:, :, CH // 2 :] = jnp.broadcast_to(tile[None], (PLANES, 8, CH // 2))


def over_pieces(parts, count):
    parts = parts.astype(F32)
    parts = parts + pltpu.roll(parts, 6, axis=1)
    total = jnp.sum(parts, axis=0)
    mean = total * (1.0 / PLANES)
    apart = parts - mean[None]
    between = jnp.sum(apart * apart, axis=0) * float(count)
    return row_of(mean, (0, 1)), row_of(total, (4, 5)) + row_of(between, (0, 1))


def forward_conv(got_ref, weight_ref, gain_ref, bias_ref, dact_ref, act_ref, x_ref, conv_ref, out_ref, stat_ref):
    center, squares = over_pieces(got_ref[:, :, CH // 2 :], ROWS * LINES)
    spread = jnp.sqrt(squares * (1.0 / COUNTED) + 1e-05)
    stat_ref[0:1, :] = center
    stat_ref[1:2, :] = spread
    x = unwoven(got_ref[:, :, : CH // 2])
    x_ref[...] = x.astype(BF16)
    pre = flat(gain_ref) * ((x - center) / spread) + flat(bias_ref)
    act = gelu_of(pre, tanh_of(pre)).astype(BF16)
    act_ref[...] = act
    terms = matmul(act, weight_ref[...], ((1,), (0,)))
    conv = later(terms[:, :MID]) + terms[:, MID : 2 * MID] + earlier(terms[:, 2 * MID :])
    conv_ref[...] = conv
    mean = sum_rows(conv) * (1.0 / ROWS)
    apart = conv - mean
    tile = tile_of(in_two(mean, 128) + in_two(sum_rows(apart * apart), 128), 128).astype(BF16)
    out_ref[:, :, :128] = dact_ref[...]
    out_ref[:, :, 128:] = jnp.broadcast_to(tile[None], (PLANES, 8, 128))


def middle_line(got_ref, out_ref):
    mean, squares = over_pieces(got_ref[:, :, 128:], ROWS)
    copies(out_ref, slice(0, MID), mean)
    copies(out_ref, slice(MID, 2 * MID), squares)


def middle(got_ref, plane_ref, gain_ref, bias_ref, conv_ref, act_ref, normed_ref, dpre_ref, sums_ref, spread_ref):
    means = got_ref[:, :, :MID]
    center = jnp.sum(means, axis=0) * (1.0 / LINES)
    apart = means - center[None]
    squares = jnp.sum(got_ref[:, :, MID:] + float(ROWS * PLANES) * (apart * apart), axis=0)
    spread = jnp.sqrt(squares * (1.0 / COUNTED) + 1e-05)
    spread_ref[0:1, :] = spread
    normed = (conv_ref[...] - center) / spread
    pre = flat(gain_ref) * normed + flat(bias_ref)
    inner = tanh_of(pre)
    dpre = unwoven(plane_ref[:, :, :128]) * slope_of(pre, inner)
    copies(sums_ref, slice(0, MID), sum_rows(dpre))
    copies(sums_ref, slice(MID, 2 * MID), sum_rows(dpre * normed))
    normed_ref[...] = normed
    dpre_ref[...] = dpre
    act_ref[...] = woven(gelu_of(pre, inner))


def middle_plane(sums_ref, act_ref, out_ref):
    tile = tile_of(in_two(jnp.sum(sums_ref[...], axis=0), 128), 128).astype(BF16)
    out_ref[:, :, :128] = act_ref[...]
    out_ref[:, :, 128:] = jnp.broadcast_to(tile[None], (PLANES, 8, 128))


def in_four(value):
    blank = jnp.zeros((1, HALF - CH // 2), F32)
    return tile_of([jnp.concatenate([row, blank], axis=1) for row in in_two(value, CH // 2)], HALF)


def from_four(tile):
    return jnp.concatenate([tile[k : k + 1, : CH // 2] + tile[k + 2 : k + 3, : CH // 2] for k in range(2)], axis=1)


def filter_parts(
    got_ref,
    gain_ref,
    cot_ref,
    weight_ref,
    gain_in_ref,
    bias_in_ref,
    dpre_ref,
    normed_ref,
    spread_ref,
    act_in_ref,
    x_ref,
    stat_ref,
    kept_ref,
    sent_ref,
    act_ref,
    back_ref,
):
    tile = jnp.sum(got_ref[:, :, 128:].astype(F32), axis=0) * (1.0 / COUNTED)
    tile = tile + pltpu.roll(tile, 4, axis=0)
    first, second = row_of(tile, (0, 1)), row_of(tile, (2, 3))
    dconv = dpre_ref[...] - first - normed_ref[...] * second
    dconv = flat(gain_ref) * dconv / spread_ref[0:1, :]
    stacked = jnp.concatenate([earlier(dconv), dconv, later(dconv)], axis=1).astype(BF16)
    conv_part = matmul(act_in_ref[...], stacked, ((0,), (0,)))
    act = unwoven(got_ref[:, :, :128]).astype(BF16)
    act_ref[...] = act
    proj_part = matmul(cot_ref[...], act, ((0,), (0,)))
    normed = (x_ref[...].astype(F32) - stat_ref[0:1, :]) / stat_ref[1:2, :]
    pre = flat(gain_in_ref) * normed + flat(bias_in_ref)
    dpre = matmul(stacked, weight_ref[...], ((1,), (1,))) * slope_of(pre, tanh_of(pre))
    sums = in_four(sum_rows(dpre)).astype(BF16), in_four(sum_rows(dpre * normed)).astype(BF16)

    def place(left_ref, right_ref):
        left_ref[:CH, :] = conv_part[:, :HALF].astype(BF16)
        right_ref[:CH, : HALF - MID] = conv_part[:, HALF:].astype(BF16)
        right_ref[:CH, HALF - MID :] = proj_part.astype(BF16)
        left_ref[CH:, :] = sums[0]
        right_ref[CH:, :] = sums[1]

    core = lax.axis_index("core")
    pl.when(core == 0)(lambda: place(kept_ref, sent_ref))
    pl.when(core == 1)(lambda: place(sent_ref, kept_ref))
    back_ref[...] = woven(dpre)


def to_plane(got_ref, kept_ref, back_ref, out_ref):
    both = kept_ref[...].astype(F32) + got_ref[...].astype(F32)
    pieces = both[:CH].astype(BF16).reshape(PLANES, 3, 8, HALF)
    for k in range(3):
        out_ref[:, :, HALF * k : HALF * (k + 1)] = pieces[:, k]
    begin = 3 * HALF + CH // 2
    out_ref[:, :, 3 * HALF : begin] = back_ref[...]
    sums = from_four(both[CH:])
    tile = tile_of([sums[:, k : k + 128] for k in range(0, CH, 128)], 128).astype(BF16)
    out_ref[:, :, begin:] = jnp.broadcast_to(tile[None], (PLANES, 8, 128))


def to_line(got_ref, out_ref):
    tiles = [
        jnp.sum(got_ref[:, :, HALF * k : HALF * (k + 1)].astype(F32), axis=0) for k in range(3)
    ]
    sums = jnp.sum(got_ref[:, :, 3 * HALF + CH // 2 :].astype(F32), axis=0)
    low = pltpu.roll(in_four(row_of(sums, range(6))), 4, axis=0)
    upper = lax.broadcasted_iota(jnp.int32, (8, HALF), 0) < 4
    turned = [pltpu.roll(tile, 4, axis=0) for tile in tiles]
    own = (
        (tiles[0], jnp.where(upper, tiles[1], low)),
        (jnp.where(upper, turned[1], turned[2]), jnp.where(upper, turned[2], low)),
    )
    for core in range(2):
        for k in range(2):
            out_ref[core * BATCH : (core + 1) * BATCH, :, HALF * k : HALF * (k + 1)] = (
                jnp.broadcast_to(own[core][k].astype(BF16)[None], (BATCH, 8, HALF))
            )


def last_rows(
    got_ref, plane_ref, x_ref, cot_ref, proj_ref, gain_ref, act_ref, stat_ref, out_ref, grad_ref, conv_ref, proj_grad_ref
):
    x = x_ref[...].astype(F32)
    update = matmul(act_ref[...], proj_ref[...], ((1,), (0,)))
    out_ref[...] = (x + update).astype(BF16)
    left, right = (
        jnp.sum(got_ref[BATCH * k : BATCH * (k + 1)].astype(F32), axis=0) for k in range(2)
    )
    first, second = (from_four(half[4:8, HALF:]) * (1.0 / COUNTED) for half in (left, right))
    spread = stat_ref[1:2, :]
    normed = (x - stat_ref[0:1, :]) / spread
    dpre = unwoven(plane_ref[:, :, 3 * HALF : 3 * HALF + CH // 2])
    change = flat(gain_ref) * (dpre - first - normed * second) / spread
    grad_ref[...] = (cot_ref[...].astype(F32) + change).astype(BF16)
    for rows, lanes, count in ((slice(0, 8), 0, 8), (slice(8, 12), HALF, 4)):
        conv_ref[rows, :HALF] = left[:count, lanes : lanes + HALF]
        conv_ref[rows, HALF:] = right[:count, lanes : lanes + CH - HALF]
        proj_grad_ref[rows, :] = right[:count, lanes + CH - HALF : lanes + HALF]


def per_device(inputs, cotangent, conv_weight, proj_weight, gain_in, bias_in, gain_mid, bias_mid):
    x = inputs.reshape(ROWS, CH)
    cot = cotangent.reshape(ROWS, CH)
    rows, rows_mid = (ROWS, CH), (ROWS, MID)

    far, near = pl.BlockSpec(memory_space=pltpu.HBM), pl.BlockSpec(memory_space=pltpu.VMEM)
    sums, data, dact = pl.pallas_call(
        opening,
        out_shape=(
            jax.ShapeDtypeStruct((LINES, 1, 2 * CH), F32),
            jax.ShapeDtypeStruct((PLANES, 8, CH // 2), BF16),
            jax.ShapeDtypeStruct((PLANES, 8, 128), BF16),
        ),
        in_specs=[far] * 3,
        out_specs=(near,) * 3,
        scratch_shapes=[
            pltpu.VMEM(rows, BF16),
            pltpu.VMEM(rows, BF16),
            pltpu.VMEM((MID, CH), BF16),
            pltpu.SemaphoreType.DMA((3,)),
        ],
        name="opening",
        compiler_params=pltpu.CompilerParams(vmem_limit_bytes=24 << 20),
    )(*(pltpu.with_memory_space_constraint(v, pltpu.HBM) for v in (x, cot, proj_weight)))
    sums = exchange(sums, LINE)
    (both,) = kernel(spread_all, ((PLANES, 8, CH), BF16), name="spread_all")(
        data, near=(sums,)
    )
    both = exchange(both, PLANE)

    act_in, far_x, conv, both, stat_in = kernel(
        forward_conv,
        (rows, BF16),
        (rows, BF16),
        (rows_mid, F32),
        ((PLANES, 8, 256), BF16),
        ((8, CH), F32),
        name="forward_conv",
    )(dact, near=(both, conv_weight, gain_in, bias_in))
    both = exchange(both, PLANE)
    (sums,) = kernel(middle_line, ((LINES, 1, 2 * MID), F32), name="middle_line")(near=(both,))
    sums = exchange(sums, LINE)

    act_mid, normed_mid, dpre_mid, sums, spread_mid = kernel(
        middle,
        ((PLANES, 8, 128), BF16),
        (rows_mid, F32),
        (rows_mid, F32),
        ((LINES, 1, 2 * MID), F32),
        ((8, MID), F32),
        name="middle",
    )(conv, near=(sums, both, gain_mid, bias_mid))
    sums = exchange(sums, LINE)
    (both,) = kernel(middle_plane, ((PLANES, 8, 256), BF16), name="middle_plane")(
        act_mid, near=(sums,)
    )
    both = exchange(both, PLANE)

    kept, sent, act_mid, back = kernel(
        filter_parts,
        ((CH + 8, HALF), BF16),
        ((CH + 8, HALF), BF16),
        (rows_mid, BF16),
        ((PLANES, 8, CH // 2), BF16),
        name="filter_parts",
    )(
        dpre_mid,
        normed_mid,
        spread_mid,
        act_in,
        far_x,
        stat_in,
        near=(both, gain_mid, cot, conv_weight, gain_in, bias_in),
    )
    got = lax.ppermute(sent, "core", [(0, 1), (1, 0)])
    (plane,) = kernel(to_plane, ((PLANES, 8, 3 * HALF + CH // 2 + 128), BF16), name="to_plane")(
        kept, back, near=(got,)
    )
    plane = exchange(plane, PLANE)
    (line,) = kernel(to_line, ((LINES, 8, 2 * HALF), BF16), name="to_line")(near=(plane,))
    line = exchange(line, LINE)
    block_out, input_grad, conv_grad, proj_grad = kernel(
        last_rows, (rows, BF16), (rows, BF16), ((12, CH), F32), ((12, MID), F32), name="last_rows"
    )(act_mid, stat_in, near=(line, plane, x, cot, proj_weight, gain_in))
    return (
        block_out.reshape(inputs.shape),
        input_grad.reshape(inputs.shape),
        conv_grad,
        proj_grad,
    )


def solution(mesh):
    split = Mesh(mesh.devices.reshape(4, 2, 4, 2, 8), ("x", "z_hi", "z_lo", "core", "dp"))
    rows = P("dp", SEQ, None)
    return jax.shard_map(
        per_device,
        mesh=split,
        in_specs=(rows, rows, P(), P(), P(), P(), P(), P()),
        out_specs=(rows, rows, P(SEQ, None), P(SEQ, None)),
        check_vma=False,
    )
```

```python
import math

import jax
import jax.numpy as jnp
from jax import lax
from jax.experimental import pallas as pl
from jax.experimental.pallas import tpu as pltpu
from jax.sharding import Mesh
from jax.sharding import PartitionSpec as P

SEQ = ("x", "z_hi", "z_lo", "core")
PLANE = ("x", "z_hi", "z_lo")
LINE = ("core", "dp")
BF16, F32 = jnp.bfloat16, jnp.float32
CH, MID = 768, 256
ROWS, SHIFT = 128, 16
PLANES, LINES, BATCH = 32, 16, 8
HALF = 512
COUNTED = 8.0 * 8192.0
COEFF = math.sqrt(2.0 / math.pi)


def exchange(pieces, axes):
    return lax.all_to_all(pieces, axes, split_axis=0, concat_axis=0, tiled=True)


def kernel(body, *outs, name):
    shapes = tuple(jax.ShapeDtypeStruct(shape, dtype) for shape, dtype in outs)
    whole = pl.BlockSpec(memory_space=pltpu.VMEM)

    def call(*args, near=()):
        near = tuple(pltpu.with_memory_space_constraint(a, pltpu.VMEM) for a in near)
        args = (*near, *args)
        return pl.pallas_call(
            body,
            out_shape=shapes,
            in_specs=[whole] * len(args),
            out_specs=(whole,) * len(shapes),
            name=name,
            compiler_params=pltpu.CompilerParams(vmem_limit_bytes=24 << 20),
        )(*args)

    return call


def matmul(a, b, dims):
    return lax.dot_general(a, b, (dims, ((), ())), preferred_element_type=F32)


def later(x):
    return jnp.concatenate([jnp.zeros_like(x[:SHIFT]), x[:-SHIFT]], axis=0)


def earlier(x):
    return jnp.concatenate([x[SHIFT:], jnp.zeros_like(x[:SHIFT])], axis=0)


def woven(value):
    width = value.shape[1] // 2
    tiles = value.astype(F32).reshape(ROWS // 8, 8, 2 * width)
    a, b = tiles[:, :, :width], tiles[:, :, width:]
    upper = lax.broadcasted_iota(jnp.int32, a.shape, 1) < 4
    even = jnp.where(upper, a, pltpu.roll(b, 4, axis=1))
    odd = jnp.where(upper, pltpu.roll(a, 4, axis=1), b)
    return jnp.stack([even, odd], axis=1).reshape(PLANES, 8, width).astype(BF16)


def unwoven(pieces):
    width = pieces.shape[2]
    pairs = pieces.astype(F32).reshape(ROWS // 8, 2, 8, width)
    even, odd = pairs[:, 0], pairs[:, 1]
    upper = lax.broadcasted_iota(jnp.int32, even.shape, 1) < 4
    a = jnp.where(upper, even, pltpu.roll(odd, 4, axis=1))
    b = jnp.where(upper, pltpu.roll(even, 4, axis=1), odd)
    return jnp.concatenate([a.reshape(ROWS, width), b.reshape(ROWS, width)], axis=1)


def rounded(value):
    return value.astype(BF16).astype(F32)


def tile_of(pieces, width):
    row = lax.broadcasted_iota(jnp.int32, (8, width), 0)
    tile = jnp.zeros((8, width), F32)
    for k, piece in enumerate(pieces):
        tile = jnp.where(row == k, piece, tile)
    return tile


def in_two(value, width):
    high = rounded(value)
    return [
        part[:, k : k + width] for part in (high, value - high) for k in range(0, value.shape[1], width)
    ]


def row_of(tile, rows):
    return jnp.concatenate([tile[k : k + 1] for k in rows], axis=1)


def sum_rows(value):
    return jnp.sum(value, axis=0, keepdims=True)


def flat(ref):
    return ref[...].reshape(1, ref.shape[0])


def copies(ref, index, row):
    ref[:, :, index] = jnp.broadcast_to(row, (ref.shape[0], 1, row.shape[1]))


def tanh_of(value):
    return jnp.tanh(COEFF * (value + 0.044715 * value * value * value))


def gelu_of(value, inner):
    return 0.5 * value * (1.0 + inner)


def slope_of(value, inner):
    return 0.5 * (1.0 + inner) + 0.5 * value * (1.0 - inner * inner) * COEFF * (
        1.0 + 3.0 * 0.044715 * value * value
    )


def opening(x_hbm, sums_ref, data_ref, x_ref, sem):
    load = pltpu.make_async_copy(x_hbm, x_ref, sem)
    load.start()
    load.wait()
    x = x_ref[...].astype(F32)
    mean = sum_rows(x) * (1.0 / ROWS)
    apart = x - mean
    copies(sums_ref, slice(0, CH), mean)
    copies(sums_ref, slice(CH, 2 * CH), sum_rows(apart * apart))
    data_ref[...] = woven(x)


def spread_all(sums_ref, data_ref, out_ref):
    sums = sums_ref[...]
    means = sums[:, :, :CH]
    mean = jnp.sum(means, axis=0) * (1.0 / LINES)
    apart = means - mean[None]
    squares = jnp.sum(sums[:, :, CH:] + float(ROWS) * (apart * apart), axis=0)
    tile = tile_of(in_two(mean, CH // 2) + in_two(squares, CH // 2), CH // 2).astype(BF16)
    out_ref[:, :, : CH // 2] = data_ref[...]
    out_ref[:, :, CH // 2 :] = jnp.broadcast_to(tile[None], (PLANES, 8, CH // 2))


def over_pieces(parts, count):
    parts = parts.astype(F32)
    parts = parts + pltpu.roll(parts, 6, axis=1)
    total = jnp.sum(parts, axis=0)
    mean = total * (1.0 / PLANES)
    apart = parts - mean[None]
    between = jnp.sum(apart * apart, axis=0) * float(count)
    return row_of(mean, (0, 1)), row_of(total, (4, 5)) + row_of(between, (0, 1))


def forward_conv(got_ref, weight_ref, gain_ref, bias_ref, cot_ref, proj_ref, act_ref, x_ref, conv_ref, out_ref, stat_ref):
    center, squares = over_pieces(got_ref[:, :, CH // 2 :], ROWS * LINES)
    spread = jnp.sqrt(squares * (1.0 / COUNTED) + 1e-05)
    stat_ref[0:1, :] = center
    stat_ref[1:2, :] = spread
    x = unwoven(got_ref[:, :, : CH // 2])
    x_ref[...] = x.astype(BF16)
    pre = flat(gain_ref) * ((x - center) / spread) + flat(bias_ref)
    act = gelu_of(pre, tanh_of(pre)).astype(BF16)
    act_ref[...] = act
    terms = matmul(act, weight_ref[...], ((1,), (0,)))
    conv = later(terms[:, :MID]) + terms[:, MID : 2 * MID] + earlier(terms[:, 2 * MID :])
    conv_ref[...] = conv
    mean = sum_rows(conv) * (1.0 / ROWS)
    apart = conv - mean
    tile = tile_of(in_two(mean, 128) + in_two(sum_rows(apart * apart), 128), 128).astype(BF16)
    out_ref[:, :, :128] = woven(matmul(cot_ref[...], proj_ref[...], ((1,), (1,))))
    out_ref[:, :, 128:] = jnp.broadcast_to(tile[None], (PLANES, 8, 128))


def middle_line(got_ref, out_ref):
    mean, squares = over_pieces(got_ref[:, :, 128:], ROWS)
    copies(out_ref, slice(0, MID), mean)
    copies(out_ref, slice(MID, 2 * MID), squares)


def middle(got_ref, plane_ref, gain_ref, bias_ref, conv_ref, act_ref, normed_ref, dpre_ref, sums_ref, spread_ref):
    means = got_ref[:, :, :MID]
    center = jnp.sum(means, axis=0) * (1.0 / LINES)
    apart = means - center[None]
    squares = jnp.sum(got_ref[:, :, MID:] + float(ROWS * PLANES) * (apart * apart), axis=0)
    spread = jnp.sqrt(squares * (1.0 / COUNTED) + 1e-05)
    spread_ref[0:1, :] = spread
    normed = (conv_ref[...] - center) / spread
    pre = flat(gain_ref) * normed + flat(bias_ref)
    inner = tanh_of(pre)
    dpre = unwoven(plane_ref[:, :, :128]) * slope_of(pre, inner)
    copies(sums_ref, slice(0, MID), sum_rows(dpre))
    copies(sums_ref, slice(MID, 2 * MID), sum_rows(dpre * normed))
    normed_ref[...] = normed
    dpre_ref[...] = dpre
    act_ref[...] = woven(gelu_of(pre, inner))


def middle_plane(sums_ref, act_ref, out_ref):
    tile = tile_of(in_two(jnp.sum(sums_ref[...], axis=0), 128), 128).astype(BF16)
    out_ref[:, :, :128] = act_ref[...]
    out_ref[:, :, 128:] = jnp.broadcast_to(tile[None], (PLANES, 8, 128))


def in_four(value):
    blank = jnp.zeros((1, HALF - CH // 2), F32)
    return tile_of([jnp.concatenate([row, blank], axis=1) for row in in_two(value, CH // 2)], HALF)


def from_four(tile):
    return jnp.concatenate([tile[k : k + 1, : CH // 2] + tile[k + 2 : k + 3, : CH // 2] for k in range(2)], axis=1)


def filter_sent(
    got_ref,
    gain_ref,
    cot_ref,
    weight_ref,
    gain_in_ref,
    bias_in_ref,
    dpre_ref,
    normed_ref,
    spread_ref,
    act_in_ref,
    x_ref,
    stat_ref,
    sent_ref,
    stacked_ref,
    act_ref,
    dpre_out_ref,
    sums_ref,
):
    tile = jnp.sum(got_ref[:, :, 128:].astype(F32), axis=0) * (1.0 / COUNTED)
    tile = tile + pltpu.roll(tile, 4, axis=0)
    first, second = row_of(tile, (0, 1)), row_of(tile, (2, 3))
    dconv = dpre_ref[...] - first - normed_ref[...] * second
    dconv = flat(gain_ref) * dconv / spread_ref[0:1, :]
    stacked = jnp.concatenate([earlier(dconv), dconv, later(dconv)], axis=1).astype(BF16)
    stacked_ref[...] = stacked
    act_ref[...] = unwoven(got_ref[:, :, :128]).astype(BF16)
    normed = (x_ref[...].astype(F32) - stat_ref[0:1, :]) / stat_ref[1:2, :]
    pre = flat(gain_in_ref) * normed + flat(bias_in_ref)
    dpre = matmul(stacked, weight_ref[...], ((1,), (1,))) * slope_of(pre, tanh_of(pre))
    dpre_out_ref[...] = dpre
    both = in_four(sum_rows(dpre)).astype(BF16), in_four(sum_rows(dpre * normed)).astype(BF16)
    core = lax.axis_index("core")

    @pl.when(core == 0)
    def _():
        right_half(sent_ref, act_in_ref, stacked_ref, cot_ref, act_ref)
        sent_ref[CH:, :] = both[1]
        sums_ref[...] = both[0]

    @pl.when(core == 1)
    def _():
        left_half(sent_ref, act_in_ref, stacked_ref)
        sent_ref[CH:, :] = both[0]
        sums_ref[...] = both[1]


def left_half(out_ref, act_in_ref, stacked_ref):
    part = matmul(act_in_ref[...], stacked_ref[:, :HALF], ((0,), (0,)))
    out_ref[:CH, :] = part.astype(BF16)


def right_half(out_ref, act_in_ref, stacked_ref, cot_ref, act_ref):
    part = matmul(act_in_ref[...], stacked_ref[:, HALF:], ((0,), (0,)))
    out_ref[:CH, : HALF - MID] = part.astype(BF16)
    part = matmul(cot_ref[...], act_ref[...], ((0,), (0,)))
    out_ref[:CH, HALF - MID :] = part.astype(BF16)


def filter_kept(cot_ref, act_in_ref, stacked_ref, act_ref, dpre_ref, sums_ref, kept_ref, back_ref):
    core = lax.axis_index("core")
    kept_ref[CH:, :] = sums_ref[...]
    back_ref[...] = woven(dpre_ref[...])

    @pl.when(core == 0)
    def _():
        left_half(kept_ref, act_in_ref, stacked_ref)

    @pl.when(core == 1)
    def _():
        right_half(kept_ref, act_in_ref, stacked_ref, cot_ref, act_ref)


def to_plane(got_ref, kept_ref, back_ref, out_ref):
    both = kept_ref[...].astype(F32) + got_ref[...].astype(F32)
    pieces = both[:CH].astype(BF16).reshape(PLANES, 3, 8, HALF)
    for k in range(3):
        out_ref[:, :, HALF * k : HALF * (k + 1)] = pieces[:, k]
    begin = 3 * HALF + CH // 2
    out_ref[:, :, 3 * HALF : begin] = back_ref[...]
    sums = from_four(both[CH:])
    tile = tile_of([sums[:, k : k + 128] for k in range(0, CH, 128)], 128).astype(BF16)
    out_ref[:, :, begin:] = jnp.broadcast_to(tile[None], (PLANES, 8, 128))


def to_line(got_ref, out_ref):
    tiles = [
        jnp.sum(got_ref[:, :, HALF * k : HALF * (k + 1)].astype(F32), axis=0) for k in range(3)
    ]
    sums = jnp.sum(got_ref[:, :, 3 * HALF + CH // 2 :].astype(F32), axis=0)
    low = pltpu.roll(in_four(row_of(sums, range(6))), 4, axis=0)
    upper = lax.broadcasted_iota(jnp.int32, (8, HALF), 0) < 4
    turned = [pltpu.roll(tile, 4, axis=0) for tile in tiles]
    own = (
        (tiles[0], jnp.where(upper, tiles[1], low)),
        (jnp.where(upper, turned[1], turned[2]), jnp.where(upper, turned[2], low)),
    )
    for core in range(2):
        for k in range(2):
            out_ref[core * BATCH : (core + 1) * BATCH, :, HALF * k : HALF * (k + 1)] = (
                jnp.broadcast_to(own[core][k].astype(BF16)[None], (BATCH, 8, HALF))
            )


def last_rows(
    got_ref, plane_ref, x_ref, cot_ref, proj_ref, gain_ref, act_ref, stat_ref, out_ref, grad_ref, conv_ref, proj_grad_ref
):
    x = x_ref[...].astype(F32)
    update = matmul(act_ref[...], proj_ref[...], ((1,), (0,)))
    out_ref[...] = (x + update).astype(BF16)
    left, right = (
        jnp.sum(got_ref[BATCH * k : BATCH * (k + 1)].astype(F32), axis=0) for k in range(2)
    )
    first, second = (from_four(half[4:8, HALF:]) * (1.0 / COUNTED) for half in (left, right))
    spread = stat_ref[1:2, :]
    normed = (x - stat_ref[0:1, :]) / spread
    dpre = unwoven(plane_ref[:, :, 3 * HALF : 3 * HALF + CH // 2])
    change = flat(gain_ref) * (dpre - first - normed * second) / spread
    grad_ref[...] = (cot_ref[...].astype(F32) + change).astype(BF16)
    for rows, lanes, count in ((slice(0, 8), 0, 8), (slice(8, 12), HALF, 4)):
        conv_ref[rows, :HALF] = left[:count, lanes : lanes + HALF]
        conv_ref[rows, HALF:] = right[:count, lanes : lanes + CH - HALF]
        proj_grad_ref[rows, :] = right[:count, lanes + CH - HALF : lanes + HALF]


def per_device(inputs, cotangent, conv_weight, proj_weight, gain_in, bias_in, gain_mid, bias_mid):
    x = inputs.reshape(ROWS, CH)
    cot = cotangent.reshape(ROWS, CH)
    rows, rows_mid = (ROWS, CH), (ROWS, MID)

    far, near = pl.BlockSpec(memory_space=pltpu.HBM), pl.BlockSpec(memory_space=pltpu.VMEM)
    sums, data = pl.pallas_call(
        opening,
        out_shape=(
            jax.ShapeDtypeStruct((LINES, 1, 2 * CH), F32),
            jax.ShapeDtypeStruct((PLANES, 8, CH // 2), BF16),
        ),
        in_specs=[far],
        out_specs=(near, near),
        scratch_shapes=[pltpu.VMEM(rows, BF16), pltpu.SemaphoreType.DMA],
        name="opening",
        compiler_params=pltpu.CompilerParams(vmem_limit_bytes=24 << 20),
    )(pltpu.with_memory_space_constraint(x, pltpu.HBM))
    sums = exchange(sums, LINE)
    (both,) = kernel(spread_all, ((PLANES, 8, CH), BF16), name="spread_all")(
        data, near=(sums,)
    )
    both = exchange(both, PLANE)

    act_in, far_x, conv, both, stat_in = kernel(
        forward_conv,
        (rows, BF16),
        (rows, BF16),
        (rows_mid, F32),
        ((PLANES, 8, 256), BF16),
        ((8, CH), F32),
        name="forward_conv",
    )(near=(both, conv_weight, gain_in, bias_in, cot, proj_weight))
    both = exchange(both, PLANE)
    (sums,) = kernel(middle_line, ((LINES, 1, 2 * MID), F32), name="middle_line")(near=(both,))
    sums = exchange(sums, LINE)

    act_mid, normed_mid, dpre_mid, sums, spread_mid = kernel(
        middle,
        ((PLANES, 8, 128), BF16),
        (rows_mid, F32),
        (rows_mid, F32),
        ((LINES, 1, 2 * MID), F32),
        ((8, MID), F32),
        name="middle",
    )(conv, near=(sums, both, gain_mid, bias_mid))
    sums = exchange(sums, LINE)
    (both,) = kernel(middle_plane, ((PLANES, 8, 256), BF16), name="middle_plane")(
        act_mid, near=(sums,)
    )
    both = exchange(both, PLANE)

    sent, stacked, act_mid, dpre_in, sums = kernel(
        filter_sent,
        ((CH + 8, HALF), BF16),
        (rows, BF16),
        (rows_mid, BF16),
        (rows, F32),
        ((8, HALF), BF16),
        name="filter_sent",
    )(
        dpre_mid,
        normed_mid,
        spread_mid,
        act_in,
        far_x,
        stat_in,
        near=(both, gain_mid, cot, conv_weight, gain_in, bias_in),
    )
    got = lax.ppermute(sent, "core", [(0, 1), (1, 0)])
    kept, back = kernel(
        filter_kept, ((CH + 8, HALF), BF16), ((PLANES, 8, CH // 2), BF16), name="filter_kept"
    )(act_in, stacked, act_mid, dpre_in, sums, near=(cot,))
    (plane,) = kernel(to_plane, ((PLANES, 8, 3 * HALF + CH // 2 + 128), BF16), name="to_plane")(
        kept, back, near=(got,)
    )
    plane = exchange(plane, PLANE)
    (line,) = kernel(to_line, ((LINES, 8, 2 * HALF), BF16), name="to_line")(near=(plane,))
    line = exchange(line, LINE)
    block_out, input_grad, conv_grad, proj_grad = kernel(
        last_rows, (rows, BF16), (rows, BF16), ((12, CH), F32), ((12, MID), F32), name="last_rows"
    )(act_mid, stat_in, near=(line, plane, x, cot, proj_weight, gain_in))
    return (
        block_out.reshape(inputs.shape),
        input_grad.reshape(inputs.shape),
        conv_grad,
        proj_grad,
    )


def solution(mesh):
    split = Mesh(mesh.devices.reshape(4, 2, 4, 2, 8), ("x", "z_hi", "z_lo", "core", "dp"))
    rows = P("dp", SEQ, None)
    return jax.shard_map(
        per_device,
        mesh=split,
        in_specs=(rows, rows, P(), P(), P(), P(), P(), P()),
        out_specs=(rows, rows, P(SEQ, None), P(SEQ, None)),
        check_vma=False,
    )
```

```python
import math

import jax
import jax.numpy as jnp
from jax import lax
from jax.experimental import pallas as pl
from jax.experimental.pallas import tpu as pltpu
from jax.sharding import Mesh
from jax.sharding import PartitionSpec as P

SEQ = ("x", "z_hi", "z_lo", "core")
PLANE = ("x", "z_hi", "z_lo")
LINE = ("core", "dp")
BF16, F32 = jnp.bfloat16, jnp.float32
CH, MID = 768, 256
ROWS, SHIFT = 128, 16
PLANES, LINES, BATCH = 32, 16, 8
HALF = 512
COUNTED = 8.0 * 8192.0
COEFF = math.sqrt(2.0 / math.pi)


def exchange(pieces, axes):
    return lax.all_to_all(pieces, axes, split_axis=0, concat_axis=0, tiled=True)


def kernel(body, *outs, name):
    shapes = tuple(jax.ShapeDtypeStruct(shape, dtype) for shape, dtype in outs)
    whole = pl.BlockSpec(memory_space=pltpu.VMEM)

    def call(*args, near=()):
        near = tuple(pltpu.with_memory_space_constraint(a, pltpu.VMEM) for a in near)
        args = (*near, *args)
        return pl.pallas_call(
            body,
            out_shape=shapes,
            in_specs=[whole] * len(args),
            out_specs=(whole,) * len(shapes),
            name=name,
            compiler_params=pltpu.CompilerParams(vmem_limit_bytes=24 << 20),
        )(*args)

    return call


def matmul(a, b, dims):
    return lax.dot_general(a, b, (dims, ((), ())), preferred_element_type=F32)


def later(x):
    return jnp.concatenate([jnp.zeros_like(x[:SHIFT]), x[:-SHIFT]], axis=0)


def earlier(x):
    return jnp.concatenate([x[SHIFT:], jnp.zeros_like(x[:SHIFT])], axis=0)


def woven(value):
    width = value.shape[1] // 2
    tiles = value.astype(F32).reshape(ROWS // 8, 8, 2 * width)
    a, b = tiles[:, :, :width], tiles[:, :, width:]
    upper = lax.broadcasted_iota(jnp.int32, a.shape, 1) < 4
    even = jnp.where(upper, a, pltpu.roll(b, 4, axis=1))
    odd = jnp.where(upper, pltpu.roll(a, 4, axis=1), b)
    return jnp.stack([even, odd], axis=1).reshape(PLANES, 8, width).astype(BF16)


def unwoven(pieces):
    width = pieces.shape[2]
    pairs = pieces.astype(F32).reshape(ROWS // 8, 2, 8, width)
    even, odd = pairs[:, 0], pairs[:, 1]
    upper = lax.broadcasted_iota(jnp.int32, even.shape, 1) < 4
    a = jnp.where(upper, even, pltpu.roll(odd, 4, axis=1))
    b = jnp.where(upper, pltpu.roll(even, 4, axis=1), odd)
    return jnp.concatenate([a.reshape(ROWS, width), b.reshape(ROWS, width)], axis=1)


def rounded(value):
    return value.astype(BF16).astype(F32)


def tile_of(pieces, width):
    row = lax.broadcasted_iota(jnp.int32, (8, width), 0)
    tile = jnp.zeros((8, width), F32)
    for k, piece in enumerate(pieces):
        tile = jnp.where(row == k, piece, tile)
    return tile


def in_two(value, width):
    high = rounded(value)
    return [
        part[:, k : k + width] for part in (high, value - high) for k in range(0, value.shape[1], width)
    ]


def row_of(tile, rows):
    return jnp.concatenate([tile[k : k + 1] for k in rows], axis=1)


def sum_rows(value):
    return jnp.sum(value, axis=0, keepdims=True)


def flat(ref):
    return ref[...].reshape(1, ref.shape[0])


def copies(ref, index, row):
    ref[:, :, index] = jnp.broadcast_to(row, (ref.shape[0], 1, row.shape[1]))


def tanh_of(value):
    return jnp.tanh(COEFF * (value + 0.044715 * value * value * value))


def gelu_of(value, inner):
    return 0.5 * value * (1.0 + inner)


def slope_of(value, inner):
    return 0.5 * (1.0 + inner) + 0.5 * value * (1.0 - inner * inner) * COEFF * (
        1.0 + 3.0 * 0.044715 * value * value
    )


def opening(x_hbm, sums_ref, data_ref, x_ref, sem):
    load = pltpu.make_async_copy(x_hbm, x_ref, sem)
    load.start()
    load.wait()
    x = x_ref[...].astype(F32)
    mean = sum_rows(x) * (1.0 / ROWS)
    apart = x - mean
    copies(sums_ref, slice(0, CH), mean)
    copies(sums_ref, slice(CH, 2 * CH), sum_rows(apart * apart))
    data_ref[...] = woven(x)


def spread_all(sums_ref, data_ref, out_ref):
    sums = sums_ref[...]
    means = sums[:, :, :CH]
    mean = jnp.sum(means, axis=0) * (1.0 / LINES)
    apart = means - mean[None]
    squares = jnp.sum(sums[:, :, CH:] + float(ROWS) * (apart * apart), axis=0)
    tile = tile_of(in_two(mean, CH // 2) + in_two(squares, CH // 2), CH // 2).astype(BF16)
    out_ref[:, :, : CH // 2] = data_ref[...]
    out_ref[:, :, CH // 2 :] = jnp.broadcast_to(tile[None], (PLANES, 8, CH // 2))


def over_pieces(parts, count):
    parts = parts.astype(F32)
    parts = parts + pltpu.roll(parts, 6, axis=1)
    total = jnp.sum(parts, axis=0)
    mean = total * (1.0 / PLANES)
    apart = parts - mean[None]
    between = jnp.sum(apart * apart, axis=0) * float(count)
    return row_of(mean, (0, 1)), row_of(total, (4, 5)) + row_of(between, (0, 1))


def forward_conv(got_ref, weight_ref, gain_ref, bias_ref, cot_ref, proj_ref, act_ref, x_ref, conv_ref, out_ref, stat_ref):
    center, squares = over_pieces(got_ref[:, :, CH // 2 :], ROWS * LINES)
    spread = jnp.sqrt(squares * (1.0 / COUNTED) + 1e-05)
    stat_ref[0:1, :] = center
    stat_ref[1:2, :] = spread
    x = unwoven(got_ref[:, :, : CH // 2])
    x_ref[...] = x.astype(BF16)
    pre = flat(gain_ref) * ((x - center) / spread) + flat(bias_ref)
    act = gelu_of(pre, tanh_of(pre)).astype(BF16)
    act_ref[...] = act
    terms = matmul(act, weight_ref[...], ((1,), (0,)))
    conv = later(terms[:, :MID]) + terms[:, MID : 2 * MID] + earlier(terms[:, 2 * MID :])
    conv_ref[...] = conv
    mean = sum_rows(conv) * (1.0 / ROWS)
    apart = conv - mean
    tile = tile_of(in_two(mean, 128) + in_two(sum_rows(apart * apart), 128), 128).astype(BF16)
    out_ref[:, :, :128] = woven(matmul(cot_ref[...], proj_ref[...], ((1,), (1,))))
    out_ref[:, :, 128:] = jnp.broadcast_to(tile[None], (PLANES, 8, 128))


def middle_line(got_ref, out_ref):
    mean, squares = over_pieces(got_ref[:, :, 128:], ROWS)
    copies(out_ref, slice(0, MID), mean)
    copies(out_ref, slice(MID, 2 * MID), squares)


def middle(got_ref, plane_ref, gain_ref, bias_ref, conv_ref, act_ref, normed_ref, dpre_ref, sums_ref, spread_ref):
    means = got_ref[:, :, :MID]
    center = jnp.sum(means, axis=0) * (1.0 / LINES)
    apart = means - center[None]
    squares = jnp.sum(got_ref[:, :, MID:] + float(ROWS * PLANES) * (apart * apart), axis=0)
    spread = jnp.sqrt(squares * (1.0 / COUNTED) + 1e-05)
    spread_ref[0:1, :] = spread
    normed = (conv_ref[...] - center) / spread
    pre = flat(gain_ref) * normed + flat(bias_ref)
    inner = tanh_of(pre)
    dpre = unwoven(plane_ref[:, :, :128]) * slope_of(pre, inner)
    copies(sums_ref, slice(0, MID), sum_rows(dpre))
    copies(sums_ref, slice(MID, 2 * MID), sum_rows(dpre * normed))
    normed_ref[...] = normed
    dpre_ref[...] = dpre
    act_ref[...] = woven(gelu_of(pre, inner))


def middle_plane(sums_ref, act_ref, out_ref):
    tile = tile_of(in_two(jnp.sum(sums_ref[...], axis=0), 128), 128).astype(BF16)
    out_ref[:, :, :128] = act_ref[...]
    out_ref[:, :, 128:] = jnp.broadcast_to(tile[None], (PLANES, 8, 128))


def in_four(value):
    blank = jnp.zeros((1, HALF - CH // 2), F32)
    return tile_of([jnp.concatenate([row, blank], axis=1) for row in in_two(value, CH // 2)], HALF)


def from_four(tile):
    return jnp.concatenate([tile[k : k + 1, : CH // 2] + tile[k + 2 : k + 3, : CH // 2] for k in range(2)], axis=1)


def filter_sent(
    got_ref,
    gain_ref,
    cot_ref,
    weight_ref,
    gain_in_ref,
    bias_in_ref,
    dpre_ref,
    normed_ref,
    spread_ref,
    act_in_ref,
    x_ref,
    stat_ref,
    sent_ref,
    stacked_ref,
    act_ref,
    dpre_out_ref,
    sums_ref,
):
    tile = jnp.sum(got_ref[:, :, 128:].astype(F32), axis=0) * (1.0 / COUNTED)
    tile = tile + pltpu.roll(tile, 4, axis=0)
    first, second = row_of(tile, (0, 1)), row_of(tile, (2, 3))
    dconv = dpre_ref[...] - first - normed_ref[...] * second
    dconv = flat(gain_ref) * dconv / spread_ref[0:1, :]
    stacked = jnp.concatenate([earlier(dconv), dconv, later(dconv)], axis=1).astype(BF16)
    stacked_ref[...] = stacked
    act_ref[...] = unwoven(got_ref[:, :, :128]).astype(BF16)
    normed = (x_ref[...].astype(F32) - stat_ref[0:1, :]) / stat_ref[1:2, :]
    pre = flat(gain_in_ref) * normed + flat(bias_in_ref)
    dpre = matmul(stacked, weight_ref[...], ((1,), (1,))) * slope_of(pre, tanh_of(pre))
    dpre_out_ref[...] = dpre
    both = in_four(sum_rows(dpre)).astype(BF16), in_four(sum_rows(dpre * normed)).astype(BF16)
    core = lax.axis_index("core")

    @pl.when(core == 0)
    def _():
        right_half(sent_ref, act_in_ref, stacked_ref, cot_ref, act_ref)
        sent_ref[CH:, :] = both[1]
        sums_ref[...] = both[0]

    @pl.when(core == 1)
    def _():
        left_half(sent_ref, act_in_ref, stacked_ref)
        sent_ref[CH:, :] = both[0]
        sums_ref[...] = both[1]


def left_half(out_ref, act_in_ref, stacked_ref):
    part = matmul(act_in_ref[...], stacked_ref[:, :HALF], ((0,), (0,)))
    out_ref[:CH, :] = part.astype(BF16)


def right_half(out_ref, act_in_ref, stacked_ref, cot_ref, act_ref):
    part = matmul(act_in_ref[...], stacked_ref[:, HALF:], ((0,), (0,)))
    out_ref[:CH, : HALF - MID] = part.astype(BF16)
    part = matmul(cot_ref[...], act_ref[...], ((0,), (0,)))
    out_ref[:CH, HALF - MID :] = part.astype(BF16)


def filter_kept(
    cot_ref, x_ref, proj_ref, act_in_ref, stacked_ref, act_ref, dpre_ref, sums_ref, kept_ref, back_ref, out_ref
):
    core = lax.axis_index("core")
    update = matmul(act_ref[...], proj_ref[...], ((1,), (0,)))
    out_ref[...] = (x_ref[...].astype(F32) + update).astype(BF16)
    kept_ref[CH:, :] = sums_ref[...]
    back_ref[...] = woven(dpre_ref[...])

    @pl.when(core == 0)
    def _():
        left_half(kept_ref, act_in_ref, stacked_ref)

    @pl.when(core == 1)
    def _():
        right_half(kept_ref, act_in_ref, stacked_ref, cot_ref, act_ref)


def to_plane(got_ref, kept_ref, back_ref, out_ref):
    both = kept_ref[...].astype(F32) + got_ref[...].astype(F32)
    pieces = both[:CH].astype(BF16).reshape(PLANES, 3, 8, HALF)
    for k in range(3):
        out_ref[:, :, HALF * k : HALF * (k + 1)] = pieces[:, k]
    begin = 3 * HALF + CH // 2
    out_ref[:, :, 3 * HALF : begin] = back_ref[...]
    sums = from_four(both[CH:])
    tile = tile_of([sums[:, k : k + 128] for k in range(0, CH, 128)], 128).astype(BF16)
    out_ref[:, :, begin:] = jnp.broadcast_to(tile[None], (PLANES, 8, 128))


def to_line(got_ref, out_ref):
    tiles = [
        jnp.sum(got_ref[:, :, HALF * k : HALF * (k + 1)].astype(F32), axis=0) for k in range(3)
    ]
    sums = jnp.sum(got_ref[:, :, 3 * HALF + CH // 2 :].astype(F32), axis=0)
    low = pltpu.roll(in_four(row_of(sums, range(6))), 4, axis=0)
    upper = lax.broadcasted_iota(jnp.int32, (8, HALF), 0) < 4
    turned = [pltpu.roll(tile, 4, axis=0) for tile in tiles]
    own = (
        (tiles[0], jnp.where(upper, tiles[1], low)),
        (jnp.where(upper, turned[1], turned[2]), jnp.where(upper, turned[2], low)),
    )
    for core in range(2):
        for k in range(2):
            out_ref[core * BATCH : (core + 1) * BATCH, :, HALF * k : HALF * (k + 1)] = (
                jnp.broadcast_to(own[core][k].astype(BF16)[None], (BATCH, 8, HALF))
            )


def last_rows(
    got_ref, plane_ref, x_ref, cot_ref, gain_ref, stat_ref, grad_ref, conv_ref, proj_grad_ref
):
    x = x_ref[...].astype(F32)
    left, right = (
        jnp.sum(got_ref[BATCH * k : BATCH * (k + 1)].astype(F32), axis=0) for k in range(2)
    )
    first, second = (from_four(half[4:8, HALF:]) * (1.0 / COUNTED) for half in (left, right))
    spread = stat_ref[1:2, :]
    normed = (x - stat_ref[0:1, :]) / spread
    dpre = unwoven(plane_ref[:, :, 3 * HALF : 3 * HALF + CH // 2])
    change = flat(gain_ref) * (dpre - first - normed * second) / spread
    grad_ref[...] = (cot_ref[...].astype(F32) + change).astype(BF16)
    for rows, lanes, count in ((slice(0, 8), 0, 8), (slice(8, 12), HALF, 4)):
        conv_ref[rows, :HALF] = left[:count, lanes : lanes + HALF]
        conv_ref[rows, HALF:] = right[:count, lanes : lanes + CH - HALF]
        proj_grad_ref[rows, :] = right[:count, lanes + CH - HALF : lanes + HALF]


def per_device(inputs, cotangent, conv_weight, proj_weight, gain_in, bias_in, gain_mid, bias_mid):
    x = inputs.reshape(ROWS, CH)
    cot = cotangent.reshape(ROWS, CH)
    rows, rows_mid = (ROWS, CH), (ROWS, MID)

    far, near = pl.BlockSpec(memory_space=pltpu.HBM), pl.BlockSpec(memory_space=pltpu.VMEM)
    sums, data = pl.pallas_call(
        opening,
        out_shape=(
            jax.ShapeDtypeStruct((LINES, 1, 2 * CH), F32),
            jax.ShapeDtypeStruct((PLANES, 8, CH // 2), BF16),
        ),
        in_specs=[far],
        out_specs=(near, near),
        scratch_shapes=[pltpu.VMEM(rows, BF16), pltpu.SemaphoreType.DMA],
        name="opening",
        compiler_params=pltpu.CompilerParams(vmem_limit_bytes=24 << 20),
    )(pltpu.with_memory_space_constraint(x, pltpu.HBM))
    sums = exchange(sums, LINE)
    (both,) = kernel(spread_all, ((PLANES, 8, CH), BF16), name="spread_all")(
        data, near=(sums,)
    )
    both = exchange(both, PLANE)

    act_in, far_x, conv, both, stat_in = kernel(
        forward_conv,
        (rows, BF16),
        (rows, BF16),
        (rows_mid, F32),
        ((PLANES, 8, 256), BF16),
        ((8, CH), F32),
        name="forward_conv",
    )(near=(both, conv_weight, gain_in, bias_in, cot, proj_weight))
    both = exchange(both, PLANE)
    (sums,) = kernel(middle_line, ((LINES, 1, 2 * MID), F32), name="middle_line")(near=(both,))
    sums = exchange(sums, LINE)

    act_mid, normed_mid, dpre_mid, sums, spread_mid = kernel(
        middle,
        ((PLANES, 8, 128), BF16),
        (rows_mid, F32),
        (rows_mid, F32),
        ((LINES, 1, 2 * MID), F32),
        ((8, MID), F32),
        name="middle",
    )(conv, near=(sums, both, gain_mid, bias_mid))
    sums = exchange(sums, LINE)
    (both,) = kernel(middle_plane, ((PLANES, 8, 256), BF16), name="middle_plane")(
        act_mid, near=(sums,)
    )
    both = exchange(both, PLANE)

    sent, stacked, act_mid, dpre_in, sums = kernel(
        filter_sent,
        ((CH + 8, HALF), BF16),
        (rows, BF16),
        (rows_mid, BF16),
        (rows, F32),
        ((8, HALF), BF16),
        name="filter_sent",
    )(
        dpre_mid,
        normed_mid,
        spread_mid,
        act_in,
        far_x,
        stat_in,
        near=(both, gain_mid, cot, conv_weight, gain_in, bias_in),
    )
    got = lax.ppermute(sent, "core", [(0, 1), (1, 0)])
    kept, back, block_out = kernel(
        filter_kept,
        ((CH + 8, HALF), BF16),
        ((PLANES, 8, CH // 2), BF16),
        (rows, BF16),
        name="filter_kept",
    )(act_in, stacked, act_mid, dpre_in, sums, near=(cot, x, proj_weight))
    (plane,) = kernel(to_plane, ((PLANES, 8, 3 * HALF + CH // 2 + 128), BF16), name="to_plane")(
        kept, back, near=(got,)
    )
    plane = exchange(plane, PLANE)
    (line,) = kernel(to_line, ((LINES, 8, 2 * HALF), BF16), name="to_line")(near=(plane,))
    line = exchange(line, LINE)
    input_grad, conv_grad, proj_grad = kernel(
        last_rows, (rows, BF16), ((12, CH), F32), ((12, MID), F32), name="last_rows"
    )(stat_in, near=(line, plane, x, cot, gain_in))
    return (
        block_out.reshape(inputs.shape),
        input_grad.reshape(inputs.shape),
        conv_grad,
        proj_grad,
    )


def solution(mesh):
    split = Mesh(mesh.devices.reshape(4, 2, 4, 2, 8), ("x", "z_hi", "z_lo", "core", "dp"))
    rows = P("dp", SEQ, None)
    return jax.shard_map(
        per_device,
        mesh=split,
        in_specs=(rows, rows, P(), P(), P(), P(), P(), P()),
        out_specs=(rows, rows, P(SEQ, None), P(SEQ, None)),
        check_vma=False,
    )
```
